256 devices in a mesh: sec: 2 (over y_lo), lat: 32 (over y_hi, z, core), col: 4 (over x).
Axes of the slice: x: 4, y: 4 (y_hi: 2, y_lo: 2; y = y_hi * 2 + y_lo), z: 8, core: 2. Of those that a mesh axis runs over, the one named last changes fastest.
Arguments:
- sources: bfloat16 [4, 128, 2, 128, 128], P('sec', ('lat', 'col')), may hold values from -6 to 6
- inverse_tiles: bfloat16 [4, 128, 8, 2, 128, 128], P('sec', 'lat', 'col'), may hold values from -0.15625 to 0.15625
- pattern: int32 [4, 128, 8], P('sec', 'lat', 'col'), may hold values 0 or 1
- phase_index: int32 [1], replicated, may hold values from 1 to 15
Outputs:
- solution: float32 [4, 128, 2, 128, 128], P('sec', ('lat', 'col'))
The draws below stay inside these ranges and needn't reach their ends.
All inputs are finite; a program needn't handle non-finite values. No bound on the sum of `pattern` on one device may be relied on, other than what follows from the above.
Results may differ from the reference program's by a relative error of at most 0.015.
Values may be sent and summed in bfloat16 or wider, within the bound.
A program may use at most 64 MiB of HBM per device.

```python
import jax
import jax.numpy as jnp
from jax import lax

BLK = 128
OFF = 8
PHASES = 16
NRHS = 128
SLABS = 4
ROWBLK = 128


def with_ends(array, rng, smallest, high):
    longest = array.shape.index(max(array.shape))
    spots = []
    for shift in (0, 1):
        where = [jax.random.randint(jax.random.fold_in(rng, axis), (), 0, length) for axis, length in enumerate(array.shape)]
        where[longest] = (where[longest] + shift) % array.shape[longest]
        spots.append(tuple(where))
    return array.at[spots[0]].set(smallest).at[spots[1]].set(high)


def block_levels(key, extent, cuts, least, top_value):
    def one(axis_at, blocks):
        draws = jax.random.uniform(jax.random.fold_in(jax.random.fold_in(key, 6), axis_at), (blocks,), jnp.float32, least / len(cuts), top_value / len(cuts))
        return jnp.repeat(jnp.exp(draws), extent[axis_at] // blocks).reshape((-1,) + (1,) * (len(extent) - axis_at - 1))

    loudness = one(*cuts[0])
    for cut in cuts[1:]:
        loudness = loudness * one(*cut)
    return loudness


def bell_draw(own_key, dims, scale, bound, cuts=(), kind=jnp.bfloat16):
    values = jax.random.normal(own_key, dims, jnp.float32) * scale
    if len(cuts) > 0:
        values = block_levels(own_key, dims, cuts, -0.22, 0.18) * values
    return jnp.clip(values, min=-bound, max=bound).astype(kind)


def setup_inputs(seed: int = 0) -> dict:
    splits = jax.random.split(jax.random.key(seed), 5)
    sources = bell_draw(splits[0], (SLABS, ROWBLK, 2, BLK, NRHS), 1.0, 6.0, ((0, 2), (1, 128)))
    inverse_tiles = bell_draw(splits[1], (SLABS, ROWBLK, OFF, 2, BLK, BLK), (3 * BLK * OFF // 2) ** -0.5, 0.15625, ((0, 2), (1, 32), (2, 4)))
    pattern = with_ends((jax.random.randint(splits[2], (SLABS, ROWBLK, OFF), 0, 4) < 3).astype(jnp.int32), jax.random.fold_in(splits[2], 1), 0, 1)
    phase_index = jax.random.randint(splits[3], (1,), 1, PHASES).astype(jnp.int32)
    return {"sources": sources, "inverse_tiles": inverse_tiles, "pattern": pattern, "phase_index": phase_index}


coupling = 0.8


def rotated(part, cos_value, sin_value):
    wide = part.astype(jnp.float32)
    real_part = wide[:, 0] * cos_value - wide[:, 1] * sin_value
    imag_part = wide[:, 0] * sin_value + wide[:, 1] * cos_value
    return jnp.stack([real_part, imag_part], 1).astype(jnp.bfloat16)


def apply_inverse(tiles_slab, mask_slab, field, cos_value, sin_value):
    reach_blocks = OFF // 2
    extended = jnp.concatenate([rotated(field[-reach_blocks:], cos_value, -sin_value), field, rotated(field[:reach_blocks], cos_value, sin_value)], 0)
    masked = tiles_slab * mask_slab.astype(jnp.bfloat16)[:, :, None, None, None]

    def add_offset(total, offset):
        window = lax.dynamic_slice_in_dim(extended, offset, ROWBLK, 0).astype(jnp.float32)
        tile_part = lax.dynamic_index_in_dim(masked, offset, 1, keepdims=False).astype(jnp.float32)
        parts = jnp.einsum("rkab,rcbn->rkcan", tile_part, window)
        term = jnp.stack([parts[:, 0, 0] - parts[:, 1, 1], parts[:, 1, 0] + parts[:, 0, 1]], 1)
        return total + term, None

    total, _ = lax.scan(add_offset, jnp.zeros(field.shape, jnp.float32), jnp.arange(OFF, dtype=jnp.int32))
    return total


def reference(sources, inverse_tiles, pattern, phase_index):
    angle = 2.0 * jnp.pi * phase_index[0].astype(jnp.float32) / PHASES
    cos_value = jnp.cos(angle)
    sin_value = jnp.sin(angle)
    forward_fields = []
    previous = jnp.zeros(sources.shape[1:], jnp.float32)
    for slab in range(SLABS):
        field = (sources[slab].astype(jnp.float32) + coupling * previous).astype(jnp.bfloat16)
        previous = apply_inverse(inverse_tiles[slab], pattern[slab], field, cos_value, sin_value)
        forward_fields.append(previous)
    results = [None] * SLABS
    following = jnp.zeros(sources.shape[1:], jnp.float32)
    for slab in reversed(range(SLABS)):
        field = following.astype(jnp.bfloat16)
        following = forward_fields[slab] + coupling * apply_inverse(inverse_tiles[slab], pattern[slab], field, cos_value, sin_value)
        results[slab] = following
    return jnp.stack(results, 0)
```

```python
import functools

import jax
import jax.numpy as jnp
from jax import lax
from jax.experimental import pallas as pl
from jax.experimental.pallas import tpu as pltpu
from jax.sharding import PartitionSpec as P

OFF = 8
PHASES = 16
APPS = 7

coupling = 0.8

MESH_ID = pl.DeviceIdType.MESH


def row_targets(c0, ncol, nlat, koff, reach, width):
    out = []
    for dl in range(-2, 3):
        if abs(dl) >= nlat:
            continue
        for c in range(ncol):
            slot = c0 - dl * ncol + reach - c * koff
            if 0 <= slot < width:
                out.append((dl, c, slot))
    return out


def sweep_kernel(
    nlat, ncol, koff, reach, width,
    trig_ref, pat_ref, src_ref, tiles_ref, out_ref,
    xbuf, accbuf, pbuf, fbuf, vbuf, srcbuf,
    rs1, ss1, rs2, ss2, rsrc, ssrc,
):
    sec = lax.axis_index("sec")
    lat = lax.axis_index("lat")
    col = lax.axis_index("col")
    cos_v = trig_ref[0]
    sin_v = trig_ref[1]
    nrows = nlat * ncol
    own_slot = reach - col * koff + col

    def send_rows(n, to_sec, local):
        for c0v in range(ncol):
            targets = row_targets(c0v, ncol, nlat, koff, reach, width)

            @pl.when(col == c0v)
            def _():
                for t, (dl, c, slot) in enumerate(targets):
                    if local and dl == 0 and c == c0v:
                        continue
                    pltpu.make_async_remote_copy(
                        src_ref=fbuf.at[n],
                        dst_ref=xbuf.at[n, slot],
                        send_sem=ss1.at[n, t],
                        recv_sem=rs1.at[n, slot],
                        device_id=(to_sec, (lat + dl + nlat) % nlat, c),
                        device_id_type=MESH_ID,
                    ).start()

    def wait_row_sends(n, to_sec, local):
        for c0v in range(ncol):
            targets = row_targets(c0v, ncol, nlat, koff, reach, width)

            @pl.when(col == c0v)
            def _():
                for t, (dl, c, slot) in enumerate(targets):
                    if local and dl == 0 and c == c0v:
                        continue
                    pltpu.make_async_remote_copy(
                        src_ref=fbuf.at[n],
                        dst_ref=xbuf.at[n, slot],
                        send_sem=ss1.at[n, t],
                        recv_sem=rs1.at[n, slot],
                        device_id=(to_sec, (lat + dl + nlat) % nlat, c),
                        device_id_type=MESH_ID,
                    ).wait_send()

    def wait_rows(n, local):
        for i in range(width):
            desc = pltpu.make_async_remote_copy(
                src_ref=fbuf.at[n],
                dst_ref=xbuf.at[n, i],
                send_sem=ss1.at[n, 0],
                recv_sem=rs1.at[n, i],
                device_id=(sec, lat, col),
                device_id_type=MESH_ID,
            )
            if local:
                @pl.when(own_slot != i)
                def _():
                    desc.wait_recv()
            else:
                desc.wait_recv()

    def compute(n, slab):
        base = lat * ncol - reach + col * koff
        for i in range(width):
            g = base + i
            lo = g < 0
            hi = g >= nrows
            cs = jnp.where(lo | hi, cos_v, jnp.float32(1.0))
            sn = jnp.where(lo, -sin_v, jnp.where(hi, sin_v, jnp.float32(0.0)))
            x = xbuf[n, i].astype(jnp.float32)
            xr = x[0] * cs - x[1] * sn
            xi = x[0] * sn + x[1] * cs
            xbuf[n, i, 0] = xr.astype(jnp.bfloat16)
            xbuf[n, i, 1] = xi.astype(jnp.bfloat16)

        @pl.loop(0, ncol)
        def _(r):
            acc_r = None
            acc_i = None
            for j in range(koff):
                p = pat_ref[slab, r, j].astype(jnp.float32)
                tr = tiles_ref[slab, r, j, 0]
                ti = tiles_ref[slab, r, j, 1]
                xr = xbuf[n, r + j, 0]
                xi = xbuf[n, r + j, 1]
                dot = functools.partial(jnp.dot, preferred_element_type=jnp.float32)
                re = dot(tr, xr) - dot(ti, xi)
                im = dot(ti, xr) + dot(tr, xi)
                re = p * re
                im = p * im
                acc_r = re if acc_r is None else acc_r + re
                acc_i = im if acc_i is None else acc_i + im
            accbuf[n, r, 0] = acc_r
            accbuf[n, r, 1] = acc_i

    def reduce_cols(n):
        for c0v in range(ncol):
            @pl.when(col == c0v)
            def _():
                for r in range(ncol):
                    if r == c0v:
                        continue
                    pltpu.make_async_remote_copy(
                        src_ref=accbuf.at[n, r],
                        dst_ref=pbuf.at[n, c0v],
                        send_sem=ss2.at[n, r],
                        recv_sem=rs2.at[n, c0v],
                        device_id=(sec, lat, r),
                        device_id_type=MESH_ID,
                    ).start()
        pbuf[n, col] = accbuf[n, col]
        for c in range(ncol):
            @pl.when(col != c)
            def _():
                pltpu.make_async_remote_copy(
                    src_ref=accbuf.at[n, c],
                    dst_ref=pbuf.at[n, c],
                    send_sem=ss2.at[n, c],
                    recv_sem=rs2.at[n, c],
                    device_id=(sec, lat, col),
                    device_id_type=MESH_ID,
                ).wait_recv()
        total = pbuf[n, 0]
        for c in range(1, ncol):
            total = total + pbuf[n, c]
        for c0v in range(ncol):
            @pl.when(col == c0v)
            def _():
                for r in range(ncol):
                    if r == c0v:
                        continue
                    pltpu.make_async_remote_copy(
                        src_ref=accbuf.at[n, r],
                        dst_ref=pbuf.at[n, c0v],
                        send_sem=ss2.at[n, r],
                        recv_sem=rs2.at[n, c0v],
                        device_id=(sec, lat, r),
                        device_id_type=MESH_ID,
                    ).wait_send()
        return total

    def apply_local(n, slab):
        send_rows(n, sec, True)
        xbuf[n, own_slot] = fbuf[n]
        wait_rows(n, True)
        compute(n, slab)
        total = reduce_cols(n)
        wait_row_sends(n, sec, True)
        return total

    def apply_remote(n, slab):
        wait_rows(n, False)
        compute(n, slab)
        return reduce_cols(n)

    @pl.when(sec == 0)
    def _():
        fbuf[0] = src_ref[0, 0]
        v0 = apply_local(0, 0)
        vbuf[0] = v0
        fbuf[1] = (src_ref[1, 0].astype(jnp.float32) + coupling * v0).astype(jnp.bfloat16)
        v1 = apply_local(1, 1)
        vbuf[1] = v1
        src_copy = pltpu.make_async_remote_copy(
            src_ref=src_ref.at[0, 0], dst_ref=srcbuf, send_sem=ssrc, recv_sem=rsrc,
            device_id=(1, lat, col), device_id_type=MESH_ID,
        )
        src_copy.wait_recv()
        fbuf[2] = (srcbuf[...].astype(jnp.float32) + coupling * v1).astype(jnp.bfloat16)
        send_rows(2, 1, False)
        g1 = apply_remote(5, 1)
        sol1 = vbuf[1] + coupling * g1
        out_ref[1, 0] = sol1
        fbuf[6] = sol1.astype(jnp.bfloat16)
        g0 = apply_local(6, 0)
        out_ref[0, 0] = vbuf[0] + coupling * g0
        wait_row_sends(2, 1, False)

    @pl.when(sec == 1)
    def _():
        src_copy = pltpu.make_async_remote_copy(
            src_ref=src_ref.at[0, 0], dst_ref=srcbuf, send_sem=ssrc, recv_sem=rsrc,
            device_id=(0, lat, col), device_id_type=MESH_ID,
        )
        src_copy.start()
        v2 = apply_remote(2, 0)
        vbuf[0] = v2
        fbuf[3] = (src_ref[1, 0].astype(jnp.float32) + coupling * v2).astype(jnp.bfloat16)
        v3 = apply_local(3, 1)
        out_ref[1, 0] = v3
        fbuf[4] = v3.astype(jnp.bfloat16)
        g2 = apply_local(4, 0)
        sol2 = vbuf[0] + coupling * g2
        out_ref[0, 0] = sol2
        fbuf[5] = sol2.astype(jnp.bfloat16)
        send_rows(5, 0, False)
        wait_row_sends(5, 0, False)
        src_copy.wait_send()


def shards(sources, inverse_tiles, pattern, phase_index):
    nlat = lax.axis_size("lat")
    ncol = lax.axis_size("col")
    koff = inverse_tiles.shape[2]
    reach = OFF // 2
    width = ncol + koff - 1
    blk, nrhs = sources.shape[3], sources.shape[4]
    angle = 2.0 * jnp.pi * phase_index[0].astype(jnp.float32) / PHASES
    trig = jnp.stack([jnp.cos(angle), jnp.sin(angle)])
    kernel = functools.partial(sweep_kernel, nlat, ncol, koff, reach, width)
    vmem = pl.BlockSpec(memory_space=pltpu.VMEM)
    smem = pl.BlockSpec(memory_space=pltpu.SMEM)
    return pl.pallas_call(
        kernel,
        out_shape=jax.ShapeDtypeStruct(sources.shape, jnp.float32),
        in_specs=[smem, smem, vmem, vmem],
        out_specs=vmem,
        scratch_shapes=[
            pltpu.VMEM((APPS, width, 2, blk, nrhs), jnp.bfloat16),
            pltpu.VMEM((APPS, ncol, 2, blk, nrhs), jnp.float32),
            pltpu.VMEM((APPS, ncol, 2, blk, nrhs), jnp.float32),
            pltpu.VMEM((APPS, 2, blk, nrhs), jnp.bfloat16),
            pltpu.VMEM((2, 2, blk, nrhs), jnp.float32),
            pltpu.VMEM((2, blk, nrhs), jnp.bfloat16),
            pltpu.SemaphoreType.DMA((APPS, width)),
            pltpu.SemaphoreType.DMA((APPS, 16)),
            pltpu.SemaphoreType.DMA((APPS, ncol)),
            pltpu.SemaphoreType.DMA((APPS, ncol)),
            pltpu.SemaphoreType.DMA(()),
            pltpu.SemaphoreType.DMA(()),
        ],
        compiler_params=pltpu.CompilerParams(
            has_side_effects=True, vmem_limit_bytes=48 * 1024 * 1024
        ),
    )(trig, pattern, sources, inverse_tiles)


def solution(mesh):
    placed = (
        P("sec", ("lat", "col"), None, None, None),
        P("sec", "lat", "col", None, None, None),
        P("sec", "lat", "col"),
        P(),
    )
    return jax.shard_map(
        shards,
        mesh=mesh,
        in_specs=placed,
        out_specs=P("sec", ("lat", "col"), None, None, None),
        check_vma=False,
    )
```

```python
import functools

import jax
import jax.numpy as jnp
from jax import lax
from jax.experimental import pallas as pl
from jax.experimental.pallas import tpu as pltpu
from jax.sharding import PartitionSpec as P

OFF = 8
PHASES = 16
APPS = 7

coupling = 0.8

MESH_ID = pl.DeviceIdType.MESH


def row_targets(c0, ncol, nlat, koff, reach, width):
    out = []
    for dl in range(-2, 3):
        if abs(dl) >= nlat:
            continue
        for c in range(ncol):
            slot = c0 - dl * ncol + reach - c * koff
            if 0 <= slot < width:
                out.append((dl, c, slot))
    return out


def sweep_kernel(
    nlat, ncol, koff, reach, width,
    trig_ref, pat_ref, src_ref, tiles_ref, out_ref,
    xbuf, accbuf, sendbuf, pbuf, fbuf, vbuf, srcbuf,
    rs1, ss1, rs2, ss2, rsrc, ssrc,
):
    sec = lax.axis_index("sec")
    lat = lax.axis_index("lat")
    col = lax.axis_index("col")
    cos_v = trig_ref[0]
    sin_v = trig_ref[1]
    nrows = nlat * ncol
    own_slot = reach - col * koff + col

    barrier = pltpu.get_barrier_semaphore()
    partners = 0
    for ds in range(2):
        for dl in (-1, 0, 1):
            for c in range(ncol):
                if ds == 0 and dl == 0:
                    continue
                pl.semaphore_signal(
                    barrier, 1,
                    device_id=((sec + ds) % 2, (lat + dl + nlat) % nlat, (col + c) % ncol),
                    device_id_type=MESH_ID,
                )
                partners += 1
    for c in range(1, ncol):
        pl.semaphore_signal(
            barrier, 1, device_id=(sec, lat, (col + c) % ncol), device_id_type=MESH_ID
        )
        partners += 1
    pl.semaphore_wait(barrier, partners)

    def send_rows(n, to_sec, local):
        for c0v in range(ncol):
            targets = row_targets(c0v, ncol, nlat, koff, reach, width)

            @pl.when(col == c0v)
            def _():
                for t, (dl, c, slot) in enumerate(targets):
                    if local and dl == 0 and c == c0v:
                        continue
                    pltpu.make_async_remote_copy(
                        src_ref=fbuf.at[n],
                        dst_ref=xbuf.at[n, slot],
                        send_sem=ss1.at[n, t],
                        recv_sem=rs1.at[n, slot],
                        device_id=(to_sec, (lat + dl + nlat) % nlat, c),
                        device_id_type=MESH_ID,
                    ).start()

    def wait_row_sends(n, to_sec, local):
        for c0v in range(ncol):
            targets = row_targets(c0v, ncol, nlat, koff, reach, width)

            @pl.when(col == c0v)
            def _():
                for t, (dl, c, slot) in enumerate(targets):
                    if local and dl == 0 and c == c0v:
                        continue
                    pltpu.make_async_remote_copy(
                        src_ref=fbuf.at[n],
                        dst_ref=xbuf.at[n, slot],
                        send_sem=ss1.at[n, t],
                        recv_sem=rs1.at[n, slot],
                        device_id=(to_sec, (lat + dl + nlat) % nlat, c),
                        device_id_type=MESH_ID,
                    ).wait_send()

    def wait_rows(n, local):
        for i in range(width):
            desc = pltpu.make_async_remote_copy(
                src_ref=fbuf.at[n],
                dst_ref=xbuf.at[n, i],
                send_sem=ss1.at[n, 0],
                recv_sem=rs1.at[n, i],
                device_id=(sec, lat, col),
                device_id_type=MESH_ID,
            )
            if local:
                @pl.when(own_slot != i)
                def _():
                    desc.wait_recv()
            else:
                desc.wait_recv()

    def compute(n, slab):
        base = lat * ncol - reach + col * koff
        for i in range(width):
            g = base + i
            lo = g < 0
            hi = g >= nrows
            cs = jnp.where(lo | hi, cos_v, jnp.float32(1.0))
            sn = jnp.where(lo, -sin_v, jnp.where(hi, sin_v, jnp.float32(0.0)))
            x = xbuf[n, i].astype(jnp.float32)
            xr = x[0] * cs - x[1] * sn
            xi = x[0] * sn + x[1] * cs
            xbuf[n, i, 0] = xr.astype(jnp.bfloat16)
            xbuf[n, i, 1] = xi.astype(jnp.bfloat16)

        @pl.loop(0, ncol)
        def _(r):
            acc_r = None
            acc_i = None
            for j in range(koff):
                p = pat_ref[slab, r, j].astype(jnp.float32)
                tr = tiles_ref[slab, r, j, 0]
                ti = tiles_ref[slab, r, j, 1]
                xr = xbuf[n, r + j, 0]
                xi = xbuf[n, r + j, 1]
                dot = functools.partial(jnp.dot, preferred_element_type=jnp.float32)
                re = dot(tr, xr) - dot(ti, xi)
                im = dot(ti, xr) + dot(tr, xi)
                re = p * re
                im = p * im
                acc_r = re if acc_r is None else acc_r + re
                acc_i = im if acc_i is None else acc_i + im
            accbuf[n, r, 0] = acc_r
            accbuf[n, r, 1] = acc_i
            sendbuf[n, r, 0] = acc_r.astype(jnp.bfloat16)
            sendbuf[n, r, 1] = acc_i.astype(jnp.bfloat16)

    def reduce_cols(n):
        pbuf[n, col] = jnp.zeros(pbuf.shape[2:], pbuf.dtype)
        for c0v in range(ncol):
            @pl.when(col == c0v)
            def _():
                for r in range(ncol):
                    if r == c0v:
                        continue
                    pltpu.make_async_remote_copy(
                        src_ref=sendbuf.at[n, r],
                        dst_ref=pbuf.at[n, c0v],
                        send_sem=ss2.at[n, r],
                        recv_sem=rs2.at[n, c0v],
                        device_id=(sec, lat, r),
                        device_id_type=MESH_ID,
                    ).start()
        for c in range(ncol):
            @pl.when(col != c)
            def _():
                pltpu.make_async_remote_copy(
                    src_ref=sendbuf.at[n, c],
                    dst_ref=pbuf.at[n, c],
                    send_sem=ss2.at[n, c],
                    recv_sem=rs2.at[n, c],
                    device_id=(sec, lat, col),
                    device_id_type=MESH_ID,
                ).wait_recv()
        total = accbuf[n, col]
        for c in range(ncol):
            total = total + pbuf[n, c].astype(jnp.float32)
        for c0v in range(ncol):
            @pl.when(col == c0v)
            def _():
                for r in range(ncol):
                    if r == c0v:
                        continue
                    pltpu.make_async_remote_copy(
                        src_ref=sendbuf.at[n, r],
                        dst_ref=pbuf.at[n, c0v],
                        send_sem=ss2.at[n, r],
                        recv_sem=rs2.at[n, c0v],
                        device_id=(sec, lat, r),
                        device_id_type=MESH_ID,
                    ).wait_send()
        return total

    def apply_local(n, slab):
        send_rows(n, sec, True)
        xbuf[n, own_slot] = fbuf[n]
        wait_rows(n, True)
        compute(n, slab)
        total = reduce_cols(n)
        wait_row_sends(n, sec, True)
        return total

    def apply_remote(n, slab):
        wait_rows(n, False)
        compute(n, slab)
        return reduce_cols(n)

    @pl.when(sec == 0)
    def _():
        fbuf[0] = src_ref[0, 0]
        v0 = apply_local(0, 0)
        vbuf[0] = v0
        fbuf[1] = (src_ref[1, 0].astype(jnp.float32) + coupling * v0).astype(jnp.bfloat16)
        v1 = apply_local(1, 1)
        vbuf[1] = v1
        src_copy = pltpu.make_async_remote_copy(
            src_ref=src_ref.at[0, 0], dst_ref=srcbuf, send_sem=ssrc, recv_sem=rsrc,
            device_id=(1, lat, col), device_id_type=MESH_ID,
        )
        src_copy.wait_recv()
        fbuf[2] = (srcbuf[...].astype(jnp.float32) + coupling * v1).astype(jnp.bfloat16)
        send_rows(2, 1, False)
        g1 = apply_remote(5, 1)
        sol1 = vbuf[1] + coupling * g1
        out_ref[1, 0] = sol1
        fbuf[6] = sol1.astype(jnp.bfloat16)
        g0 = apply_local(6, 0)
        out_ref[0, 0] = vbuf[0] + coupling * g0
        wait_row_sends(2, 1, False)

    @pl.when(sec == 1)
    def _():
        src_copy = pltpu.make_async_remote_copy(
            src_ref=src_ref.at[0, 0], dst_ref=srcbuf, send_sem=ssrc, recv_sem=rsrc,
            device_id=(0, lat, col), device_id_type=MESH_ID,
        )
        src_copy.start()
        v2 = apply_remote(2, 0)
        vbuf[0] = v2
        fbuf[3] = (src_ref[1, 0].astype(jnp.float32) + coupling * v2).astype(jnp.bfloat16)
        v3 = apply_local(3, 1)
        out_ref[1, 0] = v3
        fbuf[4] = v3.astype(jnp.bfloat16)
        g2 = apply_local(4, 0)
        sol2 = vbuf[0] + coupling * g2
        out_ref[0, 0] = sol2
        fbuf[5] = sol2.astype(jnp.bfloat16)
        send_rows(5, 0, False)
        wait_row_sends(5, 0, False)
        src_copy.wait_send()


def shards(sources, inverse_tiles, pattern, phase_index):
    nlat = lax.axis_size("lat")
    ncol = lax.axis_size("col")
    koff = inverse_tiles.shape[2]
    reach = OFF // 2
    width = ncol + koff - 1
    blk, nrhs = sources.shape[3], sources.shape[4]
    angle = 2.0 * jnp.pi * phase_index[0].astype(jnp.float32) / PHASES
    trig = jnp.stack([jnp.cos(angle), jnp.sin(angle)])
    kernel = functools.partial(sweep_kernel, nlat, ncol, koff, reach, width)
    vmem = pl.BlockSpec(memory_space=pltpu.VMEM)
    smem = pl.BlockSpec(memory_space=pltpu.SMEM)
    return pl.pallas_call(
        kernel,
        out_shape=jax.ShapeDtypeStruct(sources.shape, jnp.float32),
        in_specs=[smem, smem, vmem, vmem],
        out_specs=vmem,
        scratch_shapes=[
            pltpu.VMEM((APPS, width, 2, blk, nrhs), jnp.bfloat16),
            pltpu.VMEM((APPS, ncol, 2, blk, nrhs), jnp.float32),
            pltpu.VMEM((APPS, ncol, 2, blk, nrhs), jnp.bfloat16),
            pltpu.VMEM((APPS, ncol, 2, blk, nrhs), jnp.bfloat16),
            pltpu.VMEM((APPS, 2, blk, nrhs), jnp.bfloat16),
            pltpu.VMEM((2, 2, blk, nrhs), jnp.float32),
            pltpu.VMEM((2, blk, nrhs), jnp.bfloat16),
            pltpu.SemaphoreType.DMA((APPS, width)),
            pltpu.SemaphoreType.DMA((APPS, 16)),
            pltpu.SemaphoreType.DMA((APPS, ncol)),
            pltpu.SemaphoreType.DMA((APPS, ncol)),
            pltpu.SemaphoreType.DMA(()),
            pltpu.SemaphoreType.DMA(()),
        ],
        compiler_params=pltpu.CompilerParams(
            has_side_effects=True, collective_id=0, vmem_limit_bytes=48 * 1024 * 1024
        ),
    )(trig, pattern, sources, inverse_tiles)


def solution(mesh):
    placed = (
        P("sec", ("lat", "col"), None, None, None),
        P("sec", "lat", "col", None, None, None),
        P("sec", "lat", "col"),
        P(),
    )
    return jax.shard_map(
        shards,
        mesh=mesh,
        in_specs=placed,
        out_specs=P("sec", ("lat", "col"), None, None, None),
        check_vma=False,
    )
```

```python
import functools

import jax
import jax.numpy as jnp
from jax import lax
from jax.experimental import pallas as pl
from jax.experimental.pallas import tpu as pltpu
from jax.sharding import PartitionSpec as P

OFF = 8
PHASES = 16
APPS = 7

coupling = 0.8

MESH_ID = pl.DeviceIdType.MESH


def sweep_kernel(
    nlat, ncol, koff, reach,
    trig_ref, pat_ref, src_ref, tiles_ref, out_ref,
    mtiles, tiles2, xbuf, fbuf, vbuf, srcbuf,
    rs1, ss1, rst, sst, rsrc, ssrc,
):
    sec = lax.axis_index("sec")
    lat = lax.axis_index("lat")
    col = lax.axis_index("col")
    cos_v = trig_ref[0]
    sin_v = trig_ref[1]
    nrows = nlat * ncol
    noff = koff * ncol
    shifts = [d for d in range(reach - noff + 1, reach + 1)]

    barrier = pltpu.get_barrier_semaphore()
    partners = 0
    for ds in range(2):
        for dl in (-1, 0, 1):
            for c in range(ncol):
                if ds == 0 and dl == 0:
                    continue
                pl.semaphore_signal(
                    barrier, 1,
                    device_id=((sec + ds) % 2, (lat + dl + nlat) % nlat, (col + c) % ncol),
                    device_id_type=MESH_ID,
                )
                partners += 1
    for c in range(1, ncol):
        pl.semaphore_signal(
            barrier, 1, device_id=(sec, lat, (col + c) % ncol), device_id_type=MESH_ID
        )
        partners += 1
    pl.semaphore_wait(barrier, partners)

    def tile_copy(slab, c0v, r):
        return pltpu.make_async_remote_copy(
            src_ref=mtiles.at[slab, r],
            dst_ref=tiles2.at[slab, pl.ds(c0v * koff, koff)],
            send_sem=sst.at[slab, r],
            recv_sem=rst.at[slab, c0v],
            device_id=(sec, lat, r),
            device_id_type=MESH_ID,
        )

    def share_tiles(slab):
        for r in range(ncol):
            for j in range(koff):
                p = pat_ref[slab, r, j].astype(jnp.float32)
                mtiles[slab, r, j] = (tiles_ref[slab, r, j].astype(jnp.float32) * p).astype(jnp.bfloat16)
        for c0v in range(ncol):
            @pl.when(col == c0v)
            def _():
                for r in range(ncol):
                    if r != c0v:
                        tile_copy(slab, c0v, r).start()
                tiles2[slab, pl.ds(c0v * koff, koff)] = mtiles[slab, c0v]

    def wait_tiles(slab):
        for c in range(ncol):
            @pl.when(col != c)
            def _():
                tile_copy(slab, c, c).wait_recv()

    def wait_tile_sends(slab):
        for c0v in range(ncol):
            @pl.when(col == c0v)
            def _():
                for r in range(ncol):
                    if r != c0v:
                        tile_copy(slab, c0v, r).wait_send()

    def row_copy(n, to_sec, c0v, d):
        q = c0v + d
        return pltpu.make_async_remote_copy(
            src_ref=fbuf.at[n],
            dst_ref=xbuf.at[n, reach - d],
            send_sem=ss1.at[n, reach - d],
            recv_sem=rs1.at[n, reach - d],
            device_id=(to_sec, (lat + q // ncol + nlat) % nlat, q % ncol),
            device_id_type=MESH_ID,
        )

    def send_rows(n, to_sec, local):
        for c0v in range(ncol):
            @pl.when(col == c0v)
            def _():
                for d in shifts:
                    if local and d == 0:
                        continue
                    row_copy(n, to_sec, c0v, d).start()
        if local:
            xbuf[n, reach] = fbuf[n]

    def wait_row_sends(n, to_sec, local):
        for c0v in range(ncol):
            @pl.when(col == c0v)
            def _():
                for d in shifts:
                    if local and d == 0:
                        continue
                    row_copy(n, to_sec, c0v, d).wait_send()

    def wait_rows(n, local):
        for d in shifts:
            if local and d == 0:
                continue
            row_copy(n, sec, 0, d).wait_recv()

    def compute(n, slab):
        base = lat * ncol + col - reach

        def body(k, carry):
            acc_r, acc_i = carry
            g = base + k
            lo = g < 0
            hi = g >= nrows
            cs = jnp.where(lo | hi, cos_v, jnp.float32(1.0))
            sn = jnp.where(lo, -sin_v, jnp.where(hi, sin_v, jnp.float32(0.0)))
            x = xbuf[n, k].astype(jnp.float32)
            xr = (x[0] * cs - x[1] * sn).astype(jnp.bfloat16)
            xi = (x[0] * sn + x[1] * cs).astype(jnp.bfloat16)
            tr = tiles2[slab, k, 0]
            ti = tiles2[slab, k, 1]
            dot = functools.partial(jnp.dot, preferred_element_type=jnp.float32)
            acc_r = acc_r + (dot(tr, xr) - dot(ti, xi))
            acc_i = acc_i + (dot(ti, xr) + dot(tr, xi))
            return acc_r, acc_i

        zero = jnp.zeros(xbuf.shape[3:], jnp.float32)
        acc_r, acc_i = lax.fori_loop(0, noff, body, (zero, zero))
        return jnp.stack([acc_r, acc_i], 0)

    def apply(n, slab, local):
        wait_rows(n, local)
        return compute(n, slab)

    @pl.when(sec == 0)
    def _():
        share_tiles(0)
        fbuf[0] = src_ref[0, 0]
        send_rows(0, 0, True)
        share_tiles(1)
        wait_tiles(0)
        v0 = apply(0, 0, True)
        vbuf[0] = v0
        fbuf[1] = (src_ref[1, 0].astype(jnp.float32) + coupling * v0).astype(jnp.bfloat16)
        send_rows(1, 0, True)
        wait_tiles(1)
        v1 = apply(1, 1, True)
        vbuf[1] = v1
        src_copy = pltpu.make_async_remote_copy(
            src_ref=src_ref.at[0, 0], dst_ref=srcbuf, send_sem=ssrc, recv_sem=rsrc,
            device_id=(1, lat, col), device_id_type=MESH_ID,
        )
        src_copy.wait_recv()
        fbuf[2] = (srcbuf[...].astype(jnp.float32) + coupling * v1).astype(jnp.bfloat16)
        send_rows(2, 1, False)
        g1 = apply(5, 1, False)
        sol1 = vbuf[1] + coupling * g1
        out_ref[1, 0] = sol1
        fbuf[6] = sol1.astype(jnp.bfloat16)
        send_rows(6, 0, True)
        g0 = apply(6, 0, True)
        out_ref[0, 0] = vbuf[0] + coupling * g0
        wait_row_sends(0, 0, True)
        wait_row_sends(1, 0, True)
        wait_row_sends(2, 1, False)
        wait_row_sends(6, 0, True)
        wait_tile_sends(0)
        wait_tile_sends(1)

    @pl.when(sec == 1)
    def _():
        src_copy = pltpu.make_async_remote_copy(
            src_ref=src_ref.at[0, 0], dst_ref=srcbuf, send_sem=ssrc, recv_sem=rsrc,
            device_id=(0, lat, col), device_id_type=MESH_ID,
        )
        src_copy.start()
        share_tiles(0)
        share_tiles(1)
        wait_tiles(0)
        wait_tiles(1)
        v2 = apply(2, 0, False)
        vbuf[0] = v2
        fbuf[3] = (src_ref[1, 0].astype(jnp.float32) + coupling * v2).astype(jnp.bfloat16)
        send_rows(3, 1, True)
        v3 = apply(3, 1, True)
        out_ref[1, 0] = v3
        fbuf[4] = v3.astype(jnp.bfloat16)
        send_rows(4, 1, True)
        g2 = apply(4, 0, True)
        sol2 = vbuf[0] + coupling * g2
        out_ref[0, 0] = sol2
        fbuf[5] = sol2.astype(jnp.bfloat16)
        send_rows(5, 0, False)
        wait_row_sends(3, 1, True)
        wait_row_sends(4, 1, True)
        wait_row_sends(5, 0, False)
        wait_tile_sends(0)
        wait_tile_sends(1)
        src_copy.wait_send()


def shards(sources, inverse_tiles, pattern, phase_index):
    nlat = lax.axis_size("lat")
    ncol = lax.axis_size("col")
    koff = inverse_tiles.shape[2]
    reach = OFF // 2
    noff = koff * ncol
    blk, nrhs = sources.shape[3], sources.shape[4]
    angle = 2.0 * jnp.pi * phase_index[0].astype(jnp.float32) / PHASES
    trig = jnp.stack([jnp.cos(angle), jnp.sin(angle)])
    kernel = functools.partial(sweep_kernel, nlat, ncol, koff, reach)
    vmem = pl.BlockSpec(memory_space=pltpu.VMEM)
    smem = pl.BlockSpec(memory_space=pltpu.SMEM)
    slabs = inverse_tiles.shape[0]
    return pl.pallas_call(
        kernel,
        out_shape=jax.ShapeDtypeStruct(sources.shape, jnp.float32),
        in_specs=[smem, smem, vmem, vmem],
        out_specs=vmem,
        scratch_shapes=[
            pltpu.VMEM(inverse_tiles.shape, jnp.bfloat16),
            pltpu.VMEM((slabs, noff, 2, blk, blk), jnp.bfloat16),
            pltpu.VMEM((APPS, noff, 2, blk, nrhs), jnp.bfloat16),
            pltpu.VMEM((APPS, 2, blk, nrhs), jnp.bfloat16),
            pltpu.VMEM((2, 2, blk, nrhs), jnp.float32),
            pltpu.VMEM((2, blk, nrhs), jnp.bfloat16),
            pltpu.SemaphoreType.DMA((APPS, noff)),
            pltpu.SemaphoreType.DMA((APPS, noff)),
            pltpu.SemaphoreType.DMA((slabs, ncol)),
            pltpu.SemaphoreType.DMA((slabs, ncol)),
            pltpu.SemaphoreType.DMA(()),
            pltpu.SemaphoreType.DMA(()),
        ],
        compiler_params=pltpu.CompilerParams(
            has_side_effects=True, collective_id=0, vmem_limit_bytes=48 * 1024 * 1024
        ),
    )(trig, pattern, sources, inverse_tiles)


def solution(mesh):
    placed = (
        P("sec", ("lat", "col"), None, None, None),
        P("sec", "lat", "col", None, None, None),
        P("sec", "lat", "col"),
        P(),
    )
    return jax.shard_map(
        shards,
        mesh=mesh,
        in_specs=placed,
        out_specs=P("sec", ("lat", "col"), None, None, None),
        check_vma=False,
    )
```

```python
import functools

import jax
import jax.numpy as jnp
from jax import lax
from jax.experimental import pallas as pl
from jax.experimental.pallas import tpu as pltpu
from jax.sharding import PartitionSpec as P

OFF = 8
PHASES = 16
APPS = 7

coupling = 0.8

MESH_ID = pl.DeviceIdType.MESH


def sweep_kernel(
    nlat, ncol, koff, reach,
    trig_ref, pat_ref, src_ref, tiles_ref, out_ref,
    mtiles, tiles2, xbuf, fbuf, vbuf, srcbuf,
    rs1, ss1, rst, sst, rsrc, ssrc,
):
    sec = lax.axis_index("sec")
    lat = lax.axis_index("lat")
    col = lax.axis_index("col")
    cos_v = trig_ref[0]
    sin_v = trig_ref[1]
    nrows = nlat * ncol
    noff = koff * ncol
    shifts = [d for d in range(reach - noff + 1, reach + 1)]

    barrier = pltpu.get_barrier_semaphore()
    partners = 0
    for ds in range(2):
        for dl in (-1, 0, 1):
            for c in range(ncol):
                if ds == 0 and dl == 0:
                    continue
                pl.semaphore_signal(
                    barrier, 1,
                    device_id=((sec + ds) % 2, (lat + dl + nlat) % nlat, (col + c) % ncol),
                    device_id_type=MESH_ID,
                )
                partners += 1
    for c in range(1, ncol):
        pl.semaphore_signal(
            barrier, 1, device_id=(sec, lat, (col + c) % ncol), device_id_type=MESH_ID
        )
        partners += 1
    pl.semaphore_wait(barrier, partners)

    def tile_copy(slab, c0v, r):
        return pltpu.make_async_remote_copy(
            src_ref=mtiles.at[slab, r],
            dst_ref=tiles2.at[slab, pl.ds(c0v * koff, koff)],
            send_sem=sst.at[slab, r],
            recv_sem=rst.at[slab, c0v],
            device_id=(sec, lat, r),
            device_id_type=MESH_ID,
        )

    def share_tiles(slab):
        for r in range(ncol):
            for j in range(koff):
                p = pat_ref[slab, r, j].astype(jnp.float32)
                mtiles[slab, r, j] = (tiles_ref[slab, r, j].astype(jnp.float32) * p).astype(jnp.bfloat16)
        for c0v in range(ncol):
            @pl.when(col == c0v)
            def _():
                for r in range(ncol):
                    if r != c0v:
                        tile_copy(slab, c0v, r).start()
                tiles2[slab, pl.ds(c0v * koff, koff)] = mtiles[slab, c0v]

    def wait_tiles(slab):
        for c in range(ncol):
            @pl.when(col != c)
            def _():
                tile_copy(slab, c, c).wait_recv()

    def wait_tile_sends(slab):
        for c0v in range(ncol):
            @pl.when(col == c0v)
            def _():
                for r in range(ncol):
                    if r != c0v:
                        tile_copy(slab, c0v, r).wait_send()

    def row_copy(n, to_sec, c0v, d):
        q = c0v + d
        return pltpu.make_async_remote_copy(
            src_ref=fbuf.at[n],
            dst_ref=xbuf.at[n, reach - d],
            send_sem=ss1.at[n, reach - d],
            recv_sem=rs1.at[n, reach - d],
            device_id=(to_sec, (lat + q // ncol + nlat) % nlat, q % ncol),
            device_id_type=MESH_ID,
        )

    def send_rows(n, to_sec, local):
        for c0v in range(ncol):
            @pl.when(col == c0v)
            def _():
                for d in shifts:
                    if local and d == 0:
                        continue
                    row_copy(n, to_sec, c0v, d).start()
        if local:
            xbuf[n, reach] = fbuf[n]

    def wait_row_sends(n, to_sec, local):
        for c0v in range(ncol):
            @pl.when(col == c0v)
            def _():
                for d in shifts:
                    if local and d == 0:
                        continue
                    row_copy(n, to_sec, c0v, d).wait_send()

    def wait_rows(n, local):
        for d in shifts:
            if local and d == 0:
                continue
            row_copy(n, sec, 0, d).wait_recv()

    def compute(n, slab, local):
        order = sorted(range(noff), key=lambda k: (abs(k - reach), k))
        acc_r = None
        acc_i = None
        for k in order:
            d = k - reach
            if not (local and d == 0):
                row_copy(n, sec, 0, -d).wait_recv()
            lo = (lat == 0) & (k < reach - col)
            hi = (lat == nlat - 1) & (k >= reach - col + ncol)

            @pl.when(lo | hi)
            def _():
                sn = jnp.where(lo, -sin_v, sin_v)
                x = xbuf[n, k].astype(jnp.float32)
                xbuf[n, k, 0] = (x[0] * cos_v - x[1] * sn).astype(jnp.bfloat16)
                xbuf[n, k, 1] = (x[0] * sn + x[1] * cos_v).astype(jnp.bfloat16)

            xr = xbuf[n, k, 0]
            xi = xbuf[n, k, 1]
            tr = tiles2[slab, k, 0]
            ti = tiles2[slab, k, 1]
            dot = functools.partial(jnp.dot, preferred_element_type=jnp.float32)
            re = dot(tr, xr) - dot(ti, xi)
            im = dot(ti, xr) + dot(tr, xi)
            acc_r = re if acc_r is None else acc_r + re
            acc_i = im if acc_i is None else acc_i + im
        return jnp.stack([acc_r, acc_i], 0)

    def apply(n, slab, local):
        return compute(n, slab, local)

    @pl.when(sec == 0)
    def _():
        share_tiles(0)
        fbuf[0] = src_ref[0, 0]
        send_rows(0, 0, True)
        share_tiles(1)
        wait_tiles(0)
        v0 = apply(0, 0, True)
        vbuf[0] = v0
        fbuf[1] = (src_ref[1, 0].astype(jnp.float32) + coupling * v0).astype(jnp.bfloat16)
        send_rows(1, 0, True)
        wait_tiles(1)
        v1 = apply(1, 1, True)
        vbuf[1] = v1
        src_copy = pltpu.make_async_remote_copy(
            src_ref=src_ref.at[0, 0], dst_ref=srcbuf, send_sem=ssrc, recv_sem=rsrc,
            device_id=(1, lat, col), device_id_type=MESH_ID,
        )
        src_copy.wait_recv()
        fbuf[2] = (srcbuf[...].astype(jnp.float32) + coupling * v1).astype(jnp.bfloat16)
        send_rows(2, 1, False)
        g1 = apply(5, 1, False)
        sol1 = vbuf[1] + coupling * g1
        out_ref[1, 0] = sol1
        fbuf[6] = sol1.astype(jnp.bfloat16)
        send_rows(6, 0, True)
        g0 = apply(6, 0, True)
        out_ref[0, 0] = vbuf[0] + coupling * g0
        wait_row_sends(0, 0, True)
        wait_row_sends(1, 0, True)
        wait_row_sends(2, 1, False)
        wait_row_sends(6, 0, True)
        wait_tile_sends(0)
        wait_tile_sends(1)

    @pl.when(sec == 1)
    def _():
        src_copy = pltpu.make_async_remote_copy(
            src_ref=src_ref.at[0, 0], dst_ref=srcbuf, send_sem=ssrc, recv_sem=rsrc,
            device_id=(0, lat, col), device_id_type=MESH_ID,
        )
        src_copy.start()
        share_tiles(0)
        share_tiles(1)
        wait_tiles(0)
        wait_tiles(1)
        v2 = apply(2, 0, False)
        vbuf[0] = v2
        fbuf[3] = (src_ref[1, 0].astype(jnp.float32) + coupling * v2).astype(jnp.bfloat16)
        send_rows(3, 1, True)
        v3 = apply(3, 1, True)
        out_ref[1, 0] = v3
        fbuf[4] = v3.astype(jnp.bfloat16)
        send_rows(4, 1, True)
        g2 = apply(4, 0, True)
        sol2 = vbuf[0] + coupling * g2
        out_ref[0, 0] = sol2
        fbuf[5] = sol2.astype(jnp.bfloat16)
        send_rows(5, 0, False)
        wait_row_sends(3, 1, True)
        wait_row_sends(4, 1, True)
        wait_row_sends(5, 0, False)
        wait_tile_sends(0)
        wait_tile_sends(1)
        src_copy.wait_send()


def shards(sources, inverse_tiles, pattern, phase_index):
    nlat = lax.axis_size("lat")
    ncol = lax.axis_size("col")
    koff = inverse_tiles.shape[2]
    reach = OFF // 2
    noff = koff * ncol
    blk, nrhs = sources.shape[3], sources.shape[4]
    angle = 2.0 * jnp.pi * phase_index[0].astype(jnp.float32) / PHASES
    trig = jnp.stack([jnp.cos(angle), jnp.sin(angle)])
    kernel = functools.partial(sweep_kernel, nlat, ncol, koff, reach)
    vmem = pl.BlockSpec(memory_space=pltpu.VMEM)
    smem = pl.BlockSpec(memory_space=pltpu.SMEM)
    slabs = inverse_tiles.shape[0]
    return pl.pallas_call(
        kernel,
        out_shape=jax.ShapeDtypeStruct(sources.shape, jnp.float32),
        in_specs=[smem, smem, vmem, vmem],
        out_specs=vmem,
        scratch_shapes=[
            pltpu.VMEM(inverse_tiles.shape, jnp.bfloat16),
            pltpu.VMEM((slabs, noff, 2, blk, blk), jnp.bfloat16),
            pltpu.VMEM((APPS, noff, 2, blk, nrhs), jnp.bfloat16),
            pltpu.VMEM((APPS, 2, blk, nrhs), jnp.bfloat16),
            pltpu.VMEM((2, 2, blk, nrhs), jnp.float32),
            pltpu.VMEM((2, blk, nrhs), jnp.bfloat16),
            pltpu.SemaphoreType.DMA((APPS, noff)),
            pltpu.SemaphoreType.DMA((APPS, noff)),
            pltpu.SemaphoreType.DMA((slabs, ncol)),
            pltpu.SemaphoreType.DMA((slabs, ncol)),
            pltpu.SemaphoreType.DMA(()),
            pltpu.SemaphoreType.DMA(()),
        ],
        compiler_params=pltpu.CompilerParams(
            has_side_effects=True, collective_id=0, vmem_limit_bytes=48 * 1024 * 1024
        ),
    )(trig, pattern, sources, inverse_tiles)


def solution(mesh):
    placed = (
        P("sec", ("lat", "col"), None, None, None),
        P("sec", "lat", "col", None, None, None),
        P("sec", "lat", "col"),
        P(),
    )
    return jax.shard_map(
        shards,
        mesh=mesh,
        in_specs=placed,
        out_specs=P("sec", ("lat", "col"), None, None, None),
        check_vma=False,
    )
```

```python
import functools

import jax
import jax.numpy as jnp
from jax import lax
from jax.experimental import pallas as pl
from jax.experimental.pallas import tpu as pltpu
from jax.sharding import PartitionSpec as P

OFF = 8
PHASES = 16
APPS = 7
CHUNKS = 2

coupling = 0.8

MESH_ID = pl.DeviceIdType.MESH


def sweep_kernel(
    nlat, ncol, koff, reach, chunks,
    trig_ref, pat_ref, src_ref, tiles_ref, out_ref,
    mtiles, tiles2, xbuf, fbuf, srct, vt, outt, srcbuf,
    rs1, ss1, rst, sst, rsrc, ssrc,
):
    sec = lax.axis_index("sec")
    lat = lax.axis_index("lat")
    col = lax.axis_index("col")
    cos_v = trig_ref[0]
    sin_v = trig_ref[1]
    noff = koff * ncol
    shifts = [d for d in range(reach - noff + 1, reach + 1)]
    width = xbuf.shape[3] // chunks

    barrier = pltpu.get_barrier_semaphore()
    partners = 0
    for ds in range(2):
        for dl in (-1, 0, 1):
            for c in range(ncol):
                if ds == 0 and dl == 0:
                    continue
                pl.semaphore_signal(
                    barrier, 1,
                    device_id=((sec + ds) % 2, (lat + dl + nlat) % nlat, (col + c) % ncol),
                    device_id_type=MESH_ID,
                )
                partners += 1
    for c in range(1, ncol):
        pl.semaphore_signal(
            barrier, 1, device_id=(sec, lat, (col + c) % ncol), device_id_type=MESH_ID
        )
        partners += 1
    pl.semaphore_wait(barrier, partners)

    def tile_copy(slab, c0v, r):
        return pltpu.make_async_remote_copy(
            src_ref=mtiles.at[slab, r],
            dst_ref=tiles2.at[slab, pl.ds(c0v * koff, koff)],
            send_sem=sst.at[slab, r],
            recv_sem=rst.at[slab, c0v],
            device_id=(sec, lat, r),
            device_id_type=MESH_ID,
        )

    def share_tiles(slab):
        for r in range(ncol):
            for j in range(koff):
                p = pat_ref[slab, r, j].astype(jnp.float32)
                mtiles[slab, r, j] = (tiles_ref[slab, r, j].astype(jnp.float32) * p).astype(jnp.bfloat16)
        for c0v in range(ncol):
            @pl.when(col == c0v)
            def _():
                for r in range(ncol):
                    if r != c0v:
                        tile_copy(slab, c0v, r).start()
                tiles2[slab, pl.ds(c0v * koff, koff)] = mtiles[slab, c0v]

    def wait_tiles(slab):
        for c in range(ncol):
            @pl.when(col != c)
            def _():
                tile_copy(slab, c, c).wait_recv()

    def wait_tile_sends(slab):
        for c0v in range(ncol):
            @pl.when(col == c0v)
            def _():
                for r in range(ncol):
                    if r != c0v:
                        tile_copy(slab, c0v, r).wait_send()

    def part(h):
        return pl.ds(h * width, width)

    def row_copy(n, to_sec, c0v, d, h):
        q = c0v + d
        return pltpu.make_async_remote_copy(
            src_ref=fbuf.at[n, :, part(h)],
            dst_ref=xbuf.at[n, reach - d, :, part(h)],
            send_sem=ss1.at[n, reach - d, h],
            recv_sem=rs1.at[n, reach - d, h],
            device_id=(to_sec, (lat + q // ncol + nlat) % nlat, q % ncol),
            device_id_type=MESH_ID,
        )

    def send_rows(n, to_sec, local, h):
        for c0v in range(ncol):
            @pl.when(col == c0v)
            def _():
                for d in shifts:
                    if local and d == 0:
                        continue
                    row_copy(n, to_sec, c0v, d, h).start()
        if local:
            xbuf[n, reach, :, part(h)] = fbuf[n, :, part(h)]

    def wait_row_sends(n, to_sec, local):
        for c0v in range(ncol):
            @pl.when(col == c0v)
            def _():
                for h in range(chunks):
                    for d in shifts:
                        if local and d == 0:
                            continue
                        row_copy(n, to_sec, c0v, d, h).wait_send()

    def put_field(n, to_sec, local, h, value):
        fbuf[n, :, part(h)] = value.astype(jnp.bfloat16)
        send_rows(n, to_sec, local, h)

    def run_app(n, slab, local, finish):
        order = sorted(range(noff), key=lambda k: (abs(k - reach), k))
        dims = (((1,), (1,)), ((), ()))
        dot = functools.partial(lax.dot_general, dimension_numbers=dims, preferred_element_type=jnp.float32)
        for h in range(chunks):
            acc_r = None
            acc_i = None
            for k in order:
                d = k - reach
                if not (local and d == 0):
                    row_copy(n, sec, 0, -d, h).wait_recv()
                lo = (lat == 0) & (k < reach - col)
                hi = (lat == nlat - 1) & (k >= reach - col + ncol)

                @pl.when(lo | hi)
                def _():
                    sn = jnp.where(lo, -sin_v, sin_v)
                    x = xbuf[n, k, :, part(h)].astype(jnp.float32)
                    xbuf[n, k, 0, part(h)] = (x[0] * cos_v - x[1] * sn).astype(jnp.bfloat16)
                    xbuf[n, k, 1, part(h)] = (x[0] * sn + x[1] * cos_v).astype(jnp.bfloat16)

                xr = xbuf[n, k, 0, part(h)]
                xi = xbuf[n, k, 1, part(h)]
                tr = tiles2[slab, k, 0]
                ti = tiles2[slab, k, 1]
                re = dot(xr, tr) - dot(xi, ti)
                im = dot(xr, ti) + dot(xi, tr)
                acc_r = re if acc_r is None else acc_r + re
                acc_i = im if acc_i is None else acc_i + im
            finish(h, jnp.stack([acc_r, acc_i], 0))

    def transpose_in(dst, src):
        for ri in range(2):
            dst[ri] = src[ri].astype(jnp.float32).T.astype(jnp.bfloat16)

    @pl.when(sec == 0)
    def _():
        share_tiles(0)
        for ri in range(2):
            fbuf[0, ri] = src_ref[0, 0, ri].astype(jnp.float32).T.astype(jnp.bfloat16)
        for h in range(chunks):
            send_rows(0, 0, True, h)
        transpose_in(srct.at[1], src_ref.at[1, 0])
        share_tiles(1)
        wait_tiles(0)

        def fin0(h, r):
            vt[0, :, part(h)] = r
            put_field(1, 0, True, h, srct[1, :, part(h)].astype(jnp.float32) + coupling * r)

        run_app(0, 0, True, fin0)
        wait_tiles(1)
        src_copy = pltpu.make_async_remote_copy(
            src_ref=src_ref.at[0, 0], dst_ref=srcbuf, send_sem=ssrc, recv_sem=rsrc,
            device_id=(1, lat, col), device_id_type=MESH_ID,
        )

        def fin1(h, r):
            vt[1, :, part(h)] = r
            if h == 0:
                src_copy.wait_recv()
                transpose_in(srct.at[0], srcbuf)
            put_field(2, 1, False, h, srct[0, :, part(h)].astype(jnp.float32) + coupling * r)

        run_app(1, 1, True, fin1)

        def fin5(h, r):
            sol = vt[1, :, part(h)] + coupling * r
            outt[1, :, part(h)] = sol
            put_field(6, 0, True, h, sol)

        run_app(5, 1, False, fin5)

        def fin6(h, r):
            outt[0, :, part(h)] = vt[0, :, part(h)] + coupling * r

        run_app(6, 0, True, fin6)
        wait_row_sends(0, 0, True)
        wait_row_sends(1, 0, True)
        wait_row_sends(2, 1, False)
        wait_row_sends(6, 0, True)
        wait_tile_sends(0)
        wait_tile_sends(1)

    @pl.when(sec == 1)
    def _():
        src_copy = pltpu.make_async_remote_copy(
            src_ref=src_ref.at[0, 0], dst_ref=srcbuf, send_sem=ssrc, recv_sem=rsrc,
            device_id=(0, lat, col), device_id_type=MESH_ID,
        )
        src_copy.start()
        share_tiles(0)
        share_tiles(1)
        transpose_in(srct.at[1], src_ref.at[1, 0])
        wait_tiles(0)
        wait_tiles(1)

        def fin2(h, r):
            vt[0, :, part(h)] = r
            put_field(3, 1, True, h, srct[1, :, part(h)].astype(jnp.float32) + coupling * r)

        run_app(2, 0, False, fin2)

        def fin3(h, r):
            outt[1, :, part(h)] = r
            put_field(4, 1, True, h, r)

        run_app(3, 1, True, fin3)

        def fin4(h, r):
            sol = vt[0, :, part(h)] + coupling * r
            outt[0, :, part(h)] = sol
            put_field(5, 0, False, h, sol)

        run_app(4, 0, True, fin4)
        wait_row_sends(3, 1, True)
        wait_row_sends(4, 1, True)
        wait_row_sends(5, 0, False)
        wait_tile_sends(0)
        wait_tile_sends(1)
        src_copy.wait_send()

    for s in range(2):
        for ri in range(2):
            out_ref[s, 0, ri] = outt[s, ri].T


def shards(sources, inverse_tiles, pattern, phase_index):
    nlat = lax.axis_size("lat")
    ncol = lax.axis_size("col")
    koff = inverse_tiles.shape[2]
    reach = OFF // 2
    noff = koff * ncol
    blk, nrhs = sources.shape[3], sources.shape[4]
    angle = 2.0 * jnp.pi * phase_index[0].astype(jnp.float32) / PHASES
    trig = jnp.stack([jnp.cos(angle), jnp.sin(angle)])
    kernel = functools.partial(sweep_kernel, nlat, ncol, koff, reach, CHUNKS)
    vmem = pl.BlockSpec(memory_space=pltpu.VMEM)
    smem = pl.BlockSpec(memory_space=pltpu.SMEM)
    slabs = inverse_tiles.shape[0]
    return pl.pallas_call(
        kernel,
        out_shape=jax.ShapeDtypeStruct(sources.shape, jnp.float32),
        in_specs=[smem, smem, vmem, vmem],
        out_specs=vmem,
        scratch_shapes=[
            pltpu.VMEM(inverse_tiles.shape, jnp.bfloat16),
            pltpu.VMEM((slabs, noff, 2, blk, blk), jnp.bfloat16),
            pltpu.VMEM((APPS, noff, 2, nrhs, blk), jnp.bfloat16),
            pltpu.VMEM((APPS, 2, nrhs, blk), jnp.bfloat16),
            pltpu.VMEM((slabs, 2, nrhs, blk), jnp.bfloat16),
            pltpu.VMEM((slabs, 2, nrhs, blk), jnp.float32),
            pltpu.VMEM((slabs, 2, nrhs, blk), jnp.float32),
            pltpu.VMEM((2, blk, nrhs), jnp.bfloat16),
            pltpu.SemaphoreType.DMA((APPS, noff, CHUNKS)),
            pltpu.SemaphoreType.DMA((APPS, noff, CHUNKS)),
            pltpu.SemaphoreType.DMA((slabs, ncol)),
            pltpu.SemaphoreType.DMA((slabs, ncol)),
            pltpu.SemaphoreType.DMA(()),
            pltpu.SemaphoreType.DMA(()),
        ],
        compiler_params=pltpu.CompilerParams(
            has_side_effects=True, collective_id=0, vmem_limit_bytes=48 * 1024 * 1024
        ),
    )(trig, pattern, sources, inverse_tiles)


def solution(mesh):
    placed = (
        P("sec", ("lat", "col"), None, None, None),
        P("sec", "lat", "col", None, None, None),
        P("sec", "lat", "col"),
        P(),
    )
    return jax.shard_map(
        shards,
        mesh=mesh,
        in_specs=placed,
        out_specs=P("sec", ("lat", "col"), None, None, None),
        check_vma=False,
    )
```

```python
import functools

import jax
import jax.numpy as jnp
from jax import lax
from jax.experimental import pallas as pl
from jax.experimental.pallas import tpu as pltpu
from jax.sharding import PartitionSpec as P

OFF = 8
PHASES = 16
APPS = 7
CHUNKS = 2

coupling = 0.8

MESH_ID = pl.DeviceIdType.MESH


def sweep_kernel(
    nlat, ncol, koff, reach, chunks,
    trig_ref, pat_ref, src_hbm, tiles_hbm, out_ref,
    src_ref, tiles_ref, mtiles, tiles2, xbuf, fbuf, srct, vt, outt, srcbuf,
    rs1, ss1, rst, sst, rsrc, ssrc, lsem,
):
    sec = lax.axis_index("sec")
    lat = lax.axis_index("lat")
    col = lax.axis_index("col")
    cos_v = trig_ref[0]
    sin_v = trig_ref[1]
    noff = koff * ncol
    shifts = [d for d in range(reach - noff + 1, reach + 1)]
    width = xbuf.shape[3] // chunks

    loads = [pltpu.make_async_copy(src_hbm, src_ref, lsem.at[0])]
    for slab in range(tiles_ref.shape[0]):
        loads.append(pltpu.make_async_copy(tiles_hbm.at[slab], tiles_ref.at[slab], lsem.at[1 + slab]))
    for load in loads:
        load.start()

    barrier = pltpu.get_barrier_semaphore()
    partners = 0
    for ds in range(2):
        for dl in (-1, 0, 1):
            for c in range(ncol):
                if ds == 0 and dl == 0:
                    continue
                pl.semaphore_signal(
                    barrier, 1,
                    device_id=((sec + ds) % 2, (lat + dl + nlat) % nlat, (col + c) % ncol),
                    device_id_type=MESH_ID,
                )
                partners += 1
    for c in range(1, ncol):
        pl.semaphore_signal(
            barrier, 1, device_id=(sec, lat, (col + c) % ncol), device_id_type=MESH_ID
        )
        partners += 1
    pl.semaphore_wait(barrier, partners)
    loads[0].wait()

    def tile_copy(slab, c0v, r):
        return pltpu.make_async_remote_copy(
            src_ref=mtiles.at[slab, r],
            dst_ref=tiles2.at[slab, pl.ds(c0v * koff, koff)],
            send_sem=sst.at[slab, r],
            recv_sem=rst.at[slab, c0v],
            device_id=(sec, lat, r),
            device_id_type=MESH_ID,
        )

    def share_tiles(slab):
        loads[1 + slab].wait()
        for r in range(ncol):
            for j in range(koff):
                keep = pat_ref[slab, r, j] != 0
                tile = tiles_ref[slab, r, j]
                mtiles[slab, r, j] = jnp.where(keep, tile, jnp.zeros_like(tile))
        for c0v in range(ncol):
            @pl.when(col == c0v)
            def _():
                for r in range(ncol):
                    if r != c0v:
                        tile_copy(slab, c0v, r).start()
                tiles2[slab, pl.ds(c0v * koff, koff)] = mtiles[slab, c0v]

    def wait_tiles(slab):
        for c in range(ncol):
            @pl.when(col != c)
            def _():
                tile_copy(slab, c, c).wait_recv()

    def wait_tile_sends(slab):
        for c0v in range(ncol):
            @pl.when(col == c0v)
            def _():
                for r in range(ncol):
                    if r != c0v:
                        tile_copy(slab, c0v, r).wait_send()

    def part(h):
        return pl.ds(h * width, width)

    def row_copy(n, to_sec, c0v, d, h):
        q = c0v + d
        return pltpu.make_async_remote_copy(
            src_ref=fbuf.at[n, :, part(h)],
            dst_ref=xbuf.at[n, reach - d, :, part(h)],
            send_sem=ss1.at[n, reach - d, h],
            recv_sem=rs1.at[n, reach - d, h],
            device_id=(to_sec, (lat + q // ncol + nlat) % nlat, q % ncol),
            device_id_type=MESH_ID,
        )

    def send_rows(n, to_sec, local, h):
        for c0v in range(ncol):
            @pl.when(col == c0v)
            def _():
                for d in shifts:
                    if local and d == 0:
                        continue
                    row_copy(n, to_sec, c0v, d, h).start()
        if local:
            xbuf[n, reach, :, part(h)] = fbuf[n, :, part(h)]

    def wait_row_sends(n, to_sec, local):
        for c0v in range(ncol):
            @pl.when(col == c0v)
            def _():
                for h in range(chunks):
                    for d in shifts:
                        if local and d == 0:
                            continue
                        row_copy(n, to_sec, c0v, d, h).wait_send()

    def put_field(n, to_sec, local, h, value):
        fbuf[n, :, part(h)] = value.astype(jnp.bfloat16)
        send_rows(n, to_sec, local, h)

    def run_app(n, slab, local, finish):
        order = sorted(range(noff), key=lambda k: (abs(k - reach), k))
        dims = (((1,), (1,)), ((), ()))
        dot = functools.partial(lax.dot_general, dimension_numbers=dims, preferred_element_type=jnp.float32)
        for h in range(chunks):
            acc_r = None
            acc_i = None
            for k in order:
                d = k - reach
                if not (local and d == 0):
                    row_copy(n, sec, 0, -d, h).wait_recv()
                lo = (lat == 0) & (k < reach - col)
                hi = (lat == nlat - 1) & (k >= reach - col + ncol)

                @pl.when(lo | hi)
                def _():
                    sn = jnp.where(lo, -sin_v, sin_v)
                    x = xbuf[n, k, :, part(h)].astype(jnp.float32)
                    xbuf[n, k, 0, part(h)] = (x[0] * cos_v - x[1] * sn).astype(jnp.bfloat16)
                    xbuf[n, k, 1, part(h)] = (x[0] * sn + x[1] * cos_v).astype(jnp.bfloat16)

                xr = xbuf[n, k, 0, part(h)]
                xi = xbuf[n, k, 1, part(h)]
                tr = tiles2[slab, k, 0]
                ti = tiles2[slab, k, 1]
                re = dot(xr, tr) - dot(xi, ti)
                im = dot(xr, ti) + dot(xi, tr)
                acc_r = re if acc_r is None else acc_r + re
                acc_i = im if acc_i is None else acc_i + im
            finish(h, jnp.stack([acc_r, acc_i], 0))

    def transpose_in(dst, src):
        for ri in range(2):
            dst[ri] = src[ri].astype(jnp.float32).T.astype(jnp.bfloat16)

    @pl.when(sec == 0)
    def _():
        share_tiles(0)
        for ri in range(2):
            fbuf[0, ri] = src_ref[0, 0, ri].astype(jnp.float32).T.astype(jnp.bfloat16)
        for h in range(chunks):
            send_rows(0, 0, True, h)
        transpose_in(srct.at[1], src_ref.at[1, 0])
        share_tiles(1)
        wait_tiles(0)

        def fin0(h, r):
            vt[0, :, part(h)] = r
            put_field(1, 0, True, h, srct[1, :, part(h)].astype(jnp.float32) + coupling * r)

        run_app(0, 0, True, fin0)
        wait_tiles(1)
        src_copy = pltpu.make_async_remote_copy(
            src_ref=src_ref.at[0, 0], dst_ref=srcbuf, send_sem=ssrc, recv_sem=rsrc,
            device_id=(1, lat, col), device_id_type=MESH_ID,
        )

        def fin1(h, r):
            vt[1, :, part(h)] = r
            if h == 0:
                src_copy.wait_recv()
                transpose_in(srct.at[0], srcbuf)
            put_field(2, 1, False, h, srct[0, :, part(h)].astype(jnp.float32) + coupling * r)

        run_app(1, 1, True, fin1)

        def fin5(h, r):
            sol = vt[1, :, part(h)] + coupling * r
            outt[1, :, part(h)] = sol
            put_field(6, 0, True, h, sol)

        run_app(5, 1, False, fin5)

        def fin6(h, r):
            outt[0, :, part(h)] = vt[0, :, part(h)] + coupling * r

        run_app(6, 0, True, fin6)
        wait_row_sends(0, 0, True)
        wait_row_sends(1, 0, True)
        wait_row_sends(2, 1, False)
        wait_row_sends(6, 0, True)
        wait_tile_sends(0)
        wait_tile_sends(1)

    @pl.when(sec == 1)
    def _():
        src_copy = pltpu.make_async_remote_copy(
            src_ref=src_ref.at[0, 0], dst_ref=srcbuf, send_sem=ssrc, recv_sem=rsrc,
            device_id=(0, lat, col), device_id_type=MESH_ID,
        )
        src_copy.start()
        share_tiles(0)
        share_tiles(1)
        transpose_in(srct.at[1], src_ref.at[1, 0])
        wait_tiles(0)
        wait_tiles(1)

        def fin2(h, r):
            vt[0, :, part(h)] = r
            put_field(3, 1, True, h, srct[1, :, part(h)].astype(jnp.float32) + coupling * r)

        run_app(2, 0, False, fin2)

        def fin3(h, r):
            outt[1, :, part(h)] = r
            put_field(4, 1, True, h, r)

        run_app(3, 1, True, fin3)

        def fin4(h, r):
            sol = vt[0, :, part(h)] + coupling * r
            outt[0, :, part(h)] = sol
            put_field(5, 0, False, h, sol)

        run_app(4, 0, True, fin4)
        wait_row_sends(3, 1, True)
        wait_row_sends(4, 1, True)
        wait_row_sends(5, 0, False)
        wait_tile_sends(0)
        wait_tile_sends(1)
        src_copy.wait_send()

    for s in range(2):
        for ri in range(2):
            out_ref[s, 0, ri] = outt[s, ri].T


def shards(sources, inverse_tiles, pattern, phase_index):
    nlat = lax.axis_size("lat")
    ncol = lax.axis_size("col")
    koff = inverse_tiles.shape[2]
    reach = OFF // 2
    noff = koff * ncol
    blk, nrhs = sources.shape[3], sources.shape[4]
    angle = 2.0 * jnp.pi * phase_index[0].astype(jnp.float32) / PHASES
    trig = jnp.stack([jnp.cos(angle), jnp.sin(angle)])
    kernel = functools.partial(sweep_kernel, nlat, ncol, koff, reach, CHUNKS)
    vmem = pl.BlockSpec(memory_space=pltpu.VMEM)
    smem = pl.BlockSpec(memory_space=pltpu.SMEM)
    slabs = inverse_tiles.shape[0]
    return pl.pallas_call(
        kernel,
        out_shape=jax.ShapeDtypeStruct(sources.shape, jnp.float32),
        in_specs=[smem, smem, pl.BlockSpec(memory_space=pl.ANY), pl.BlockSpec(memory_space=pl.ANY)],
        out_specs=vmem,
        scratch_shapes=[
            pltpu.VMEM(sources.shape, jnp.bfloat16),
            pltpu.VMEM(inverse_tiles.shape, jnp.bfloat16),
            pltpu.VMEM(inverse_tiles.shape, jnp.bfloat16),
            pltpu.VMEM((slabs, noff, 2, blk, blk), jnp.bfloat16),
            pltpu.VMEM((APPS, noff, 2, nrhs, blk), jnp.bfloat16),
            pltpu.VMEM((APPS, 2, nrhs, blk), jnp.bfloat16),
            pltpu.VMEM((slabs, 2, nrhs, blk), jnp.bfloat16),
            pltpu.VMEM((slabs, 2, nrhs, blk), jnp.float32),
            pltpu.VMEM((slabs, 2, nrhs, blk), jnp.float32),
            pltpu.VMEM((2, blk, nrhs), jnp.bfloat16),
            pltpu.SemaphoreType.DMA((APPS, noff, CHUNKS)),
            pltpu.SemaphoreType.DMA((APPS, noff, CHUNKS)),
            pltpu.SemaphoreType.DMA((slabs, ncol)),
            pltpu.SemaphoreType.DMA((slabs, ncol)),
            pltpu.SemaphoreType.DMA(()),
            pltpu.SemaphoreType.DMA(()),
            pltpu.SemaphoreType.DMA((1 + slabs,)),
        ],
        compiler_params=pltpu.CompilerParams(
            has_side_effects=True, collective_id=0, vmem_limit_bytes=67043328
        ),
    )(trig, pattern, sources, inverse_tiles)


def solution(mesh):
    placed = (
        P("sec", ("lat", "col"), None, None, None),
        P("sec", "lat", "col", None, None, None),
        P("sec", "lat", "col"),
        P(),
    )
    return jax.shard_map(
        shards,
        mesh=mesh,
        in_specs=placed,
        out_specs=P("sec", ("lat", "col"), None, None, None),
        check_vma=False,
    )
```

```python
import functools

import jax
import jax.numpy as jnp
from jax import lax
from jax.experimental import pallas as pl
from jax.experimental.pallas import tpu as pltpu
from jax.sharding import PartitionSpec as P

OFF = 8
PHASES = 16
APPS = 7
CHUNKS = 2

coupling = 0.8

MESH_ID = pl.DeviceIdType.MESH


def sweep_kernel(
    nlat, ncol, koff, reach, chunks,
    trig_ref, pat_ref, src_hbm, tiles_hbm, out_ref,
    src_ref, tiles_ref, mtiles, tiles2, xbuf, fbuf, srct, vt, outt, srcbuf,
    rs1, ss1, rst, sst, rsrc, ssrc, lsem,
):
    sec = lax.axis_index("sec")
    lat = lax.axis_index("lat")
    col = lax.axis_index("col")
    cos_v = trig_ref[0]
    sin_v = trig_ref[1]
    noff = koff * ncol
    shifts = [d for d in range(reach - noff + 1, reach + 1)]
    width = xbuf.shape[3] // chunks

    loads = [pltpu.make_async_copy(src_hbm, src_ref, lsem.at[0])]
    for slab in range(tiles_ref.shape[0]):
        loads.append(pltpu.make_async_copy(tiles_hbm.at[slab], tiles_ref.at[slab], lsem.at[1 + slab]))
    for load in loads:
        load.start()

    barrier = pltpu.get_barrier_semaphore()
    partners = 0
    for ds in range(2):
        for dl in (-1, 0, 1):
            for c in range(ncol):
                if ds == 0 and dl == 0:
                    continue
                pl.semaphore_signal(
                    barrier, 1,
                    device_id=((sec + ds) % 2, (lat + dl + nlat) % nlat, (col + c) % ncol),
                    device_id_type=MESH_ID,
                )
                partners += 1
    for c in range(1, ncol):
        pl.semaphore_signal(
            barrier, 1, device_id=(sec, lat, (col + c) % ncol), device_id_type=MESH_ID
        )
        partners += 1
    pl.semaphore_wait(barrier, partners)
    loads[0].wait()

    def tile_copy(slab, c0v, r):
        return pltpu.make_async_remote_copy(
            src_ref=mtiles.at[slab, r],
            dst_ref=tiles2.at[slab, pl.ds(c0v * koff, koff)],
            send_sem=sst.at[slab, r],
            recv_sem=rst.at[slab, c0v],
            device_id=(sec, lat, r),
            device_id_type=MESH_ID,
        )

    def share_tiles(slab):
        loads[1 + slab].wait()
        for r in range(ncol):
            for j in range(koff):
                keep = pat_ref[slab, r, j] != 0
                tile = tiles_ref[slab, r, j]
                mtiles[slab, r, j] = jnp.where(keep, tile, jnp.zeros_like(tile))
        for c0v in range(ncol):
            @pl.when(col == c0v)
            def _():
                for r in range(ncol):
                    if r != c0v:
                        tile_copy(slab, c0v, r).start()
                tiles2[slab, pl.ds(c0v * koff, koff)] = mtiles[slab, c0v]

    def wait_tiles(slab):
        for c in range(ncol):
            @pl.when(col != c)
            def _():
                tile_copy(slab, c, c).wait_recv()

    def wait_tile_sends(slab):
        for c0v in range(ncol):
            @pl.when(col == c0v)
            def _():
                for r in range(ncol):
                    if r != c0v:
                        tile_copy(slab, c0v, r).wait_send()

    def part(h):
        return pl.ds(h * width, width)

    def row_copy(n, to_sec, c0v, d, h):
        q = c0v + d
        return pltpu.make_async_remote_copy(
            src_ref=fbuf.at[n, :, part(h)],
            dst_ref=xbuf.at[n, reach - d, :, part(h)],
            send_sem=ss1.at[n, reach - d, h],
            recv_sem=rs1.at[n, reach - d, h],
            device_id=(to_sec, (lat + q // ncol + nlat) % nlat, q % ncol),
            device_id_type=MESH_ID,
        )

    def far_first(c0v):
        def hops(d):
            q = c0v + d
            gap = abs(q % ncol - c0v)
            return min(gap, ncol - gap) + (q // ncol != 0)
        return sorted(shifts, key=lambda d: (-hops(d), d))

    def send_rows(n, to_sec, local, h):
        for c0v in range(ncol):
            @pl.when(col == c0v)
            def _():
                for d in far_first(c0v):
                    if local and d == 0:
                        continue
                    row_copy(n, to_sec, c0v, d, h).start()
        if local:
            xbuf[n, reach, :, part(h)] = fbuf[n, :, part(h)]

    def wait_row_sends(n, to_sec, local):
        for c0v in range(ncol):
            @pl.when(col == c0v)
            def _():
                for h in range(chunks):
                    for d in shifts:
                        if local and d == 0:
                            continue
                        row_copy(n, to_sec, c0v, d, h).wait_send()

    def put_field(n, to_sec, local, h, value):
        fbuf[n, :, part(h)] = value.astype(jnp.bfloat16)
        send_rows(n, to_sec, local, h)

    def run_app(n, slab, local, finish):
        order = sorted(range(noff), key=lambda k: (abs(k - reach), k))
        dims = (((1,), (1,)), ((), ()))
        dot = functools.partial(lax.dot_general, dimension_numbers=dims, preferred_element_type=jnp.float32)
        for h in range(chunks):
            acc_r = None
            acc_i = None
            for k in order:
                d = k - reach
                if not (local and d == 0):
                    row_copy(n, sec, 0, -d, h).wait_recv()
                lo = (lat == 0) & (k < reach - col)
                hi = (lat == nlat - 1) & (k >= reach - col + ncol)

                @pl.when(lo | hi)
                def _():
                    sn = jnp.where(lo, -sin_v, sin_v)
                    x = xbuf[n, k, :, part(h)].astype(jnp.float32)
                    xbuf[n, k, 0, part(h)] = (x[0] * cos_v - x[1] * sn).astype(jnp.bfloat16)
                    xbuf[n, k, 1, part(h)] = (x[0] * sn + x[1] * cos_v).astype(jnp.bfloat16)

                xr = xbuf[n, k, 0, part(h)]
                xi = xbuf[n, k, 1, part(h)]
                tr = tiles2[slab, k, 0]
                ti = tiles2[slab, k, 1]
                re = dot(xr, tr) - dot(xi, ti)
                im = dot(xr, ti) + dot(xi, tr)
                acc_r = re if acc_r is None else acc_r + re
                acc_i = im if acc_i is None else acc_i + im
            finish(h, jnp.stack([acc_r, acc_i], 0))

    def transpose_in(dst, src):
        for ri in range(2):
            dst[ri] = src[ri].astype(jnp.float32).T.astype(jnp.bfloat16)

    @pl.when(sec == 0)
    def _():
        share_tiles(0)
        for ri in range(2):
            fbuf[0, ri] = src_ref[0, 0, ri].astype(jnp.float32).T.astype(jnp.bfloat16)
        for h in range(chunks):
            send_rows(0, 0, True, h)
        transpose_in(srct.at[1], src_ref.at[1, 0])
        share_tiles(1)
        wait_tiles(0)

        def fin0(h, r):
            vt[0, :, part(h)] = r
            put_field(1, 0, True, h, srct[1, :, part(h)].astype(jnp.float32) + coupling * r)

        run_app(0, 0, True, fin0)
        wait_tiles(1)
        src_copy = pltpu.make_async_remote_copy(
            src_ref=src_ref.at[0, 0], dst_ref=srcbuf, send_sem=ssrc, recv_sem=rsrc,
            device_id=(1, lat, col), device_id_type=MESH_ID,
        )

        def fin1(h, r):
            vt[1, :, part(h)] = r
            if h == 0:
                src_copy.wait_recv()
                transpose_in(srct.at[0], srcbuf)
            put_field(2, 1, False, h, srct[0, :, part(h)].astype(jnp.float32) + coupling * r)

        run_app(1, 1, True, fin1)

        def fin5(h, r):
            sol = vt[1, :, part(h)] + coupling * r
            outt[1, :, part(h)] = sol
            put_field(6, 0, True, h, sol)

        run_app(5, 1, False, fin5)

        def fin6(h, r):
            outt[0, :, part(h)] = vt[0, :, part(h)] + coupling * r

        run_app(6, 0, True, fin6)
        wait_row_sends(0, 0, True)
        wait_row_sends(1, 0, True)
        wait_row_sends(2, 1, False)
        wait_row_sends(6, 0, True)
        wait_tile_sends(0)
        wait_tile_sends(1)

    @pl.when(sec == 1)
    def _():
        src_copy = pltpu.make_async_remote_copy(
            src_ref=src_ref.at[0, 0], dst_ref=srcbuf, send_sem=ssrc, recv_sem=rsrc,
            device_id=(0, lat, col), device_id_type=MESH_ID,
        )
        src_copy.start()
        share_tiles(0)
        share_tiles(1)
        transpose_in(srct.at[1], src_ref.at[1, 0])
        wait_tiles(0)
        wait_tiles(1)

        def fin2(h, r):
            vt[0, :, part(h)] = r
            put_field(3, 1, True, h, srct[1, :, part(h)].astype(jnp.float32) + coupling * r)

        run_app(2, 0, False, fin2)

        def fin3(h, r):
            outt[1, :, part(h)] = r
            put_field(4, 1, True, h, r)

        run_app(3, 1, True, fin3)

        def fin4(h, r):
            sol = vt[0, :, part(h)] + coupling * r
            outt[0, :, part(h)] = sol
            put_field(5, 0, False, h, sol)

        run_app(4, 0, True, fin4)
        wait_row_sends(3, 1, True)
        wait_row_sends(4, 1, True)
        wait_row_sends(5, 0, False)
        wait_tile_sends(0)
        wait_tile_sends(1)
        src_copy.wait_send()

    for s in range(2):
        for ri in range(2):
            out_ref[s, 0, ri] = outt[s, ri].T


def shards(sources, inverse_tiles, pattern, phase_index):
    nlat = lax.axis_size("lat")
    ncol = lax.axis_size("col")
    koff = inverse_tiles.shape[2]
    reach = OFF // 2
    noff = koff * ncol
    blk, nrhs = sources.shape[3], sources.shape[4]
    angle = 2.0 * jnp.pi * phase_index[0].astype(jnp.float32) / PHASES
    trig = jnp.stack([jnp.cos(angle), jnp.sin(angle)])
    kernel = functools.partial(sweep_kernel, nlat, ncol, koff, reach, CHUNKS)
    vmem = pl.BlockSpec(memory_space=pltpu.VMEM)
    smem = pl.BlockSpec(memory_space=pltpu.SMEM)
    slabs = inverse_tiles.shape[0]
    return pl.pallas_call(
        kernel,
        out_shape=jax.ShapeDtypeStruct(sources.shape, jnp.float32),
        in_specs=[smem, smem, pl.BlockSpec(memory_space=pl.ANY), pl.BlockSpec(memory_space=pl.ANY)],
        out_specs=vmem,
        scratch_shapes=[
            pltpu.VMEM(sources.shape, jnp.bfloat16),
            pltpu.VMEM(inverse_tiles.shape, jnp.bfloat16),
            pltpu.VMEM(inverse_tiles.shape, jnp.bfloat16),
            pltpu.VMEM((slabs, noff, 2, blk, blk), jnp.bfloat16),
            pltpu.VMEM((APPS, noff, 2, nrhs, blk), jnp.bfloat16),
            pltpu.VMEM((APPS, 2, nrhs, blk), jnp.bfloat16),
            pltpu.VMEM((slabs, 2, nrhs, blk), jnp.bfloat16),
            pltpu.VMEM((slabs, 2, nrhs, blk), jnp.float32),
            pltpu.VMEM((slabs, 2, nrhs, blk), jnp.float32),
            pltpu.VMEM((2, blk, nrhs), jnp.bfloat16),
            pltpu.SemaphoreType.DMA((APPS, noff, CHUNKS)),
            pltpu.SemaphoreType.DMA((APPS, noff, CHUNKS)),
            pltpu.SemaphoreType.DMA((slabs, ncol)),
            pltpu.SemaphoreType.DMA((slabs, ncol)),
            pltpu.SemaphoreType.DMA(()),
            pltpu.SemaphoreType.DMA(()),
            pltpu.SemaphoreType.DMA((1 + slabs,)),
        ],
        compiler_params=pltpu.CompilerParams(
            has_side_effects=True, collective_id=0, vmem_limit_bytes=67043328
        ),
    )(trig, pattern, sources, inverse_tiles)


def solution(mesh):
    placed = (
        P("sec", ("lat", "col"), None, None, None),
        P("sec", "lat", "col", None, None, None),
        P("sec", "lat", "col"),
        P(),
    )
    return jax.shard_map(
        shards,
        mesh=mesh,
        in_specs=placed,
        out_specs=P("sec", ("lat", "col"), None, None, None),
        check_vma=False,
    )
```

```python
import functools

import jax
import jax.numpy as jnp
from jax import lax
from jax.experimental import pallas as pl
from jax.experimental.pallas import tpu as pltpu
from jax.sharding import PartitionSpec as P

OFF = 8
PHASES = 16
APPS = 7
CHUNKS = 2

coupling = 0.8

MESH_ID = pl.DeviceIdType.MESH


def sweep_kernel(
    nlat, ncol, koff, reach, chunks,
    trig_ref, pat_ref, src_hbm, tiles_hbm, out_ref,
    src_ref, tiles_ref, mtiles, tiles2, xbuf, fbuf, srct, vt, outt, srcbuf,
    rs1, ss1, rst, sst, rsrc, ssrc, lsem,
):
    sec = lax.axis_index("sec")
    lat = lax.axis_index("lat")
    col = lax.axis_index("col")
    cos_v = trig_ref[0]
    sin_v = trig_ref[1]
    noff = koff * ncol
    shifts = [d for d in range(reach - noff + 1, reach + 1)]
    width = xbuf.shape[3] // chunks

    loads = [pltpu.make_async_copy(src_hbm, src_ref, lsem.at[0])]
    for slab in range(tiles_ref.shape[0]):
        loads.append(pltpu.make_async_copy(tiles_hbm.at[slab], tiles_ref.at[slab], lsem.at[1 + slab]))
    for load in loads:
        load.start()

    barrier = pltpu.get_barrier_semaphore()
    partners = 0
    for ds in range(2):
        for dl in (-1, 0, 1):
            for c in range(ncol):
                if ds == 0 and dl == 0:
                    continue
                pl.semaphore_signal(
                    barrier, 1,
                    device_id=((sec + ds) % 2, (lat + dl + nlat) % nlat, (col + c) % ncol),
                    device_id_type=MESH_ID,
                )
                partners += 1
    for c in range(1, ncol):
        pl.semaphore_signal(
            barrier, 1, device_id=(sec, lat, (col + c) % ncol), device_id_type=MESH_ID
        )
        partners += 1
    pl.semaphore_wait(barrier, partners)
    loads[0].wait()

    def tile_copy(slab, c0v, r):
        return pltpu.make_async_remote_copy(
            src_ref=mtiles.at[slab, r],
            dst_ref=tiles2.at[slab, pl.ds(c0v * koff, koff)],
            send_sem=sst.at[slab, r],
            recv_sem=rst.at[slab, c0v],
            device_id=(sec, lat, r),
            device_id_type=MESH_ID,
        )

    def share_tiles(slab):
        loads[1 + slab].wait()
        for r in range(ncol):
            for j in range(koff):
                keep = pat_ref[slab, r, j] != 0
                tile = tiles_ref[slab, r, j]
                mtiles[slab, r, j] = jnp.where(keep, tile, jnp.zeros_like(tile))
        for c0v in range(ncol):
            @pl.when(col == c0v)
            def _():
                for r in range(ncol):
                    if r != c0v:
                        tile_copy(slab, c0v, r).start()
                tiles2[slab, pl.ds(c0v * koff, koff)] = mtiles[slab, c0v]

    def wait_tiles(slab):
        for c in range(ncol):
            @pl.when(col != c)
            def _():
                tile_copy(slab, c, c).wait_recv()
        for k in range(noff):
            for ri in range(2):
                tiles2[slab, k, ri] = tiles2[slab, k, ri].T

    def wait_tile_sends(slab):
        for c0v in range(ncol):
            @pl.when(col == c0v)
            def _():
                for r in range(ncol):
                    if r != c0v:
                        tile_copy(slab, c0v, r).wait_send()

    def part(h):
        return pl.ds(h * width, width)

    def row_copy(n, to_sec, c0v, d, h):
        q = c0v + d
        return pltpu.make_async_remote_copy(
            src_ref=fbuf.at[n, :, part(h)],
            dst_ref=xbuf.at[n, reach - d, :, part(h)],
            send_sem=ss1.at[n, reach - d, h],
            recv_sem=rs1.at[n, reach - d, h],
            device_id=(to_sec, (lat + q // ncol + nlat) % nlat, q % ncol),
            device_id_type=MESH_ID,
        )

    def far_first(c0v):
        def hops(d):
            q = c0v + d
            gap = abs(q % ncol - c0v)
            return min(gap, ncol - gap) + (q // ncol != 0)
        return sorted(shifts, key=lambda d: (-hops(d), d))

    def send_rows(n, to_sec, local, h):
        for c0v in range(ncol):
            @pl.when(col == c0v)
            def _():
                for d in far_first(c0v):
                    if local and d == 0:
                        continue
                    row_copy(n, to_sec, c0v, d, h).start()
        if local:
            xbuf[n, reach, :, part(h)] = fbuf[n, :, part(h)]

    def wait_row_sends(n, to_sec, local):
        for c0v in range(ncol):
            @pl.when(col == c0v)
            def _():
                for h in range(chunks):
                    for d in shifts:
                        if local and d == 0:
                            continue
                        row_copy(n, to_sec, c0v, d, h).wait_send()

    def put_field(n, to_sec, local, h, value):
        fbuf[n, :, part(h)] = value.astype(jnp.bfloat16)
        send_rows(n, to_sec, local, h)

    def run_app(n, slab, local, finish):
        order = sorted(range(noff), key=lambda k: (abs(k - reach), k))
        dot = functools.partial(jnp.dot, preferred_element_type=jnp.float32)
        for h in range(chunks):
            acc_r = None
            acc_i = None
            for k in order:
                d = k - reach
                if not (local and d == 0):
                    row_copy(n, sec, 0, -d, h).wait_recv()
                lo = (lat == 0) & (k < reach - col)
                hi = (lat == nlat - 1) & (k >= reach - col + ncol)

                @pl.when(lo | hi)
                def _():
                    sn = jnp.where(lo, -sin_v, sin_v)
                    x = xbuf[n, k, :, part(h)].astype(jnp.float32)
                    xbuf[n, k, 0, part(h)] = (x[0] * cos_v - x[1] * sn).astype(jnp.bfloat16)
                    xbuf[n, k, 1, part(h)] = (x[0] * sn + x[1] * cos_v).astype(jnp.bfloat16)

                xr = xbuf[n, k, 0, part(h)]
                xi = xbuf[n, k, 1, part(h)]
                tr = tiles2[slab, k, 0]
                ti = tiles2[slab, k, 1]
                re = dot(xr, tr) - dot(xi, ti)
                im = dot(xr, ti) + dot(xi, tr)
                acc_r = re if acc_r is None else acc_r + re
                acc_i = im if acc_i is None else acc_i + im
            finish(h, jnp.stack([acc_r, acc_i], 0))

    def transpose_in(dst, src):
        for ri in range(2):
            dst[ri] = src[ri].astype(jnp.float32).T.astype(jnp.bfloat16)

    @pl.when(sec == 0)
    def _():
        share_tiles(0)
        for ri in range(2):
            fbuf[0, ri] = src_ref[0, 0, ri].astype(jnp.float32).T.astype(jnp.bfloat16)
        for h in range(chunks):
            send_rows(0, 0, True, h)
        transpose_in(srct.at[1], src_ref.at[1, 0])
        share_tiles(1)
        wait_tiles(0)

        def fin0(h, r):
            vt[0, :, part(h)] = r
            put_field(1, 0, True, h, srct[1, :, part(h)].astype(jnp.float32) + coupling * r)

        run_app(0, 0, True, fin0)
        wait_tiles(1)
        src_copy = pltpu.make_async_remote_copy(
            src_ref=src_ref.at[0, 0], dst_ref=srcbuf, send_sem=ssrc, recv_sem=rsrc,
            device_id=(1, lat, col), device_id_type=MESH_ID,
        )

        def fin1(h, r):
            vt[1, :, part(h)] = r
            if h == 0:
                src_copy.wait_recv()
                transpose_in(srct.at[0], srcbuf)
            put_field(2, 1, False, h, srct[0, :, part(h)].astype(jnp.float32) + coupling * r)

        run_app(1, 1, True, fin1)

        def fin5(h, r):
            sol = vt[1, :, part(h)] + coupling * r
            outt[1, :, part(h)] = sol
            put_field(6, 0, True, h, sol)

        run_app(5, 1, False, fin5)

        def fin6(h, r):
            outt[0, :, part(h)] = vt[0, :, part(h)] + coupling * r

        run_app(6, 0, True, fin6)
        wait_row_sends(0, 0, True)
        wait_row_sends(1, 0, True)
        wait_row_sends(2, 1, False)
        wait_row_sends(6, 0, True)
        wait_tile_sends(0)
        wait_tile_sends(1)

    @pl.when(sec == 1)
    def _():
        src_copy = pltpu.make_async_remote_copy(
            src_ref=src_ref.at[0, 0], dst_ref=srcbuf, send_sem=ssrc, recv_sem=rsrc,
            device_id=(0, lat, col), device_id_type=MESH_ID,
        )
        src_copy.start()
        share_tiles(0)
        share_tiles(1)
        transpose_in(srct.at[1], src_ref.at[1, 0])
        wait_tiles(0)
        wait_tiles(1)

        def fin2(h, r):
            vt[0, :, part(h)] = r
            put_field(3, 1, True, h, srct[1, :, part(h)].astype(jnp.float32) + coupling * r)

        run_app(2, 0, False, fin2)

        def fin3(h, r):
            outt[1, :, part(h)] = r
            put_field(4, 1, True, h, r)

        run_app(3, 1, True, fin3)

        def fin4(h, r):
            sol = vt[0, :, part(h)] + coupling * r
            outt[0, :, part(h)] = sol
            put_field(5, 0, False, h, sol)

        run_app(4, 0, True, fin4)
        wait_row_sends(3, 1, True)
        wait_row_sends(4, 1, True)
        wait_row_sends(5, 0, False)
        wait_tile_sends(0)
        wait_tile_sends(1)
        src_copy.wait_send()

    for s in range(2):
        for ri in range(2):
            out_ref[s, 0, ri] = outt[s, ri].T


def shards(sources, inverse_tiles, pattern, phase_index):
    nlat = lax.axis_size("lat")
    ncol = lax.axis_size("col")
    koff = inverse_tiles.shape[2]
    reach = OFF // 2
    noff = koff * ncol
    blk, nrhs = sources.shape[3], sources.shape[4]
    angle = 2.0 * jnp.pi * phase_index[0].astype(jnp.float32) / PHASES
    trig = jnp.stack([jnp.cos(angle), jnp.sin(angle)])
    kernel = functools.partial(sweep_kernel, nlat, ncol, koff, reach, CHUNKS)
    vmem = pl.BlockSpec(memory_space=pltpu.VMEM)
    smem = pl.BlockSpec(memory_space=pltpu.SMEM)
    slabs = inverse_tiles.shape[0]
    return pl.pallas_call(
        kernel,
        out_shape=jax.ShapeDtypeStruct(sources.shape, jnp.float32),
        in_specs=[smem, smem, pl.BlockSpec(memory_space=pl.ANY), pl.BlockSpec(memory_space=pl.ANY)],
        out_specs=vmem,
        scratch_shapes=[
            pltpu.VMEM(sources.shape, jnp.bfloat16),
            pltpu.VMEM(inverse_tiles.shape, jnp.bfloat16),
            pltpu.VMEM(inverse_tiles.shape, jnp.bfloat16),
            pltpu.VMEM((slabs, noff, 2, blk, blk), jnp.bfloat16),
            pltpu.VMEM((APPS, noff, 2, nrhs, blk), jnp.bfloat16),
            pltpu.VMEM((APPS, 2, nrhs, blk), jnp.bfloat16),
            pltpu.VMEM((slabs, 2, nrhs, blk), jnp.bfloat16),
            pltpu.VMEM((slabs, 2, nrhs, blk), jnp.float32),
            pltpu.VMEM((slabs, 2, nrhs, blk), jnp.float32),
            pltpu.VMEM((2, blk, nrhs), jnp.bfloat16),
            pltpu.SemaphoreType.DMA((APPS, noff, CHUNKS)),
            pltpu.SemaphoreType.DMA((APPS, noff, CHUNKS)),
            pltpu.SemaphoreType.DMA((slabs, ncol)),
            pltpu.SemaphoreType.DMA((slabs, ncol)),
            pltpu.SemaphoreType.DMA(()),
            pltpu.SemaphoreType.DMA(()),
            pltpu.SemaphoreType.DMA((1 + slabs,)),
        ],
        compiler_params=pltpu.CompilerParams(
            has_side_effects=True, collective_id=0, vmem_limit_bytes=67043328
        ),
    )(trig, pattern, sources, inverse_tiles)


def solution(mesh):
    placed = (
        P("sec", ("lat", "col"), None, None, None),
        P("sec", "lat", "col", None, None, None),
        P("sec", "lat", "col"),
        P(),
    )
    return jax.shard_map(
        shards,
        mesh=mesh,
        in_specs=placed,
        out_specs=P("sec", ("lat", "col"), None, None, None),
        check_vma=False,
    )
```

```python
import functools

import jax
import jax.numpy as jnp
from jax import lax
from jax.experimental import pallas as pl
from jax.experimental.pallas import tpu as pltpu
from jax.sharding import PartitionSpec as P

OFF = 8
PHASES = 16
APPS = 7
CHUNKS = 2

coupling = 0.8

MESH_ID = pl.DeviceIdType.MESH


def sweep_kernel(
    nlat, ncol, koff, reach, chunks,
    trig_ref, pat_ref, src_hbm, tiles_hbm, out_ref,
    src_ref, tiles_ref, mtiles, tiles2, xbuf, fbuf, srct, vt, outt, srcbuf,
    rs1, ss1, rst, sst, rsrc, ssrc, lsem,
):
    sec = lax.axis_index("sec")
    lat = lax.axis_index("lat")
    col = lax.axis_index("col")
    cos_v = trig_ref[0]
    sin_v = trig_ref[1]
    noff = koff * ncol
    shifts = [d for d in range(reach - noff + 1, reach + 1)]
    width = xbuf.shape[3] // chunks

    loads = [pltpu.make_async_copy(src_hbm, src_ref, lsem.at[0])]
    for slab in range(tiles_ref.shape[0]):
        loads.append(pltpu.make_async_copy(tiles_hbm.at[slab], tiles_ref.at[slab], lsem.at[1 + slab]))
    for load in loads:
        load.start()

    barrier = pltpu.get_barrier_semaphore()
    partners = 0
    for ds in range(2):
        for d in range(-reach, reach + 1):
            if ds == 0 and d == 0:
                continue
            q = col + d
            pl.semaphore_signal(
                barrier, 1,
                device_id=((sec + ds) % 2, (lat + q // ncol + nlat) % nlat, (q + ncol) % ncol),
                device_id_type=MESH_ID,
            )
            partners += 1
    pl.semaphore_wait(barrier, partners)
    loads[0].wait()

    def tile_copy(slab, c0v, r):
        return pltpu.make_async_remote_copy(
            src_ref=mtiles.at[slab, r],
            dst_ref=tiles2.at[slab, pl.ds(c0v * koff, koff)],
            send_sem=sst.at[slab, r],
            recv_sem=rst.at[slab, c0v],
            device_id=(sec, lat, r),
            device_id_type=MESH_ID,
        )

    def share_tiles(slab):
        loads[1 + slab].wait()
        for r in range(ncol):
            for j in range(koff):
                keep = pat_ref[slab, r, j] != 0
                tile = tiles_ref[slab, r, j]
                mtiles[slab, r, j] = jnp.where(keep, tile, jnp.zeros_like(tile))
        for c0v in range(ncol):
            @pl.when(col == c0v)
            def _():
                for r in range(ncol):
                    if r != c0v:
                        tile_copy(slab, c0v, r).start()
                tiles2[slab, pl.ds(c0v * koff, koff)] = mtiles[slab, c0v]

    def wait_tiles(slab):
        for c in range(ncol):
            @pl.when(col != c)
            def _():
                tile_copy(slab, c, c).wait_recv()
        for k in range(noff):
            for ri in range(2):
                tiles2[slab, k, ri] = tiles2[slab, k, ri].T

    def wait_tile_sends(slab):
        for c0v in range(ncol):
            @pl.when(col == c0v)
            def _():
                for r in range(ncol):
                    if r != c0v:
                        tile_copy(slab, c0v, r).wait_send()

    def part(h):
        return pl.ds(h * width, width)

    def row_copy(n, to_sec, c0v, d, h):
        q = c0v + d
        return pltpu.make_async_remote_copy(
            src_ref=fbuf.at[n, :, part(h)],
            dst_ref=xbuf.at[n, reach - d, :, part(h)],
            send_sem=ss1.at[n, reach - d, h],
            recv_sem=rs1.at[n, reach - d, h],
            device_id=(to_sec, (lat + q // ncol + nlat) % nlat, q % ncol),
            device_id_type=MESH_ID,
        )

    def far_first(c0v):
        def hops(d):
            q = c0v + d
            gap = abs(q % ncol - c0v)
            return min(gap, ncol - gap) + (q // ncol != 0)
        return sorted(shifts, key=lambda d: (-hops(d), d))

    def send_rows(n, to_sec, local, h):
        for c0v in range(ncol):
            @pl.when(col == c0v)
            def _():
                for d in far_first(c0v):
                    if local and d == 0:
                        continue
                    row_copy(n, to_sec, c0v, d, h).start()

    def wait_row_sends(n, to_sec, local):
        for c0v in range(ncol):
            @pl.when(col == c0v)
            def _():
                for h in range(chunks):
                    for d in shifts:
                        if local and d == 0:
                            continue
                        row_copy(n, to_sec, c0v, d, h).wait_send()

    def put_field(n, to_sec, local, h, value):
        fbuf[n, :, part(h)] = value.astype(jnp.bfloat16)
        send_rows(n, to_sec, local, h)

    def run_app(n, slab, local, finish):
        order = sorted(range(noff), key=lambda k: (abs(k - reach), k))
        dot = functools.partial(jnp.dot, preferred_element_type=jnp.float32)
        for h in range(chunks):
            acc_r = None
            acc_i = None
            for k in order:
                d = k - reach
                if not (local and d == 0):
                    row_copy(n, sec, 0, -d, h).wait_recv()
                lo = (lat == 0) & (k < reach - col)
                hi = (lat == nlat - 1) & (k >= reach - col + ncol)

                @pl.when((lo | hi) & (not (local and d == 0)))
                def _():
                    sn = jnp.where(lo, -sin_v, sin_v)
                    x = xbuf[n, k, :, part(h)].astype(jnp.float32)
                    xbuf[n, k, 0, part(h)] = (x[0] * cos_v - x[1] * sn).astype(jnp.bfloat16)
                    xbuf[n, k, 1, part(h)] = (x[0] * sn + x[1] * cos_v).astype(jnp.bfloat16)

                if local and d == 0:
                    xr = fbuf[n, 0, part(h)]
                    xi = fbuf[n, 1, part(h)]
                else:
                    xr = xbuf[n, k, 0, part(h)]
                    xi = xbuf[n, k, 1, part(h)]
                tr = tiles2[slab, k, 0]
                ti = tiles2[slab, k, 1]
                re = dot(xr, tr) - dot(xi, ti)
                im = dot(xr, ti) + dot(xi, tr)
                acc_r = re if acc_r is None else acc_r + re
                acc_i = im if acc_i is None else acc_i + im
            finish(h, jnp.stack([acc_r, acc_i], 0))

    def transpose_in(dst, src):
        for ri in range(2):
            dst[ri] = src[ri].astype(jnp.float32).T.astype(jnp.bfloat16)

    @pl.when(sec == 0)
    def _():
        share_tiles(0)
        for ri in range(2):
            fbuf[0, ri] = src_ref[0, 0, ri].astype(jnp.float32).T.astype(jnp.bfloat16)
        for h in range(chunks):
            send_rows(0, 0, True, h)
        transpose_in(srct.at[1], src_ref.at[1, 0])
        share_tiles(1)
        wait_tiles(0)

        def fin0(h, r):
            vt[0, :, part(h)] = r
            put_field(1, 0, True, h, srct[1, :, part(h)].astype(jnp.float32) + coupling * r)

        run_app(0, 0, True, fin0)
        wait_tiles(1)
        src_copy = pltpu.make_async_remote_copy(
            src_ref=src_ref.at[0, 0], dst_ref=srcbuf, send_sem=ssrc, recv_sem=rsrc,
            device_id=(1, lat, col), device_id_type=MESH_ID,
        )

        def fin1(h, r):
            vt[1, :, part(h)] = r
            if h == 0:
                src_copy.wait_recv()
                transpose_in(srct.at[0], srcbuf)
            put_field(2, 1, False, h, srct[0, :, part(h)].astype(jnp.float32) + coupling * r)

        run_app(1, 1, True, fin1)

        def fin5(h, r):
            sol = vt[1, :, part(h)] + coupling * r
            outt[1, :, part(h)] = sol
            put_field(6, 0, True, h, sol)

        run_app(5, 1, False, fin5)

        def fin6(h, r):
            outt[0, :, part(h)] = vt[0, :, part(h)] + coupling * r

        run_app(6, 0, True, fin6)
        wait_row_sends(0, 0, True)
        wait_row_sends(1, 0, True)
        wait_row_sends(2, 1, False)
        wait_row_sends(6, 0, True)
        wait_tile_sends(0)
        wait_tile_sends(1)

    @pl.when(sec == 1)
    def _():
        src_copy = pltpu.make_async_remote_copy(
            src_ref=src_ref.at[0, 0], dst_ref=srcbuf, send_sem=ssrc, recv_sem=rsrc,
            device_id=(0, lat, col), device_id_type=MESH_ID,
        )
        src_copy.start()
        share_tiles(0)
        share_tiles(1)
        transpose_in(srct.at[1], src_ref.at[1, 0])
        wait_tiles(0)
        wait_tiles(1)

        def fin2(h, r):
            vt[0, :, part(h)] = r
            put_field(3, 1, True, h, srct[1, :, part(h)].astype(jnp.float32) + coupling * r)

        run_app(2, 0, False, fin2)

        def fin3(h, r):
            outt[1, :, part(h)] = r
            put_field(4, 1, True, h, r)

        run_app(3, 1, True, fin3)

        def fin4(h, r):
            sol = vt[0, :, part(h)] + coupling * r
            outt[0, :, part(h)] = sol
            put_field(5, 0, False, h, sol)

        run_app(4, 0, True, fin4)
        wait_row_sends(3, 1, True)
        wait_row_sends(4, 1, True)
        wait_row_sends(5, 0, False)
        wait_tile_sends(0)
        wait_tile_sends(1)
        src_copy.wait_send()

    for s in range(2):
        for ri in range(2):
            out_ref[s, 0, ri] = outt[s, ri].T


def shards(sources, inverse_tiles, pattern, phase_index):
    nlat = lax.axis_size("lat")
    ncol = lax.axis_size("col")
    koff = inverse_tiles.shape[2]
    reach = OFF // 2
    noff = koff * ncol
    blk, nrhs = sources.shape[3], sources.shape[4]
    angle = 2.0 * jnp.pi * phase_index[0].astype(jnp.float32) / PHASES
    trig = jnp.stack([jnp.cos(angle), jnp.sin(angle)])
    kernel = functools.partial(sweep_kernel, nlat, ncol, koff, reach, CHUNKS)
    vmem = pl.BlockSpec(memory_space=pltpu.VMEM)
    smem = pl.BlockSpec(memory_space=pltpu.SMEM)
    slabs = inverse_tiles.shape[0]
    return pl.pallas_call(
        kernel,
        out_shape=jax.ShapeDtypeStruct(sources.shape, jnp.float32),
        in_specs=[smem, smem, pl.BlockSpec(memory_space=pl.ANY), pl.BlockSpec(memory_space=pl.ANY)],
        out_specs=vmem,
        scratch_shapes=[
            pltpu.VMEM(sources.shape, jnp.bfloat16),
            pltpu.VMEM(inverse_tiles.shape, jnp.bfloat16),
            pltpu.VMEM(inverse_tiles.shape, jnp.bfloat16),
            pltpu.VMEM((slabs, noff, 2, blk, blk), jnp.bfloat16),
            pltpu.VMEM((APPS, noff, 2, nrhs, blk), jnp.bfloat16),
            pltpu.VMEM((APPS, 2, nrhs, blk), jnp.bfloat16),
            pltpu.VMEM((slabs, 2, nrhs, blk), jnp.bfloat16),
            pltpu.VMEM((slabs, 2, nrhs, blk), jnp.float32),
            pltpu.VMEM((slabs, 2, nrhs, blk), jnp.float32),
            pltpu.VMEM((2, blk, nrhs), jnp.bfloat16),
            pltpu.SemaphoreType.DMA((APPS, noff, CHUNKS)),
            pltpu.SemaphoreType.DMA((APPS, noff, CHUNKS)),
            pltpu.SemaphoreType.DMA((slabs, ncol)),
            pltpu.SemaphoreType.DMA((slabs, ncol)),
            pltpu.SemaphoreType.DMA(()),
            pltpu.SemaphoreType.DMA(()),
            pltpu.SemaphoreType.DMA((1 + slabs,)),
        ],
        compiler_params=pltpu.CompilerParams(
            has_side_effects=True, collective_id=0, vmem_limit_bytes=67043328
        ),
    )(trig, pattern, sources, inverse_tiles)


def solution(mesh):
    placed = (
        P("sec", ("lat", "col"), None, None, None),
        P("sec", "lat", "col", None, None, None),
        P("sec", "lat", "col"),
        P(),
    )
    return jax.shard_map(
        shards,
        mesh=mesh,
        in_specs=placed,
        out_specs=P("sec", ("lat", "col"), None, None, None),
        check_vma=False,
    )
```

```python
import functools

import jax
import jax.numpy as jnp
from jax import lax
from jax.experimental import pallas as pl
from jax.experimental.pallas import tpu as pltpu
from jax.sharding import PartitionSpec as P

OFF = 8
PHASES = 16
APPS = 7
CHUNKS = 2

coupling = 0.8

MESH_ID = pl.DeviceIdType.MESH


def sweep_kernel(
    nlat, ncol, koff, reach, chunks,
    trig_ref, pat_ref, src_hbm, tiles_hbm, out_ref,
    src_ref, tiles_ref, mtiles, tiles2, wbuf, xbuf, fbuf, srct, vt, outt, srcbuf,
    rs1, ss1, rst, sst, rsrc, ssrc, lsem,
):
    sec = lax.axis_index("sec")
    lat = lax.axis_index("lat")
    col = lax.axis_index("col")
    cos_v = trig_ref[0]
    sin_v = trig_ref[1]
    noff = koff * ncol
    shifts = [d for d in range(reach - noff + 1, reach + 1)]
    width = xbuf.shape[3] // chunks

    loads = [pltpu.make_async_copy(src_hbm, src_ref, lsem.at[0])]
    for slab in range(tiles_ref.shape[0]):
        loads.append(pltpu.make_async_copy(tiles_hbm.at[slab], tiles_ref.at[slab], lsem.at[1 + slab]))
    for load in loads:
        load.start()

    barrier = pltpu.get_barrier_semaphore()
    partners = 0
    for ds in range(2):
        for d in range(-reach, reach + 1):
            if ds == 0 and d == 0:
                continue
            q = col + d
            pl.semaphore_signal(
                barrier, 1,
                device_id=((sec + ds) % 2, (lat + q // ncol + nlat) % nlat, (q + ncol) % ncol),
                device_id_type=MESH_ID,
            )
            partners += 1
    pl.semaphore_wait(barrier, partners)
    loads[0].wait()

    def tile_copy(slab, c0v, r):
        return pltpu.make_async_remote_copy(
            src_ref=mtiles.at[slab, r],
            dst_ref=tiles2.at[slab, pl.ds(c0v * koff, koff)],
            send_sem=sst.at[slab, r],
            recv_sem=rst.at[slab, c0v],
            device_id=(sec, lat, r),
            device_id_type=MESH_ID,
        )

    def share_tiles(slab):
        loads[1 + slab].wait()
        for r in range(ncol):
            for j in range(koff):
                keep = pat_ref[slab, r, j] != 0
                tile = tiles_ref[slab, r, j]
                mtiles[slab, r, j] = jnp.where(keep, tile, jnp.zeros_like(tile))
        for c0v in range(ncol):
            @pl.when(col == c0v)
            def _():
                for r in range(ncol):
                    if r != c0v:
                        tile_copy(slab, c0v, r).start()
                tiles2[slab, pl.ds(c0v * koff, koff)] = mtiles[slab, c0v]

    def wait_tiles(slab):
        for c in range(ncol):
            @pl.when(col != c)
            def _():
                tile_copy(slab, c, c).wait_recv()
        blk = tiles2.shape[3]
        for k in range(noff):
            tr_t = tiles2[slab, k, 0].T
            ti_t = tiles2[slab, k, 1].T
            wbuf[slab, k, :blk, :blk] = tr_t
            wbuf[slab, k, :blk, blk:] = ti_t
            wbuf[slab, k, blk:, :blk] = (-ti_t.astype(jnp.float32)).astype(jnp.bfloat16)
            wbuf[slab, k, blk:, blk:] = tr_t

    def wait_tile_sends(slab):
        for c0v in range(ncol):
            @pl.when(col == c0v)
            def _():
                for r in range(ncol):
                    if r != c0v:
                        tile_copy(slab, c0v, r).wait_send()

    def part(h):
        return pl.ds(h * width, width)

    def row_copy(n, to_sec, c0v, d, h):
        q = c0v + d
        return pltpu.make_async_remote_copy(
            src_ref=fbuf.at[n, :, part(h)],
            dst_ref=xbuf.at[n, reach - d, :, part(h)],
            send_sem=ss1.at[n, reach - d, h],
            recv_sem=rs1.at[n, reach - d, h],
            device_id=(to_sec, (lat + q // ncol + nlat) % nlat, q % ncol),
            device_id_type=MESH_ID,
        )

    def far_first(c0v):
        def hops(d):
            q = c0v + d
            gap = abs(q % ncol - c0v)
            return min(gap, ncol - gap) + (q // ncol != 0)
        return sorted(shifts, key=lambda d: (-hops(d), d))

    def send_rows(n, to_sec, local, h):
        for c0v in range(ncol):
            @pl.when(col == c0v)
            def _():
                for d in far_first(c0v):
                    if local and d == 0:
                        continue
                    row_copy(n, to_sec, c0v, d, h).start()

    def wait_row_sends(n, to_sec, local):
        for c0v in range(ncol):
            @pl.when(col == c0v)
            def _():
                for h in range(chunks):
                    for d in shifts:
                        if local and d == 0:
                            continue
                        row_copy(n, to_sec, c0v, d, h).wait_send()

    def put_field(n, to_sec, local, h, value):
        fbuf[n, :, part(h)] = value.astype(jnp.bfloat16)
        send_rows(n, to_sec, local, h)

    def run_app(n, slab, local, finish):
        order = sorted(range(noff), key=lambda k: (abs(k - reach), k))
        dot = functools.partial(jnp.dot, preferred_element_type=jnp.float32)
        for h in range(chunks):
            acc_r = None
            for k in order:
                d = k - reach
                if not (local and d == 0):
                    row_copy(n, sec, 0, -d, h).wait_recv()
                lo = (lat == 0) & (k < reach - col)
                hi = (lat == nlat - 1) & (k >= reach - col + ncol)

                @pl.when((lo | hi) & (not (local and d == 0)))
                def _():
                    sn = jnp.where(lo, -sin_v, sin_v)
                    x = xbuf[n, k, :, part(h)].astype(jnp.float32)
                    xbuf[n, k, 0, part(h)] = (x[0] * cos_v - x[1] * sn).astype(jnp.bfloat16)
                    xbuf[n, k, 1, part(h)] = (x[0] * sn + x[1] * cos_v).astype(jnp.bfloat16)

                if local and d == 0:
                    xr = fbuf[n, 0, part(h)]
                    xi = fbuf[n, 1, part(h)]
                else:
                    xr = xbuf[n, k, 0, part(h)]
                    xi = xbuf[n, k, 1, part(h)]
                both = dot(jnp.concatenate([xr, xi], axis=1), wbuf[slab, k])
                acc_r = both if acc_r is None else acc_r + both
            blk = xbuf.shape[4]
            finish(h, jnp.stack([acc_r[:, :blk], acc_r[:, blk:]], 0))

    def transpose_in(dst, src):
        for ri in range(2):
            dst[ri] = src[ri].astype(jnp.float32).T.astype(jnp.bfloat16)

    @pl.when(sec == 0)
    def _():
        share_tiles(0)
        for ri in range(2):
            fbuf[0, ri] = src_ref[0, 0, ri].astype(jnp.float32).T.astype(jnp.bfloat16)
        for h in range(chunks):
            send_rows(0, 0, True, h)
        transpose_in(srct.at[1], src_ref.at[1, 0])
        share_tiles(1)
        wait_tiles(0)

        def fin0(h, r):
            vt[0, :, part(h)] = r
            put_field(1, 0, True, h, srct[1, :, part(h)].astype(jnp.float32) + coupling * r)

        run_app(0, 0, True, fin0)
        wait_tiles(1)
        src_copy = pltpu.make_async_remote_copy(
            src_ref=src_ref.at[0, 0], dst_ref=srcbuf, send_sem=ssrc, recv_sem=rsrc,
            device_id=(1, lat, col), device_id_type=MESH_ID,
        )

        def fin1(h, r):
            vt[1, :, part(h)] = r
            if h == 0:
                src_copy.wait_recv()
                transpose_in(srct.at[0], srcbuf)
            put_field(2, 1, False, h, srct[0, :, part(h)].astype(jnp.float32) + coupling * r)

        run_app(1, 1, True, fin1)

        def fin5(h, r):
            sol = vt[1, :, part(h)] + coupling * r
            outt[1, :, part(h)] = sol
            put_field(6, 0, True, h, sol)

        run_app(5, 1, False, fin5)

        def fin6(h, r):
            outt[0, :, part(h)] = vt[0, :, part(h)] + coupling * r

        run_app(6, 0, True, fin6)
        wait_row_sends(0, 0, True)
        wait_row_sends(1, 0, True)
        wait_row_sends(2, 1, False)
        wait_row_sends(6, 0, True)
        wait_tile_sends(0)
        wait_tile_sends(1)

    @pl.when(sec == 1)
    def _():
        src_copy = pltpu.make_async_remote_copy(
            src_ref=src_ref.at[0, 0], dst_ref=srcbuf, send_sem=ssrc, recv_sem=rsrc,
            device_id=(0, lat, col), device_id_type=MESH_ID,
        )
        src_copy.start()
        share_tiles(0)
        share_tiles(1)
        transpose_in(srct.at[1], src_ref.at[1, 0])
        wait_tiles(0)
        wait_tiles(1)

        def fin2(h, r):
            vt[0, :, part(h)] = r
            put_field(3, 1, True, h, srct[1, :, part(h)].astype(jnp.float32) + coupling * r)

        run_app(2, 0, False, fin2)

        def fin3(h, r):
            outt[1, :, part(h)] = r
            put_field(4, 1, True, h, r)

        run_app(3, 1, True, fin3)

        def fin4(h, r):
            sol = vt[0, :, part(h)] + coupling * r
            outt[0, :, part(h)] = sol
            put_field(5, 0, False, h, sol)

        run_app(4, 0, True, fin4)
        wait_row_sends(3, 1, True)
        wait_row_sends(4, 1, True)
        wait_row_sends(5, 0, False)
        wait_tile_sends(0)
        wait_tile_sends(1)
        src_copy.wait_send()

    for s in range(2):
        for ri in range(2):
            out_ref[s, 0, ri] = outt[s, ri].T


def shards(sources, inverse_tiles, pattern, phase_index):
    nlat = lax.axis_size("lat")
    ncol = lax.axis_size("col")
    koff = inverse_tiles.shape[2]
    reach = OFF // 2
    noff = koff * ncol
    blk, nrhs = sources.shape[3], sources.shape[4]
    angle = 2.0 * jnp.pi * phase_index[0].astype(jnp.float32) / PHASES
    trig = jnp.stack([jnp.cos(angle), jnp.sin(angle)])
    kernel = functools.partial(sweep_kernel, nlat, ncol, koff, reach, CHUNKS)
    vmem = pl.BlockSpec(memory_space=pltpu.VMEM)
    smem = pl.BlockSpec(memory_space=pltpu.SMEM)
    slabs = inverse_tiles.shape[0]
    return pl.pallas_call(
        kernel,
        out_shape=jax.ShapeDtypeStruct(sources.shape, jnp.float32),
        in_specs=[smem, smem, pl.BlockSpec(memory_space=pl.ANY), pl.BlockSpec(memory_space=pl.ANY)],
        out_specs=vmem,
        scratch_shapes=[
            pltpu.VMEM(sources.shape, jnp.bfloat16),
            pltpu.VMEM(inverse_tiles.shape, jnp.bfloat16),
            pltpu.VMEM(inverse_tiles.shape, jnp.bfloat16),
            pltpu.VMEM((slabs, noff, 2, blk, blk), jnp.bfloat16),
            pltpu.VMEM((slabs, noff, 2 * blk, 2 * blk), jnp.bfloat16),
            pltpu.VMEM((APPS, noff, 2, nrhs, blk), jnp.bfloat16),
            pltpu.VMEM((APPS, 2, nrhs, blk), jnp.bfloat16),
            pltpu.VMEM((slabs, 2, nrhs, blk), jnp.bfloat16),
            pltpu.VMEM((slabs, 2, nrhs, blk), jnp.float32),
            pltpu.VMEM((slabs, 2, nrhs, blk), jnp.float32),
            pltpu.VMEM((2, blk, nrhs), jnp.bfloat16),
            pltpu.SemaphoreType.DMA((APPS, noff, CHUNKS)),
            pltpu.SemaphoreType.DMA((APPS, noff, CHUNKS)),
            pltpu.SemaphoreType.DMA((slabs, ncol)),
            pltpu.SemaphoreType.DMA((slabs, ncol)),
            pltpu.SemaphoreType.DMA(()),
            pltpu.SemaphoreType.DMA(()),
            pltpu.SemaphoreType.DMA((1 + slabs,)),
        ],
        compiler_params=pltpu.CompilerParams(
            has_side_effects=True, collective_id=0, vmem_limit_bytes=67043328
        ),
    )(trig, pattern, sources, inverse_tiles)


def solution(mesh):
    placed = (
        P("sec", ("lat", "col"), None, None, None),
        P("sec", "lat", "col", None, None, None),
        P("sec", "lat", "col"),
        P(),
    )
    return jax.shard_map(
        shards,
        mesh=mesh,
        in_specs=placed,
        out_specs=P("sec", ("lat", "col"), None, None, None),
        check_vma=False,
    )
```

```python
import functools

import jax
import jax.numpy as jnp
from jax import lax
from jax.experimental import pallas as pl
from jax.experimental.pallas import tpu as pltpu
from jax.sharding import PartitionSpec as P

OFF = 8
PHASES = 16
APPS = 7
CHUNKS = 1

coupling = 0.8

MESH_ID = pl.DeviceIdType.MESH


def sweep_kernel(
    nlat, ncol, koff, reach, chunks,
    trig_ref, pat_ref, src_hbm, tiles_hbm, out_ref,
    src_ref, tiles_ref, mtiles, tiles2, wbuf, xbuf, fbuf, srct, vt, outt, srcbuf,
    rs1, ss1, rst, sst, rsrc, ssrc, lsem,
):
    sec = lax.axis_index("sec")
    lat = lax.axis_index("lat")
    col = lax.axis_index("col")
    cos_v = trig_ref[0]
    sin_v = trig_ref[1]
    noff = koff * ncol
    shifts = [d for d in range(reach - noff + 1, reach + 1)]
    width = xbuf.shape[3] // chunks

    loads = [pltpu.make_async_copy(src_hbm, src_ref, lsem.at[0])]
    for slab in range(tiles_ref.shape[0]):
        loads.append(pltpu.make_async_copy(tiles_hbm.at[slab], tiles_ref.at[slab], lsem.at[1 + slab]))
    for load in loads:
        load.start()

    barrier = pltpu.get_barrier_semaphore()
    partners = 0
    for ds in range(2):
        for d in range(-reach, reach + 1):
            if ds == 0 and d == 0:
                continue
            q = col + d
            pl.semaphore_signal(
                barrier, 1,
                device_id=((sec + ds) % 2, (lat + q // ncol + nlat) % nlat, (q + ncol) % ncol),
                device_id_type=MESH_ID,
            )
            partners += 1
    pl.semaphore_wait(barrier, partners)
    loads[0].wait()

    def tile_copy(slab, c0v, r):
        return pltpu.make_async_remote_copy(
            src_ref=mtiles.at[slab, r],
            dst_ref=tiles2.at[slab, pl.ds(c0v * koff, koff)],
            send_sem=sst.at[slab, r],
            recv_sem=rst.at[slab, c0v],
            device_id=(sec, lat, r),
            device_id_type=MESH_ID,
        )

    def share_tiles(slab):
        loads[1 + slab].wait()
        for r in range(ncol):
            for j in range(koff):
                keep = pat_ref[slab, r, j] != 0
                tile = tiles_ref[slab, r, j]
                mtiles[slab, r, j] = jnp.where(keep, tile, jnp.zeros_like(tile))
        for c0v in range(ncol):
            @pl.when(col == c0v)
            def _():
                for r in range(ncol):
                    if r != c0v:
                        tile_copy(slab, c0v, r).start()
                tiles2[slab, pl.ds(c0v * koff, koff)] = mtiles[slab, c0v]

    def wait_tiles(slab):
        for c in range(ncol):
            @pl.when(col != c)
            def _():
                tile_copy(slab, c, c).wait_recv()
        blk = tiles2.shape[3]
        for k in range(noff):
            tr_t = tiles2[slab, k, 0].T
            ti_t = tiles2[slab, k, 1].T
            wbuf[slab, k, :blk, :blk] = tr_t
            wbuf[slab, k, :blk, blk:] = ti_t
            wbuf[slab, k, blk:, :blk] = (-ti_t.astype(jnp.float32)).astype(jnp.bfloat16)
            wbuf[slab, k, blk:, blk:] = tr_t

    def wait_tile_sends(slab):
        for c0v in range(ncol):
            @pl.when(col == c0v)
            def _():
                for r in range(ncol):
                    if r != c0v:
                        tile_copy(slab, c0v, r).wait_send()

    def part(h):
        return pl.ds(h * width, width)

    def row_copy(n, to_sec, c0v, d, h):
        q = c0v + d
        return pltpu.make_async_remote_copy(
            src_ref=fbuf.at[n, :, part(h)],
            dst_ref=xbuf.at[n, reach - d, :, part(h)],
            send_sem=ss1.at[n, reach - d, h],
            recv_sem=rs1.at[n, reach - d, h],
            device_id=(to_sec, (lat + q // ncol + nlat) % nlat, q % ncol),
            device_id_type=MESH_ID,
        )

    def far_first(c0v):
        def hops(d):
            q = c0v + d
            gap = abs(q % ncol - c0v)
            return min(gap, ncol - gap) + (q // ncol != 0)
        return sorted(shifts, key=lambda d: (-hops(d), d))

    def send_rows(n, to_sec, local, h):
        for c0v in range(ncol):
            @pl.when(col == c0v)
            def _():
                for d in far_first(c0v):
                    if local and d == 0:
                        continue
                    row_copy(n, to_sec, c0v, d, h).start()

    def wait_row_sends(n, to_sec, local):
        for c0v in range(ncol):
            @pl.when(col == c0v)
            def _():
                for h in range(chunks):
                    for d in shifts:
                        if local and d == 0:
                            continue
                        row_copy(n, to_sec, c0v, d, h).wait_send()

    def put_field(n, to_sec, local, h, value):
        fbuf[n, :, part(h)] = value.astype(jnp.bfloat16)
        send_rows(n, to_sec, local, h)

    def run_app(n, slab, local, finish):
        order = sorted(range(noff), key=lambda k: (abs(k - reach), k))
        dot = functools.partial(jnp.dot, preferred_element_type=jnp.float32)
        for h in range(chunks):
            acc_r = None
            for k in order:
                d = k - reach
                if not (local and d == 0):
                    row_copy(n, sec, 0, -d, h).wait_recv()
                lo = (lat == 0) & (k < reach - col)
                hi = (lat == nlat - 1) & (k >= reach - col + ncol)

                @pl.when((lo | hi) & (not (local and d == 0)))
                def _():
                    sn = jnp.where(lo, -sin_v, sin_v)
                    x = xbuf[n, k, :, part(h)].astype(jnp.float32)
                    xbuf[n, k, 0, part(h)] = (x[0] * cos_v - x[1] * sn).astype(jnp.bfloat16)
                    xbuf[n, k, 1, part(h)] = (x[0] * sn + x[1] * cos_v).astype(jnp.bfloat16)

                if local and d == 0:
                    xr = fbuf[n, 0, part(h)]
                    xi = fbuf[n, 1, part(h)]
                else:
                    xr = xbuf[n, k, 0, part(h)]
                    xi = xbuf[n, k, 1, part(h)]
                both = dot(jnp.concatenate([xr, xi], axis=1), wbuf[slab, k])
                acc_r = both if acc_r is None else acc_r + both
            blk = xbuf.shape[4]
            finish(h, jnp.stack([acc_r[:, :blk], acc_r[:, blk:]], 0))

    def transpose_in(dst, src):
        for ri in range(2):
            dst[ri] = src[ri].astype(jnp.float32).T.astype(jnp.bfloat16)

    @pl.when(sec == 0)
    def _():
        share_tiles(0)
        for ri in range(2):
            fbuf[0, ri] = src_ref[0, 0, ri].astype(jnp.float32).T.astype(jnp.bfloat16)
        for h in range(chunks):
            send_rows(0, 0, True, h)
        transpose_in(srct.at[1], src_ref.at[1, 0])
        share_tiles(1)
        wait_tiles(0)

        def fin0(h, r):
            vt[0, :, part(h)] = r
            put_field(1, 0, True, h, srct[1, :, part(h)].astype(jnp.float32) + coupling * r)

        run_app(0, 0, True, fin0)
        wait_tiles(1)
        src_copy = pltpu.make_async_remote_copy(
            src_ref=src_ref.at[0, 0], dst_ref=srcbuf, send_sem=ssrc, recv_sem=rsrc,
            device_id=(1, lat, col), device_id_type=MESH_ID,
        )

        def fin1(h, r):
            vt[1, :, part(h)] = r
            if h == 0:
                src_copy.wait_recv()
                transpose_in(srct.at[0], srcbuf)
            put_field(2, 1, False, h, srct[0, :, part(h)].astype(jnp.float32) + coupling * r)

        run_app(1, 1, True, fin1)

        def fin5(h, r):
            sol = vt[1, :, part(h)] + coupling * r
            outt[1, :, part(h)] = sol
            put_field(6, 0, True, h, sol)

        run_app(5, 1, False, fin5)

        def fin6(h, r):
            outt[0, :, part(h)] = vt[0, :, part(h)] + coupling * r

        run_app(6, 0, True, fin6)
        wait_row_sends(0, 0, True)
        wait_row_sends(1, 0, True)
        wait_row_sends(2, 1, False)
        wait_row_sends(6, 0, True)
        wait_tile_sends(0)
        wait_tile_sends(1)

    @pl.when(sec == 1)
    def _():
        src_copy = pltpu.make_async_remote_copy(
            src_ref=src_ref.at[0, 0], dst_ref=srcbuf, send_sem=ssrc, recv_sem=rsrc,
            device_id=(0, lat, col), device_id_type=MESH_ID,
        )
        src_copy.start()
        share_tiles(0)
        share_tiles(1)
        transpose_in(srct.at[1], src_ref.at[1, 0])
        wait_tiles(0)
        wait_tiles(1)

        def fin2(h, r):
            vt[0, :, part(h)] = r
            put_field(3, 1, True, h, srct[1, :, part(h)].astype(jnp.float32) + coupling * r)

        run_app(2, 0, False, fin2)

        def fin3(h, r):
            outt[1, :, part(h)] = r
            put_field(4, 1, True, h, r)

        run_app(3, 1, True, fin3)

        def fin4(h, r):
            sol = vt[0, :, part(h)] + coupling * r
            outt[0, :, part(h)] = sol
            put_field(5, 0, False, h, sol)

        run_app(4, 0, True, fin4)
        wait_row_sends(3, 1, True)
        wait_row_sends(4, 1, True)
        wait_row_sends(5, 0, False)
        wait_tile_sends(0)
        wait_tile_sends(1)
        src_copy.wait_send()

    for s in range(2):
        for ri in range(2):
            out_ref[s, 0, ri] = outt[s, ri].T


def shards(sources, inverse_tiles, pattern, phase_index):
    nlat = lax.axis_size("lat")
    ncol = lax.axis_size("col")
    koff = inverse_tiles.shape[2]
    reach = OFF // 2
    noff = koff * ncol
    blk, nrhs = sources.shape[3], sources.shape[4]
    angle = 2.0 * jnp.pi * phase_index[0].astype(jnp.float32) / PHASES
    trig = jnp.stack([jnp.cos(angle), jnp.sin(angle)])
    kernel = functools.partial(sweep_kernel, nlat, ncol, koff, reach, CHUNKS)
    vmem = pl.BlockSpec(memory_space=pltpu.VMEM)
    smem = pl.BlockSpec(memory_space=pltpu.SMEM)
    slabs = inverse_tiles.shape[0]
    return pl.pallas_call(
        kernel,
        out_shape=jax.ShapeDtypeStruct(sources.shape, jnp.float32),
        in_specs=[smem, smem, pl.BlockSpec(memory_space=pl.ANY), pl.BlockSpec(memory_space=pl.ANY)],
        out_specs=vmem,
        scratch_shapes=[
            pltpu.VMEM(sources.shape, jnp.bfloat16),
            pltpu.VMEM(inverse_tiles.shape, jnp.bfloat16),
            pltpu.VMEM(inverse_tiles.shape, jnp.bfloat16),
            pltpu.VMEM((slabs, noff, 2, blk, blk), jnp.bfloat16),
            pltpu.VMEM((slabs, noff, 2 * blk, 2 * blk), jnp.bfloat16),
            pltpu.VMEM((APPS, noff, 2, nrhs, blk), jnp.bfloat16),
            pltpu.VMEM((APPS, 2, nrhs, blk), jnp.bfloat16),
            pltpu.VMEM((slabs, 2, nrhs, blk), jnp.bfloat16),
            pltpu.VMEM((slabs, 2, nrhs, blk), jnp.float32),
            pltpu.VMEM((slabs, 2, nrhs, blk), jnp.float32),
            pltpu.VMEM((2, blk, nrhs), jnp.bfloat16),
            pltpu.SemaphoreType.DMA((APPS, noff, CHUNKS)),
            pltpu.SemaphoreType.DMA((APPS, noff, CHUNKS)),
            pltpu.SemaphoreType.DMA((slabs, ncol)),
            pltpu.SemaphoreType.DMA((slabs, ncol)),
            pltpu.SemaphoreType.DMA(()),
            pltpu.SemaphoreType.DMA(()),
            pltpu.SemaphoreType.DMA((1 + slabs,)),
        ],
        compiler_params=pltpu.CompilerParams(
            has_side_effects=True, collective_id=0, vmem_limit_bytes=67043328
        ),
    )(trig, pattern, sources, inverse_tiles)


def solution(mesh):
    placed = (
        P("sec", ("lat", "col"), None, None, None),
        P("sec", "lat", "col", None, None, None),
        P("sec", "lat", "col"),
        P(),
    )
    return jax.shard_map(
        shards,
        mesh=mesh,
        in_specs=placed,
        out_specs=P("sec", ("lat", "col"), None, None, None),
        check_vma=False,
    )
```

```python
import functools

import jax
import jax.numpy as jnp
from jax import lax
from jax.experimental import pallas as pl
from jax.experimental.pallas import tpu as pltpu
from jax.sharding import PartitionSpec as P

OFF = 8
PHASES = 16
APPS = 7
CHUNKS = 4

coupling = 0.8

MESH_ID = pl.DeviceIdType.MESH


def sweep_kernel(
    nlat, ncol, koff, reach, chunks,
    trig_ref, pat_ref, src_hbm, tiles_hbm, out_ref,
    src_ref, tiles_ref, mtiles, tiles2, wbuf, xbuf, fbuf, srct, vt, outt, srcbuf,
    rs1, ss1, rst, sst, rsrc, ssrc, lsem,
):
    sec = lax.axis_index("sec")
    lat = lax.axis_index("lat")
    col = lax.axis_index("col")
    cos_v = trig_ref[0]
    sin_v = trig_ref[1]
    noff = koff * ncol
    shifts = [d for d in range(reach - noff + 1, reach + 1)]
    width = xbuf.shape[3] // chunks

    loads = [pltpu.make_async_copy(src_hbm, src_ref, lsem.at[0])]
    for slab in range(tiles_ref.shape[0]):
        loads.append(pltpu.make_async_copy(tiles_hbm.at[slab], tiles_ref.at[slab], lsem.at[1 + slab]))
    for load in loads:
        load.start()

    barrier = pltpu.get_barrier_semaphore()
    partners = 0
    for ds in range(2):
        for d in range(-reach, reach + 1):
            if ds == 0 and d == 0:
                continue
            q = col + d
            pl.semaphore_signal(
                barrier, 1,
                device_id=((sec + ds) % 2, (lat + q // ncol + nlat) % nlat, (q + ncol) % ncol),
                device_id_type=MESH_ID,
            )
            partners += 1
    pl.semaphore_wait(barrier, partners)
    loads[0].wait()

    def tile_copy(slab, c0v, r):
        return pltpu.make_async_remote_copy(
            src_ref=mtiles.at[slab, r],
            dst_ref=tiles2.at[slab, pl.ds(c0v * koff, koff)],
            send_sem=sst.at[slab, r],
            recv_sem=rst.at[slab, c0v],
            device_id=(sec, lat, r),
            device_id_type=MESH_ID,
        )

    def share_tiles(slab):
        loads[1 + slab].wait()
        for r in range(ncol):
            for j in range(koff):
                keep = pat_ref[slab, r, j] != 0
                tile = tiles_ref[slab, r, j]
                mtiles[slab, r, j] = jnp.where(keep, tile, jnp.zeros_like(tile))
        for c0v in range(ncol):
            @pl.when(col == c0v)
            def _():
                for r in range(ncol):
                    if r != c0v:
                        tile_copy(slab, c0v, r).start()
                tiles2[slab, pl.ds(c0v * koff, koff)] = mtiles[slab, c0v]

    def wait_tiles(slab):
        for c in range(ncol):
            @pl.when(col != c)
            def _():
                tile_copy(slab, c, c).wait_recv()
        blk = tiles2.shape[3]
        for k in range(noff):
            tr_t = tiles2[slab, k, 0].T
            ti_t = tiles2[slab, k, 1].T
            wbuf[slab, k, :blk, :blk] = tr_t
            wbuf[slab, k, :blk, blk:] = ti_t
            wbuf[slab, k, blk:, :blk] = (-ti_t.astype(jnp.float32)).astype(jnp.bfloat16)
            wbuf[slab, k, blk:, blk:] = tr_t

    def wait_tile_sends(slab):
        for c0v in range(ncol):
            @pl.when(col == c0v)
            def _():
                for r in range(ncol):
                    if r != c0v:
                        tile_copy(slab, c0v, r).wait_send()

    def part(h):
        return pl.ds(h * width, width)

    def row_copy(n, to_sec, c0v, d, h):
        q = c0v + d
        return pltpu.make_async_remote_copy(
            src_ref=fbuf.at[n, :, part(h)],
            dst_ref=xbuf.at[n, reach - d, :, part(h)],
            send_sem=ss1.at[n, reach - d, h],
            recv_sem=rs1.at[n, reach - d, h],
            device_id=(to_sec, (lat + q // ncol + nlat) % nlat, q % ncol),
            device_id_type=MESH_ID,
        )

    def far_first(c0v):
        def hops(d):
            q = c0v + d
            gap = abs(q % ncol - c0v)
            return min(gap, ncol - gap) + (q // ncol != 0)
        return sorted(shifts, key=lambda d: (-hops(d), d))

    def send_rows(n, to_sec, local, h):
        for c0v in range(ncol):
            @pl.when(col == c0v)
            def _():
                for d in far_first(c0v):
                    if local and d == 0:
                        continue
                    row_copy(n, to_sec, c0v, d, h).start()

    def wait_row_sends(n, to_sec, local):
        for c0v in range(ncol):
            @pl.when(col == c0v)
            def _():
                for h in range(chunks):
                    for d in shifts:
                        if local and d == 0:
                            continue
                        row_copy(n, to_sec, c0v, d, h).wait_send()

    def put_field(n, to_sec, local, h, value):
        fbuf[n, :, part(h)] = value.astype(jnp.bfloat16)
        send_rows(n, to_sec, local, h)

    def run_app(n, slab, local, finish):
        order = sorted(range(noff), key=lambda k: (abs(k - reach), k))
        dot = functools.partial(jnp.dot, preferred_element_type=jnp.float32)
        for h in range(chunks):
            acc_r = None
            for k in order:
                d = k - reach
                if not (local and d == 0):
                    row_copy(n, sec, 0, -d, h).wait_recv()
                lo = (lat == 0) & (k < reach - col)
                hi = (lat == nlat - 1) & (k >= reach - col + ncol)

                @pl.when((lo | hi) & (not (local and d == 0)))
                def _():
                    sn = jnp.where(lo, -sin_v, sin_v)
                    x = xbuf[n, k, :, part(h)].astype(jnp.float32)
                    xbuf[n, k, 0, part(h)] = (x[0] * cos_v - x[1] * sn).astype(jnp.bfloat16)
                    xbuf[n, k, 1, part(h)] = (x[0] * sn + x[1] * cos_v).astype(jnp.bfloat16)

                if local and d == 0:
                    xr = fbuf[n, 0, part(h)]
                    xi = fbuf[n, 1, part(h)]
                else:
                    xr = xbuf[n, k, 0, part(h)]
                    xi = xbuf[n, k, 1, part(h)]
                both = dot(jnp.concatenate([xr, xi], axis=1), wbuf[slab, k])
                acc_r = both if acc_r is None else acc_r + both
            blk = xbuf.shape[4]
            finish(h, jnp.stack([acc_r[:, :blk], acc_r[:, blk:]], 0))

    def transpose_in(dst, src):
        for ri in range(2):
            dst[ri] = src[ri].astype(jnp.float32).T.astype(jnp.bfloat16)

    @pl.when(sec == 0)
    def _():
        share_tiles(0)
        for ri in range(2):
            fbuf[0, ri] = src_ref[0, 0, ri].astype(jnp.float32).T.astype(jnp.bfloat16)
        for h in range(chunks):
            send_rows(0, 0, True, h)
        transpose_in(srct.at[1], src_ref.at[1, 0])
        share_tiles(1)
        wait_tiles(0)

        def fin0(h, r):
            vt[0, :, part(h)] = r
            put_field(1, 0, True, h, srct[1, :, part(h)].astype(jnp.float32) + coupling * r)

        run_app(0, 0, True, fin0)
        wait_tiles(1)
        src_copy = pltpu.make_async_remote_copy(
            src_ref=src_ref.at[0, 0], dst_ref=srcbuf, send_sem=ssrc, recv_sem=rsrc,
            device_id=(1, lat, col), device_id_type=MESH_ID,
        )

        def fin1(h, r):
            vt[1, :, part(h)] = r
            if h == 0:
                src_copy.wait_recv()
                transpose_in(srct.at[0], srcbuf)
            put_field(2, 1, False, h, srct[0, :, part(h)].astype(jnp.float32) + coupling * r)

        run_app(1, 1, True, fin1)

        def fin5(h, r):
            sol = vt[1, :, part(h)] + coupling * r
            outt[1, :, part(h)] = sol
            put_field(6, 0, True, h, sol)

        run_app(5, 1, False, fin5)

        def fin6(h, r):
            outt[0, :, part(h)] = vt[0, :, part(h)] + coupling * r

        run_app(6, 0, True, fin6)
        wait_row_sends(0, 0, True)
        wait_row_sends(1, 0, True)
        wait_row_sends(2, 1, False)
        wait_row_sends(6, 0, True)
        wait_tile_sends(0)
        wait_tile_sends(1)

    @pl.when(sec == 1)
    def _():
        src_copy = pltpu.make_async_remote_copy(
            src_ref=src_ref.at[0, 0], dst_ref=srcbuf, send_sem=ssrc, recv_sem=rsrc,
            device_id=(0, lat, col), device_id_type=MESH_ID,
        )
        src_copy.start()
        share_tiles(0)
        share_tiles(1)
        transpose_in(srct.at[1], src_ref.at[1, 0])
        wait_tiles(0)
        wait_tiles(1)

        def fin2(h, r):
            vt[0, :, part(h)] = r
            put_field(3, 1, True, h, srct[1, :, part(h)].astype(jnp.float32) + coupling * r)

        run_app(2, 0, False, fin2)

        def fin3(h, r):
            outt[1, :, part(h)] = r
            put_field(4, 1, True, h, r)

        run_app(3, 1, True, fin3)

        def fin4(h, r):
            sol = vt[0, :, part(h)] + coupling * r
            outt[0, :, part(h)] = sol
            put_field(5, 0, False, h, sol)

        run_app(4, 0, True, fin4)
        wait_row_sends(3, 1, True)
        wait_row_sends(4, 1, True)
        wait_row_sends(5, 0, False)
        wait_tile_sends(0)
        wait_tile_sends(1)
        src_copy.wait_send()

    for s in range(2):
        for ri in range(2):
            out_ref[s, 0, ri] = outt[s, ri].T


def shards(sources, inverse_tiles, pattern, phase_index):
    nlat = lax.axis_size("lat")
    ncol = lax.axis_size("col")
    koff = inverse_tiles.shape[2]
    reach = OFF // 2
    noff = koff * ncol
    blk, nrhs = sources.shape[3], sources.shape[4]
    angle = 2.0 * jnp.pi * phase_index[0].astype(jnp.float32) / PHASES
    trig = jnp.stack([jnp.cos(angle), jnp.sin(angle)])
    kernel = functools.partial(sweep_kernel, nlat, ncol, koff, reach, CHUNKS)
    vmem = pl.BlockSpec(memory_space=pltpu.VMEM)
    smem = pl.BlockSpec(memory_space=pltpu.SMEM)
    slabs = inverse_tiles.shape[0]
    return pl.pallas_call(
        kernel,
        out_shape=jax.ShapeDtypeStruct(sources.shape, jnp.float32),
        in_specs=[smem, smem, pl.BlockSpec(memory_space=pl.ANY), pl.BlockSpec(memory_space=pl.ANY)],
        out_specs=vmem,
        scratch_shapes=[
            pltpu.VMEM(sources.shape, jnp.bfloat16),
            pltpu.VMEM(inverse_tiles.shape, jnp.bfloat16),
            pltpu.VMEM(inverse_tiles.shape, jnp.bfloat16),
            pltpu.VMEM((slabs, noff, 2, blk, blk), jnp.bfloat16),
            pltpu.VMEM((slabs, noff, 2 * blk, 2 * blk), jnp.bfloat16),
            pltpu.VMEM((APPS, noff, 2, nrhs, blk), jnp.bfloat16),
            pltpu.VMEM((APPS, 2, nrhs, blk), jnp.bfloat16),
            pltpu.VMEM((slabs, 2, nrhs, blk), jnp.bfloat16),
            pltpu.VMEM((slabs, 2, nrhs, blk), jnp.float32),
            pltpu.VMEM((slabs, 2, nrhs, blk), jnp.float32),
            pltpu.VMEM((2, blk, nrhs), jnp.bfloat16),
            pltpu.SemaphoreType.DMA((APPS, noff, CHUNKS)),
            pltpu.SemaphoreType.DMA((APPS, noff, CHUNKS)),
            pltpu.SemaphoreType.DMA((slabs, ncol)),
            pltpu.SemaphoreType.DMA((slabs, ncol)),
            pltpu.SemaphoreType.DMA(()),
            pltpu.SemaphoreType.DMA(()),
            pltpu.SemaphoreType.DMA((1 + slabs,)),
        ],
        compiler_params=pltpu.CompilerParams(
            has_side_effects=True, collective_id=0, vmem_limit_bytes=67043328
        ),
    )(trig, pattern, sources, inverse_tiles)


def solution(mesh):
    placed = (
        P("sec", ("lat", "col"), None, None, None),
        P("sec", "lat", "col", None, None, None),
        P("sec", "lat", "col"),
        P(),
    )
    return jax.shard_map(
        shards,
        mesh=mesh,
        in_specs=placed,
        out_specs=P("sec", ("lat", "col"), None, None, None),
        check_vma=False,
    )
```

```python
import functools

import jax
import jax.numpy as jnp
from jax import lax
from jax.experimental import pallas as pl
from jax.experimental.pallas import tpu as pltpu
from jax.sharding import PartitionSpec as P

OFF = 8
PHASES = 16
APPS = 7
CHUNKS = 4

coupling = 0.8

MESH_ID = pl.DeviceIdType.MESH


def sweep_kernel(
    nlat, ncol, koff, reach, chunks,
    trig_ref, pat_ref, src_hbm, tiles_hbm, out_ref,
    src_ref, tiles_ref, mtiles, tiles2, wbuf, xbuf, fbuf, srct, vt, outt, srcbuf,
    rs1, ss1, rst, sst, rsrc, ssrc, lsem,
):
    sec = lax.axis_index("sec")
    lat = lax.axis_index("lat")
    col = lax.axis_index("col")
    cos_v = trig_ref[0]
    sin_v = trig_ref[1]
    noff = koff * ncol
    shifts = [d for d in range(reach - noff + 1, reach + 1)]
    width = xbuf.shape[3] // chunks

    loads = [pltpu.make_async_copy(src_hbm, src_ref, lsem.at[0])]
    for slab in range(tiles_ref.shape[0]):
        loads.append(pltpu.make_async_copy(tiles_hbm.at[slab], tiles_ref.at[slab], lsem.at[1 + slab]))
    for load in loads:
        load.start()

    barrier = pltpu.get_barrier_semaphore()
    partners = 0
    for ds in range(2):
        for d in range(-reach, reach + 1):
            if ds == 0 and d == 0:
                continue
            q = col + d
            pl.semaphore_signal(
                barrier, 1,
                device_id=((sec + ds) % 2, (lat + q // ncol + nlat) % nlat, (q + ncol) % ncol),
                device_id_type=MESH_ID,
            )
            partners += 1
    pl.semaphore_wait(barrier, partners)
    loads[0].wait()

    def tile_copy(slab, c0v, r):
        return pltpu.make_async_remote_copy(
            src_ref=mtiles.at[slab, r],
            dst_ref=tiles2.at[slab, pl.ds(c0v * koff, koff)],
            send_sem=sst.at[slab, r],
            recv_sem=rst.at[slab, c0v],
            device_id=(sec, lat, r),
            device_id_type=MESH_ID,
        )

    def mask_tiles(slab):
        loads[1 + slab].wait()
        for r in range(ncol):
            for j in range(koff):
                keep = pat_ref[slab, r, j] != 0
                tile = tiles_ref[slab, r, j]
                mtiles[slab, r, j] = jnp.where(keep, tile, jnp.zeros_like(tile))

    def share_tiles(slab, masked=False):
        if not masked:
            mask_tiles(slab)
        for c0v in range(ncol):
            @pl.when(col == c0v)
            def _():
                for r in range(ncol):
                    if r != c0v:
                        tile_copy(slab, c0v, r).start()
                tiles2[slab, pl.ds(c0v * koff, koff)] = mtiles[slab, c0v]

    def wait_tiles(slab):
        for c in range(ncol):
            @pl.when(col != c)
            def _():
                tile_copy(slab, c, c).wait_recv()
        blk = tiles2.shape[3]
        for k in range(noff):
            tr_t = tiles2[slab, k, 0].T
            ti_t = tiles2[slab, k, 1].T
            wbuf[slab, k, :blk, :blk] = tr_t
            wbuf[slab, k, :blk, blk:] = ti_t
            wbuf[slab, k, blk:, :blk] = (-ti_t.astype(jnp.float32)).astype(jnp.bfloat16)
            wbuf[slab, k, blk:, blk:] = tr_t

    def wait_tile_sends(slab):
        for c0v in range(ncol):
            @pl.when(col == c0v)
            def _():
                for r in range(ncol):
                    if r != c0v:
                        tile_copy(slab, c0v, r).wait_send()

    def part(h):
        return pl.ds(h * width, width)

    def row_copy(n, to_sec, c0v, d, h):
        q = c0v + d
        return pltpu.make_async_remote_copy(
            src_ref=fbuf.at[n, :, part(h)],
            dst_ref=xbuf.at[n, reach - d, :, part(h)],
            send_sem=ss1.at[n, reach - d, h],
            recv_sem=rs1.at[n, reach - d, h],
            device_id=(to_sec, (lat + q // ncol + nlat) % nlat, q % ncol),
            device_id_type=MESH_ID,
        )

    def far_first(c0v):
        def hops(d):
            q = c0v + d
            gap = abs(q % ncol - c0v)
            return min(gap, ncol - gap) + (q // ncol != 0)
        return sorted(shifts, key=lambda d: (-hops(d), d))

    def send_rows(n, to_sec, local, h):
        for c0v in range(ncol):
            @pl.when(col == c0v)
            def _():
                for d in far_first(c0v):
                    if local and d == 0:
                        continue
                    row_copy(n, to_sec, c0v, d, h).start()

    def wait_row_sends(n, to_sec, local):
        for c0v in range(ncol):
            @pl.when(col == c0v)
            def _():
                for h in range(chunks):
                    for d in shifts:
                        if local and d == 0:
                            continue
                        row_copy(n, to_sec, c0v, d, h).wait_send()

    def put_field(n, to_sec, local, h, value):
        fbuf[n, :, part(h)] = value.astype(jnp.bfloat16)
        send_rows(n, to_sec, local, h)

    def run_app(n, slab, local, finish):
        order = sorted(range(noff), key=lambda k: (abs(k - reach), k))
        dot = functools.partial(jnp.dot, preferred_element_type=jnp.float32)
        for h in range(chunks):
            acc_r = None
            for k in order:
                d = k - reach
                if not (local and d == 0):
                    row_copy(n, sec, 0, -d, h).wait_recv()
                lo = (lat == 0) & (k < reach - col)
                hi = (lat == nlat - 1) & (k >= reach - col + ncol)

                @pl.when((lo | hi) & (not (local and d == 0)))
                def _():
                    sn = jnp.where(lo, -sin_v, sin_v)
                    x = xbuf[n, k, :, part(h)].astype(jnp.float32)
                    xbuf[n, k, 0, part(h)] = (x[0] * cos_v - x[1] * sn).astype(jnp.bfloat16)
                    xbuf[n, k, 1, part(h)] = (x[0] * sn + x[1] * cos_v).astype(jnp.bfloat16)

                if local and d == 0:
                    xr = fbuf[n, 0, part(h)]
                    xi = fbuf[n, 1, part(h)]
                else:
                    xr = xbuf[n, k, 0, part(h)]
                    xi = xbuf[n, k, 1, part(h)]
                both = dot(jnp.concatenate([xr, xi], axis=1), wbuf[slab, k])
                acc_r = both if acc_r is None else acc_r + both
            blk = xbuf.shape[4]
            finish(h, jnp.stack([acc_r[:, :blk], acc_r[:, blk:]], 0))

    def transpose_in(dst, src):
        for ri in range(2):
            dst[ri] = src[ri].astype(jnp.float32).T.astype(jnp.bfloat16)

    @pl.when(sec == 0)
    def _():
        share_tiles(0)
        for ri in range(2):
            fbuf[0, ri] = src_ref[0, 0, ri].astype(jnp.float32).T.astype(jnp.bfloat16)
        for h in range(chunks):
            send_rows(0, 0, True, h)
        mask_tiles(1)
        transpose_in(srct.at[1], src_ref.at[1, 0])
        wait_tiles(0)
        share_tiles(1, masked=True)

        def fin0(h, r):
            vt[0, :, part(h)] = r
            put_field(1, 0, True, h, srct[1, :, part(h)].astype(jnp.float32) + coupling * r)

        run_app(0, 0, True, fin0)
        wait_tiles(1)
        src_copy = pltpu.make_async_remote_copy(
            src_ref=src_ref.at[0, 0], dst_ref=srcbuf, send_sem=ssrc, recv_sem=rsrc,
            device_id=(1, lat, col), device_id_type=MESH_ID,
        )

        def fin1(h, r):
            vt[1, :, part(h)] = r
            if h == 0:
                src_copy.wait_recv()
                transpose_in(srct.at[0], srcbuf)
            put_field(2, 1, False, h, srct[0, :, part(h)].astype(jnp.float32) + coupling * r)

        run_app(1, 1, True, fin1)

        def fin5(h, r):
            sol = vt[1, :, part(h)] + coupling * r
            outt[1, :, part(h)] = sol
            put_field(6, 0, True, h, sol)

        run_app(5, 1, False, fin5)

        def fin6(h, r):
            outt[0, :, part(h)] = vt[0, :, part(h)] + coupling * r

        run_app(6, 0, True, fin6)
        wait_row_sends(0, 0, True)
        wait_row_sends(1, 0, True)
        wait_row_sends(2, 1, False)
        wait_row_sends(6, 0, True)
        wait_tile_sends(0)
        wait_tile_sends(1)

    @pl.when(sec == 1)
    def _():
        src_copy = pltpu.make_async_remote_copy(
            src_ref=src_ref.at[0, 0], dst_ref=srcbuf, send_sem=ssrc, recv_sem=rsrc,
            device_id=(0, lat, col), device_id_type=MESH_ID,
        )
        src_copy.start()
        share_tiles(0)
        share_tiles(1)
        transpose_in(srct.at[1], src_ref.at[1, 0])
        wait_tiles(0)
        wait_tiles(1)

        def fin2(h, r):
            vt[0, :, part(h)] = r
            put_field(3, 1, True, h, srct[1, :, part(h)].astype(jnp.float32) + coupling * r)

        run_app(2, 0, False, fin2)

        def fin3(h, r):
            outt[1, :, part(h)] = r
            put_field(4, 1, True, h, r)

        run_app(3, 1, True, fin3)

        def fin4(h, r):
            sol = vt[0, :, part(h)] + coupling * r
            outt[0, :, part(h)] = sol
            put_field(5, 0, False, h, sol)

        run_app(4, 0, True, fin4)
        wait_row_sends(3, 1, True)
        wait_row_sends(4, 1, True)
        wait_row_sends(5, 0, False)
        wait_tile_sends(0)
        wait_tile_sends(1)
        src_copy.wait_send()

    for s in range(2):
        for ri in range(2):
            out_ref[s, 0, ri] = outt[s, ri].T


def shards(sources, inverse_tiles, pattern, phase_index):
    nlat = lax.axis_size("lat")
    ncol = lax.axis_size("col")
    koff = inverse_tiles.shape[2]
    reach = OFF // 2
    noff = koff * ncol
    blk, nrhs = sources.shape[3], sources.shape[4]
    angle = 2.0 * jnp.pi * phase_index[0].astype(jnp.float32) / PHASES
    trig = jnp.stack([jnp.cos(angle), jnp.sin(angle)])
    kernel = functools.partial(sweep_kernel, nlat, ncol, koff, reach, CHUNKS)
    vmem = pl.BlockSpec(memory_space=pltpu.VMEM)
    smem = pl.BlockSpec(memory_space=pltpu.SMEM)
    slabs = inverse_tiles.shape[0]
    return pl.pallas_call(
        kernel,
        out_shape=jax.ShapeDtypeStruct(sources.shape, jnp.float32),
        in_specs=[smem, smem, pl.BlockSpec(memory_space=pl.ANY), pl.BlockSpec(memory_space=pl.ANY)],
        out_specs=vmem,
        scratch_shapes=[
            pltpu.VMEM(sources.shape, jnp.bfloat16),
            pltpu.VMEM(inverse_tiles.shape, jnp.bfloat16),
            pltpu.VMEM(inverse_tiles.shape, jnp.bfloat16),
            pltpu.VMEM((slabs, noff, 2, blk, blk), jnp.bfloat16),
            pltpu.VMEM((slabs, noff, 2 * blk, 2 * blk), jnp.bfloat16),
            pltpu.VMEM((APPS, noff, 2, nrhs, blk), jnp.bfloat16),
            pltpu.VMEM((APPS, 2, nrhs, blk), jnp.bfloat16),
            pltpu.VMEM((slabs, 2, nrhs, blk), jnp.bfloat16),
            pltpu.VMEM((slabs, 2, nrhs, blk), jnp.float32),
            pltpu.VMEM((slabs, 2, nrhs, blk), jnp.float32),
            pltpu.VMEM((2, blk, nrhs), jnp.bfloat16),
            pltpu.SemaphoreType.DMA((APPS, noff, CHUNKS)),
            pltpu.SemaphoreType.DMA((APPS, noff, CHUNKS)),
            pltpu.SemaphoreType.DMA((slabs, ncol)),
            pltpu.SemaphoreType.DMA((slabs, ncol)),
            pltpu.SemaphoreType.DMA(()),
            pltpu.SemaphoreType.DMA(()),
            pltpu.SemaphoreType.DMA((1 + slabs,)),
        ],
        compiler_params=pltpu.CompilerParams(
            has_side_effects=True, collective_id=0, vmem_limit_bytes=67043328
        ),
    )(trig, pattern, sources, inverse_tiles)


def solution(mesh):
    placed = (
        P("sec", ("lat", "col"), None, None, None),
        P("sec", "lat", "col", None, None, None),
        P("sec", "lat", "col"),
        P(),
    )
    return jax.shard_map(
        shards,
        mesh=mesh,
        in_specs=placed,
        out_specs=P("sec", ("lat", "col"), None, None, None),
        check_vma=False,
    )
```

```python
import functools

import jax
import jax.numpy as jnp
from jax import lax
from jax.experimental import pallas as pl
from jax.experimental.pallas import tpu as pltpu
from jax.sharding import PartitionSpec as P

OFF = 8
PHASES = 16
APPS = 7
CHUNKS = 8

coupling = 0.8

MESH_ID = pl.DeviceIdType.MESH


def sweep_kernel(
    nlat, ncol, koff, reach, chunks,
    trig_ref, pat_ref, src_hbm, tiles_hbm, out_ref,
    src_ref, tiles_ref, mtiles, tiles2, wbuf, xbuf, fbuf, srct, vt, outt, srcbuf,
    rs1, ss1, rst, sst, rsrc, ssrc, lsem,
):
    sec = lax.axis_index("sec")
    lat = lax.axis_index("lat")
    col = lax.axis_index("col")
    cos_v = trig_ref[0]
    sin_v = trig_ref[1]
    noff = koff * ncol
    shifts = [d for d in range(reach - noff + 1, reach + 1)]
    width = xbuf.shape[3] // chunks

    loads = [pltpu.make_async_copy(src_hbm, src_ref, lsem.at[0])]
    for slab in range(tiles_ref.shape[0]):
        loads.append(pltpu.make_async_copy(tiles_hbm.at[slab], tiles_ref.at[slab], lsem.at[1 + slab]))
    for load in loads:
        load.start()

    barrier = pltpu.get_barrier_semaphore()
    partners = 0
    for ds in range(2):
        for d in range(-reach, reach + 1):
            if ds == 0 and d == 0:
                continue
            q = col + d
            pl.semaphore_signal(
                barrier, 1,
                device_id=((sec + ds) % 2, (lat + q // ncol + nlat) % nlat, (q + ncol) % ncol),
                device_id_type=MESH_ID,
            )
            partners += 1
    pl.semaphore_wait(barrier, partners)
    loads[0].wait()

    def tile_copy(slab, c0v, r):
        return pltpu.make_async_remote_copy(
            src_ref=mtiles.at[slab, r],
            dst_ref=tiles2.at[slab, pl.ds(c0v * koff, koff)],
            send_sem=sst.at[slab, r],
            recv_sem=rst.at[slab, c0v],
            device_id=(sec, lat, r),
            device_id_type=MESH_ID,
        )

    def share_tiles(slab):
        loads[1 + slab].wait()
        for r in range(ncol):
            for j in range(koff):
                keep = pat_ref[slab, r, j] != 0
                tile = tiles_ref[slab, r, j]
                mtiles[slab, r, j] = jnp.where(keep, tile, jnp.zeros_like(tile))
        for c0v in range(ncol):
            @pl.when(col == c0v)
            def _():
                for r in range(ncol):
                    if r != c0v:
                        tile_copy(slab, c0v, r).start()
                tiles2[slab, pl.ds(c0v * koff, koff)] = mtiles[slab, c0v]

    def wait_tiles(slab):
        for c in range(ncol):
            @pl.when(col != c)
            def _():
                tile_copy(slab, c, c).wait_recv()
        blk = tiles2.shape[3]
        for k in range(noff):
            tr_t = tiles2[slab, k, 0].T
            ti_t = tiles2[slab, k, 1].T
            wbuf[slab, k, :blk, :blk] = tr_t
            wbuf[slab, k, :blk, blk:] = ti_t
            wbuf[slab, k, blk:, :blk] = (-ti_t.astype(jnp.float32)).astype(jnp.bfloat16)
            wbuf[slab, k, blk:, blk:] = tr_t

    def wait_tile_sends(slab):
        for c0v in range(ncol):
            @pl.when(col == c0v)
            def _():
                for r in range(ncol):
                    if r != c0v:
                        tile_copy(slab, c0v, r).wait_send()

    def part(h):
        return pl.ds(h * width, width)

    def row_copy(n, to_sec, c0v, d, h):
        q = c0v + d
        return pltpu.make_async_remote_copy(
            src_ref=fbuf.at[n, :, part(h)],
            dst_ref=xbuf.at[n, reach - d, :, part(h)],
            send_sem=ss1.at[n, reach - d, h],
            recv_sem=rs1.at[n, reach - d, h],
            device_id=(to_sec, (lat + q // ncol + nlat) % nlat, q % ncol),
            device_id_type=MESH_ID,
        )

    def far_first(c0v):
        def hops(d):
            q = c0v + d
            gap = abs(q % ncol - c0v)
            return min(gap, ncol - gap) + (q // ncol != 0)
        return sorted(shifts, key=lambda d: (-hops(d), d))

    def send_rows(n, to_sec, local, h):
        for c0v in range(ncol):
            @pl.when(col == c0v)
            def _():
                for d in far_first(c0v):
                    if local and d == 0:
                        continue
                    row_copy(n, to_sec, c0v, d, h).start()

    def wait_row_sends(n, to_sec, local):
        for c0v in range(ncol):
            @pl.when(col == c0v)
            def _():
                for h in range(chunks):
                    for d in shifts:
                        if local and d == 0:
                            continue
                        row_copy(n, to_sec, c0v, d, h).wait_send()

    def put_field(n, to_sec, local, h, value):
        fbuf[n, :, part(h)] = value.astype(jnp.bfloat16)
        send_rows(n, to_sec, local, h)

    def run_app(n, slab, local, finish):
        order = sorted(range(noff), key=lambda k: (abs(k - reach), k))
        dot = functools.partial(jnp.dot, preferred_element_type=jnp.float32)
        for h in range(chunks):
            acc_r = None
            for k in order:
                d = k - reach
                if not (local and d == 0):
                    row_copy(n, sec, 0, -d, h).wait_recv()
                lo = (lat == 0) & (k < reach - col)
                hi = (lat == nlat - 1) & (k >= reach - col + ncol)

                @pl.when((lo | hi) & (not (local and d == 0)))
                def _():
                    sn = jnp.where(lo, -sin_v, sin_v)
                    x = xbuf[n, k, :, part(h)].astype(jnp.float32)
                    xbuf[n, k, 0, part(h)] = (x[0] * cos_v - x[1] * sn).astype(jnp.bfloat16)
                    xbuf[n, k, 1, part(h)] = (x[0] * sn + x[1] * cos_v).astype(jnp.bfloat16)

                if local and d == 0:
                    xr = fbuf[n, 0, part(h)]
                    xi = fbuf[n, 1, part(h)]
                else:
                    xr = xbuf[n, k, 0, part(h)]
                    xi = xbuf[n, k, 1, part(h)]
                both = dot(jnp.concatenate([xr, xi], axis=1), wbuf[slab, k])
                acc_r = both if acc_r is None else acc_r + both
            blk = xbuf.shape[4]
            finish(h, jnp.stack([acc_r[:, :blk], acc_r[:, blk:]], 0))

    def transpose_in(dst, src):
        for ri in range(2):
            dst[ri] = src[ri].astype(jnp.float32).T.astype(jnp.bfloat16)

    @pl.when(sec == 0)
    def _():
        share_tiles(0)
        for ri in range(2):
            fbuf[0, ri] = src_ref[0, 0, ri].astype(jnp.float32).T.astype(jnp.bfloat16)
        for h in range(chunks):
            send_rows(0, 0, True, h)
        transpose_in(srct.at[1], src_ref.at[1, 0])
        share_tiles(1)
        wait_tiles(0)

        def fin0(h, r):
            vt[0, :, part(h)] = r
            put_field(1, 0, True, h, srct[1, :, part(h)].astype(jnp.float32) + coupling * r)

        run_app(0, 0, True, fin0)
        wait_tiles(1)
        src_copy = pltpu.make_async_remote_copy(
            src_ref=src_ref.at[0, 0], dst_ref=srcbuf, send_sem=ssrc, recv_sem=rsrc,
            device_id=(1, lat, col), device_id_type=MESH_ID,
        )

        def fin1(h, r):
            vt[1, :, part(h)] = r
            if h == 0:
                src_copy.wait_recv()
                transpose_in(srct.at[0], srcbuf)
            put_field(2, 1, False, h, srct[0, :, part(h)].astype(jnp.float32) + coupling * r)

        run_app(1, 1, True, fin1)

        def fin5(h, r):
            sol = vt[1, :, part(h)] + coupling * r
            outt[1, :, part(h)] = sol
            put_field(6, 0, True, h, sol)

        run_app(5, 1, False, fin5)

        def fin6(h, r):
            outt[0, :, part(h)] = vt[0, :, part(h)] + coupling * r

        run_app(6, 0, True, fin6)
        wait_row_sends(0, 0, True)
        wait_row_sends(1, 0, True)
        wait_row_sends(2, 1, False)
        wait_row_sends(6, 0, True)
        wait_tile_sends(0)
        wait_tile_sends(1)

    @pl.when(sec == 1)
    def _():
        src_copy = pltpu.make_async_remote_copy(
            src_ref=src_ref.at[0, 0], dst_ref=srcbuf, send_sem=ssrc, recv_sem=rsrc,
            device_id=(0, lat, col), device_id_type=MESH_ID,
        )
        src_copy.start()
        share_tiles(0)
        share_tiles(1)
        transpose_in(srct.at[1], src_ref.at[1, 0])
        wait_tiles(0)
        wait_tiles(1)

        def fin2(h, r):
            vt[0, :, part(h)] = r
            put_field(3, 1, True, h, srct[1, :, part(h)].astype(jnp.float32) + coupling * r)

        run_app(2, 0, False, fin2)

        def fin3(h, r):
            outt[1, :, part(h)] = r
            put_field(4, 1, True, h, r)

        run_app(3, 1, True, fin3)

        def fin4(h, r):
            sol = vt[0, :, part(h)] + coupling * r
            outt[0, :, part(h)] = sol
            put_field(5, 0, False, h, sol)

        run_app(4, 0, True, fin4)
        wait_row_sends(3, 1, True)
        wait_row_sends(4, 1, True)
        wait_row_sends(5, 0, False)
        wait_tile_sends(0)
        wait_tile_sends(1)
        src_copy.wait_send()

    for s in range(2):
        for ri in range(2):
            out_ref[s, 0, ri] = outt[s, ri].T


def shards(sources, inverse_tiles, pattern, phase_index):
    nlat = lax.axis_size("lat")
    ncol = lax.axis_size("col")
    koff = inverse_tiles.shape[2]
    reach = OFF // 2
    noff = koff * ncol
    blk, nrhs = sources.shape[3], sources.shape[4]
    angle = 2.0 * jnp.pi * phase_index[0].astype(jnp.float32) / PHASES
    trig = jnp.stack([jnp.cos(angle), jnp.sin(angle)])
    kernel = functools.partial(sweep_kernel, nlat, ncol, koff, reach, CHUNKS)
    vmem = pl.BlockSpec(memory_space=pltpu.VMEM)
    smem = pl.BlockSpec(memory_space=pltpu.SMEM)
    slabs = inverse_tiles.shape[0]
    return pl.pallas_call(
        kernel,
        out_shape=jax.ShapeDtypeStruct(sources.shape, jnp.float32),
        in_specs=[smem, smem, pl.BlockSpec(memory_space=pl.ANY), pl.BlockSpec(memory_space=pl.ANY)],
        out_specs=vmem,
        scratch_shapes=[
            pltpu.VMEM(sources.shape, jnp.bfloat16),
            pltpu.VMEM(inverse_tiles.shape, jnp.bfloat16),
            pltpu.VMEM(inverse_tiles.shape, jnp.bfloat16),
            pltpu.VMEM((slabs, noff, 2, blk, blk), jnp.bfloat16),
            pltpu.VMEM((slabs, noff, 2 * blk, 2 * blk), jnp.bfloat16),
            pltpu.VMEM((APPS, noff, 2, nrhs, blk), jnp.bfloat16),
            pltpu.VMEM((APPS, 2, nrhs, blk), jnp.bfloat16),
            pltpu.VMEM((slabs, 2, nrhs, blk), jnp.bfloat16),
            pltpu.VMEM((slabs, 2, nrhs, blk), jnp.float32),
            pltpu.VMEM((slabs, 2, nrhs, blk), jnp.float32),
            pltpu.VMEM((2, blk, nrhs), jnp.bfloat16),
            pltpu.SemaphoreType.DMA((APPS, noff, CHUNKS)),
            pltpu.SemaphoreType.DMA((APPS, noff, CHUNKS)),
            pltpu.SemaphoreType.DMA((slabs, ncol)),
            pltpu.SemaphoreType.DMA((slabs, ncol)),
            pltpu.SemaphoreType.DMA(()),
            pltpu.SemaphoreType.DMA(()),
            pltpu.SemaphoreType.DMA((1 + slabs,)),
        ],
        compiler_params=pltpu.CompilerParams(
            has_side_effects=True, collective_id=0, vmem_limit_bytes=67043328
        ),
    )(trig, pattern, sources, inverse_tiles)


def solution(mesh):
    placed = (
        P("sec", ("lat", "col"), None, None, None),
        P("sec", "lat", "col", None, None, None),
        P("sec", "lat", "col"),
        P(),
    )
    return jax.shard_map(
        shards,
        mesh=mesh,
        in_specs=placed,
        out_specs=P("sec", ("lat", "col"), None, None, None),
        check_vma=False,
    )
```

```python
import functools

import jax
import jax.numpy as jnp
from jax import lax
from jax.experimental import pallas as pl
from jax.experimental.pallas import tpu as pltpu
from jax.sharding import PartitionSpec as P

OFF = 8
PHASES = 16
APPS = 7
CHUNKS = 4

coupling = 0.8

MESH_ID = pl.DeviceIdType.MESH


def sweep_kernel(
    nlat, ncol, koff, reach, chunks,
    trig_ref, pat_ref, src_hbm, tiles_hbm, out_ref,
    src_ref, tiles_ref, mtiles, tiles2, wbuf, xbuf, fbuf, srct, vt, outt, srcbuf,
    rs1, ss1, rst, sst, rsrc, ssrc, lsem,
):
    sec = lax.axis_index("sec")
    lat = lax.axis_index("lat")
    col = lax.axis_index("col")
    cos_v = trig_ref[0]
    sin_v = trig_ref[1]
    noff = koff * ncol
    shifts = [d for d in range(reach - noff + 1, reach + 1)]
    width = xbuf.shape[3] // chunks

    loads = [pltpu.make_async_copy(src_hbm, src_ref, lsem.at[0])]
    for slab in range(tiles_ref.shape[0]):
        loads.append(pltpu.make_async_copy(tiles_hbm.at[slab], tiles_ref.at[slab], lsem.at[1 + slab]))
    for load in loads:
        load.start()

    barrier = pltpu.get_barrier_semaphore()
    partners = 0
    for ds in range(2):
        for d in range(-reach, reach + 1):
            if ds == 0 and d == 0:
                continue
            q = col + d
            pl.semaphore_signal(
                barrier, 1,
                device_id=((sec + ds) % 2, (lat + q // ncol + nlat) % nlat, (q + ncol) % ncol),
                device_id_type=MESH_ID,
            )
            partners += 1
    pl.semaphore_wait(barrier, partners)
    loads[0].wait()

    def tile_copy(slab, c0v, r):
        return pltpu.make_async_remote_copy(
            src_ref=mtiles.at[slab, r],
            dst_ref=tiles2.at[slab, pl.ds(c0v * koff, koff)],
            send_sem=sst.at[slab, r],
            recv_sem=rst.at[slab, c0v],
            device_id=(sec, lat, r),
            device_id_type=MESH_ID,
        )

    def share_tiles(slab):
        loads[1 + slab].wait()
        for r in range(ncol):
            for j in range(koff):
                keep = pat_ref[slab, r, j] != 0
                tile = tiles_ref[slab, r, j]
                mtiles[slab, r, j] = jnp.where(keep, tile, jnp.zeros_like(tile))
        for c0v in range(ncol):
            @pl.when(col == c0v)
            def _():
                for r in range(ncol):
                    if r != c0v:
                        tile_copy(slab, c0v, r).start()
                tiles2[slab, pl.ds(c0v * koff, koff)] = mtiles[slab, c0v]

    def build_block(slab, k):
        blk = tiles2.shape[3]
        tr_t = tiles2[slab, k, 0].T
        ti_t = tiles2[slab, k, 1].T
        wbuf[slab, k, :blk, :blk] = tr_t
        wbuf[slab, k, :blk, blk:] = ti_t
        wbuf[slab, k, blk:, :blk] = (-ti_t.astype(jnp.float32)).astype(jnp.bfloat16)
        wbuf[slab, k, blk:, blk:] = tr_t

    def build_own_blocks(slab):
        for j in range(koff):
            build_block(slab, col * koff + j)

    def wait_tiles(slab):
        for c in range(ncol):
            @pl.when(col != c)
            def _():
                tile_copy(slab, c, c).wait_recv()
        for k in range(noff):
            @pl.when(col != k // koff)
            def _():
                build_block(slab, k)

    def wait_tile_sends(slab):
        for c0v in range(ncol):
            @pl.when(col == c0v)
            def _():
                for r in range(ncol):
                    if r != c0v:
                        tile_copy(slab, c0v, r).wait_send()

    def part(h):
        return pl.ds(h * width, width)

    def row_copy(n, to_sec, c0v, d, h):
        q = c0v + d
        return pltpu.make_async_remote_copy(
            src_ref=fbuf.at[n, :, part(h)],
            dst_ref=xbuf.at[n, reach - d, :, part(h)],
            send_sem=ss1.at[n, reach - d, h],
            recv_sem=rs1.at[n, reach - d, h],
            device_id=(to_sec, (lat + q // ncol + nlat) % nlat, q % ncol),
            device_id_type=MESH_ID,
        )

    def far_first(c0v):
        def hops(d):
            q = c0v + d
            gap = abs(q % ncol - c0v)
            return min(gap, ncol - gap) + (q // ncol != 0)
        return sorted(shifts, key=lambda d: (-hops(d), d))

    def send_rows(n, to_sec, local, h):
        for c0v in range(ncol):
            @pl.when(col == c0v)
            def _():
                for d in far_first(c0v):
                    if local and d == 0:
                        continue
                    row_copy(n, to_sec, c0v, d, h).start()

    def wait_row_sends(n, to_sec, local):
        for c0v in range(ncol):
            @pl.when(col == c0v)
            def _():
                for h in range(chunks):
                    for d in shifts:
                        if local and d == 0:
                            continue
                        row_copy(n, to_sec, c0v, d, h).wait_send()

    def put_field(n, to_sec, local, h, value):
        fbuf[n, :, part(h)] = value.astype(jnp.bfloat16)
        send_rows(n, to_sec, local, h)

    def run_app(n, slab, local, finish):
        order = sorted(range(noff), key=lambda k: (abs(k - reach), k))
        dot = functools.partial(jnp.dot, preferred_element_type=jnp.float32)
        for h in range(chunks):
            acc_r = None
            for k in order:
                d = k - reach
                if not (local and d == 0):
                    row_copy(n, sec, 0, -d, h).wait_recv()
                lo = (lat == 0) & (k < reach - col)
                hi = (lat == nlat - 1) & (k >= reach - col + ncol)

                @pl.when((lo | hi) & (not (local and d == 0)))
                def _():
                    sn = jnp.where(lo, -sin_v, sin_v)
                    x = xbuf[n, k, :, part(h)].astype(jnp.float32)
                    xbuf[n, k, 0, part(h)] = (x[0] * cos_v - x[1] * sn).astype(jnp.bfloat16)
                    xbuf[n, k, 1, part(h)] = (x[0] * sn + x[1] * cos_v).astype(jnp.bfloat16)

                if local and d == 0:
                    xr = fbuf[n, 0, part(h)]
                    xi = fbuf[n, 1, part(h)]
                else:
                    xr = xbuf[n, k, 0, part(h)]
                    xi = xbuf[n, k, 1, part(h)]
                both = dot(jnp.concatenate([xr, xi], axis=1), wbuf[slab, k])
                acc_r = both if acc_r is None else acc_r + both
            blk = xbuf.shape[4]
            finish(h, jnp.stack([acc_r[:, :blk], acc_r[:, blk:]], 0))

    def transpose_in(dst, src):
        for ri in range(2):
            dst[ri] = src[ri].astype(jnp.float32).T.astype(jnp.bfloat16)

    @pl.when(sec == 0)
    def _():
        for ri in range(2):
            fbuf[0, ri] = src_ref[0, 0, ri].astype(jnp.float32).T.astype(jnp.bfloat16)
        for h in range(chunks):
            send_rows(0, 0, True, h)
        share_tiles(0)
        build_own_blocks(0)
        transpose_in(srct.at[1], src_ref.at[1, 0])
        share_tiles(1)
        build_own_blocks(1)
        wait_tiles(0)

        def fin0(h, r):
            vt[0, :, part(h)] = r
            put_field(1, 0, True, h, srct[1, :, part(h)].astype(jnp.float32) + coupling * r)

        run_app(0, 0, True, fin0)
        wait_tiles(1)
        src_copy = pltpu.make_async_remote_copy(
            src_ref=src_ref.at[0, 0], dst_ref=srcbuf, send_sem=ssrc, recv_sem=rsrc,
            device_id=(1, lat, col), device_id_type=MESH_ID,
        )

        def fin1(h, r):
            vt[1, :, part(h)] = r
            if h == 0:
                src_copy.wait_recv()
                transpose_in(srct.at[0], srcbuf)
            put_field(2, 1, False, h, srct[0, :, part(h)].astype(jnp.float32) + coupling * r)

        run_app(1, 1, True, fin1)

        def fin5(h, r):
            sol = vt[1, :, part(h)] + coupling * r
            outt[1, :, part(h)] = sol
            put_field(6, 0, True, h, sol)

        run_app(5, 1, False, fin5)

        def fin6(h, r):
            outt[0, :, part(h)] = vt[0, :, part(h)] + coupling * r

        run_app(6, 0, True, fin6)
        wait_row_sends(0, 0, True)
        wait_row_sends(1, 0, True)
        wait_row_sends(2, 1, False)
        wait_row_sends(6, 0, True)
        wait_tile_sends(0)
        wait_tile_sends(1)

    @pl.when(sec == 1)
    def _():
        src_copy = pltpu.make_async_remote_copy(
            src_ref=src_ref.at[0, 0], dst_ref=srcbuf, send_sem=ssrc, recv_sem=rsrc,
            device_id=(0, lat, col), device_id_type=MESH_ID,
        )
        src_copy.start()
        share_tiles(0)
        share_tiles(1)
        build_own_blocks(0)
        build_own_blocks(1)
        transpose_in(srct.at[1], src_ref.at[1, 0])
        wait_tiles(0)
        wait_tiles(1)

        def fin2(h, r):
            vt[0, :, part(h)] = r
            put_field(3, 1, True, h, srct[1, :, part(h)].astype(jnp.float32) + coupling * r)

        run_app(2, 0, False, fin2)

        def fin3(h, r):
            outt[1, :, part(h)] = r
            put_field(4, 1, True, h, r)

        run_app(3, 1, True, fin3)

        def fin4(h, r):
            sol = vt[0, :, part(h)] + coupling * r
            outt[0, :, part(h)] = sol
            put_field(5, 0, False, h, sol)

        run_app(4, 0, True, fin4)
        wait_row_sends(3, 1, True)
        wait_row_sends(4, 1, True)
        wait_row_sends(5, 0, False)
        wait_tile_sends(0)
        wait_tile_sends(1)
        src_copy.wait_send()

    for s in range(2):
        for ri in range(2):
            out_ref[s, 0, ri] = outt[s, ri].T


def shards(sources, inverse_tiles, pattern, phase_index):
    nlat = lax.axis_size("lat")
    ncol = lax.axis_size("col")
    koff = inverse_tiles.shape[2]
    reach = OFF // 2
    noff = koff * ncol
    blk, nrhs = sources.shape[3], sources.shape[4]
    angle = 2.0 * jnp.pi * phase_index[0].astype(jnp.float32) / PHASES
    trig = jnp.stack([jnp.cos(angle), jnp.sin(angle)])
    kernel = functools.partial(sweep_kernel, nlat, ncol, koff, reach, CHUNKS)
    vmem = pl.BlockSpec(memory_space=pltpu.VMEM)
    smem = pl.BlockSpec(memory_space=pltpu.SMEM)
    slabs = inverse_tiles.shape[0]
    return pl.pallas_call(
        kernel,
        out_shape=jax.ShapeDtypeStruct(sources.shape, jnp.float32),
        in_specs=[smem, smem, pl.BlockSpec(memory_space=pl.ANY), pl.BlockSpec(memory_space=pl.ANY)],
        out_specs=vmem,
        scratch_shapes=[
            pltpu.VMEM(sources.shape, jnp.bfloat16),
            pltpu.VMEM(inverse_tiles.shape, jnp.bfloat16),
            pltpu.VMEM(inverse_tiles.shape, jnp.bfloat16),
            pltpu.VMEM((slabs, noff, 2, blk, blk), jnp.bfloat16),
            pltpu.VMEM((slabs, noff, 2 * blk, 2 * blk), jnp.bfloat16),
            pltpu.VMEM((APPS, noff, 2, nrhs, blk), jnp.bfloat16),
            pltpu.VMEM((APPS, 2, nrhs, blk), jnp.bfloat16),
            pltpu.VMEM((slabs, 2, nrhs, blk), jnp.bfloat16),
            pltpu.VMEM((slabs, 2, nrhs, blk), jnp.float32),
            pltpu.VMEM((slabs, 2, nrhs, blk), jnp.float32),
            pltpu.VMEM((2, blk, nrhs), jnp.bfloat16),
            pltpu.SemaphoreType.DMA((APPS, noff, CHUNKS)),
            pltpu.SemaphoreType.DMA((APPS, noff, CHUNKS)),
            pltpu.SemaphoreType.DMA((slabs, ncol)),
            pltpu.SemaphoreType.DMA((slabs, ncol)),
            pltpu.SemaphoreType.DMA(()),
            pltpu.SemaphoreType.DMA(()),
            pltpu.SemaphoreType.DMA((1 + slabs,)),
        ],
        compiler_params=pltpu.CompilerParams(
            has_side_effects=True, collective_id=0, vmem_limit_bytes=67043328
        ),
    )(trig, pattern, sources, inverse_tiles)


def solution(mesh):
    placed = (
        P("sec", ("lat", "col"), None, None, None),
        P("sec", "lat", "col", None, None, None),
        P("sec", "lat", "col"),
        P(),
    )
    return jax.shard_map(
        shards,
        mesh=mesh,
        in_specs=placed,
        out_specs=P("sec", ("lat", "col"), None, None, None),
        check_vma=False,
    )
```

```python
import functools

import jax
import jax.numpy as jnp
from jax import lax
from jax.experimental import pallas as pl
from jax.experimental.pallas import tpu as pltpu
from jax.sharding import PartitionSpec as P

OFF = 8
PHASES = 16
APPS = 7
CHUNKS = 4

coupling = 0.8

MESH_ID = pl.DeviceIdType.MESH


def sweep_kernel(
    nlat, ncol, koff, reach, chunks,
    trig_ref, pat_ref, src_hbm, tiles_hbm, out_ref,
    src_ref, tiles_ref, mtiles, tiles2, wbuf, xbuf, fbuf, srct, vt, outt, srcbuf,
    rs1, ss1, rst, sst, rsrc, ssrc, lsem,
):
    sec = lax.axis_index("sec")
    lat = lax.axis_index("lat")
    col = lax.axis_index("col")
    cos_v = trig_ref[0]
    sin_v = trig_ref[1]
    noff = koff * ncol
    shifts = [d for d in range(reach - noff + 1, reach + 1)]
    width = xbuf.shape[3] // chunks

    loads = [pltpu.make_async_copy(src_hbm, src_ref, lsem.at[0])]
    for slab in range(tiles_ref.shape[0]):
        loads.append(pltpu.make_async_copy(tiles_hbm.at[slab], tiles_ref.at[slab], lsem.at[1 + slab]))
    for load in loads:
        load.start()

    barrier = pltpu.get_barrier_semaphore()
    partners = 0
    for ds in range(2):
        for d in range(-reach, reach + 1):
            if ds == 0 and d == 0:
                continue
            q = col + d
            pl.semaphore_signal(
                barrier, 1,
                device_id=((sec + ds) % 2, (lat + q // ncol + nlat) % nlat, (q + ncol) % ncol),
                device_id_type=MESH_ID,
            )
            partners += 1
    pl.semaphore_wait(barrier, partners)
    loads[0].wait()

    def tile_copy(slab, c0v, r):
        return pltpu.make_async_remote_copy(
            src_ref=mtiles.at[slab, r],
            dst_ref=tiles2.at[slab, pl.ds(c0v * koff, koff)],
            send_sem=sst.at[slab, r],
            recv_sem=rst.at[slab, c0v],
            device_id=(sec, lat, r),
            device_id_type=MESH_ID,
        )

    def share_tiles(slab):
        loads[1 + slab].wait()
        for r in range(ncol):
            for j in range(koff):
                keep = pat_ref[slab, r, j] != 0
                tile = tiles_ref[slab, r, j]
                mtiles[slab, r, j] = jnp.where(keep, tile, jnp.zeros_like(tile))
        for c0v in range(ncol):
            @pl.when(col == c0v)
            def _():
                for r in range(ncol):
                    if r != c0v:
                        tile_copy(slab, c0v, r).start()
                tiles2[slab, pl.ds(c0v * koff, koff)] = mtiles[slab, c0v]

    def wait_tiles(slab):
        for c in range(ncol):
            @pl.when(col != c)
            def _():
                tile_copy(slab, c, c).wait_recv()
        blk = tiles2.shape[3]
        for k in range(noff):
            tr_t = tiles2[slab, k, 0].T
            ti_t = tiles2[slab, k, 1].T
            pair, half = (k - reach, 0) if k >= reach else (reach - 1 - k, 1)
            top = half * 2 * blk
            wbuf[slab, pair, top:top + blk, :blk] = tr_t
            wbuf[slab, pair, top:top + blk, blk:] = ti_t
            wbuf[slab, pair, top + blk:top + 2 * blk, :blk] = (-ti_t.astype(jnp.float32)).astype(jnp.bfloat16)
            wbuf[slab, pair, top + blk:top + 2 * blk, blk:] = tr_t

    def wait_tile_sends(slab):
        for c0v in range(ncol):
            @pl.when(col == c0v)
            def _():
                for r in range(ncol):
                    if r != c0v:
                        tile_copy(slab, c0v, r).wait_send()

    def part(h):
        return pl.ds(h * width, width)

    def row_copy(n, to_sec, c0v, d, h):
        q = c0v + d
        return pltpu.make_async_remote_copy(
            src_ref=fbuf.at[n, :, part(h)],
            dst_ref=xbuf.at[n, reach - d, :, part(h)],
            send_sem=ss1.at[n, reach - d, h],
            recv_sem=rs1.at[n, reach - d, h],
            device_id=(to_sec, (lat + q // ncol + nlat) % nlat, q % ncol),
            device_id_type=MESH_ID,
        )

    def far_first(c0v):
        def hops(d):
            q = c0v + d
            gap = abs(q % ncol - c0v)
            return min(gap, ncol - gap) + (q // ncol != 0)
        return sorted(shifts, key=lambda d: (-hops(d), d))

    def send_rows(n, to_sec, local, h):
        for c0v in range(ncol):
            @pl.when(col == c0v)
            def _():
                for d in far_first(c0v):
                    if local and d == 0:
                        continue
                    row_copy(n, to_sec, c0v, d, h).start()

    def wait_row_sends(n, to_sec, local):
        for c0v in range(ncol):
            @pl.when(col == c0v)
            def _():
                for h in range(chunks):
                    for d in shifts:
                        if local and d == 0:
                            continue
                        row_copy(n, to_sec, c0v, d, h).wait_send()

    def put_field(n, to_sec, local, h, value):
        fbuf[n, :, part(h)] = value.astype(jnp.bfloat16)
        send_rows(n, to_sec, local, h)

    def run_app(n, slab, local, finish):
        order = sorted(range(noff), key=lambda k: (abs(k - reach), k))
        dot = functools.partial(jnp.dot, preferred_element_type=jnp.float32)
        for h in range(chunks):
            acc_r = None
            pieces = []
            for k in order:
                d = k - reach
                if not (local and d == 0):
                    row_copy(n, sec, 0, -d, h).wait_recv()
                lo = (lat == 0) & (k < reach - col)
                hi = (lat == nlat - 1) & (k >= reach - col + ncol)

                @pl.when((lo | hi) & (not (local and d == 0)))
                def _():
                    sn = jnp.where(lo, -sin_v, sin_v)
                    x = xbuf[n, k, :, part(h)].astype(jnp.float32)
                    xbuf[n, k, 0, part(h)] = (x[0] * cos_v - x[1] * sn).astype(jnp.bfloat16)
                    xbuf[n, k, 1, part(h)] = (x[0] * sn + x[1] * cos_v).astype(jnp.bfloat16)

                if local and d == 0:
                    xr = fbuf[n, 0, part(h)]
                    xi = fbuf[n, 1, part(h)]
                else:
                    xr = xbuf[n, k, 0, part(h)]
                    xi = xbuf[n, k, 1, part(h)]
                pieces += [xr, xi]
                if len(pieces) == 4:
                    pair = max(k, 2 * reach - 1 - k) - reach
                    both = dot(jnp.concatenate(pieces, axis=1), wbuf[slab, pair])
                    acc_r = both if acc_r is None else acc_r + both
                    pieces = []
            blk = xbuf.shape[4]
            finish(h, jnp.stack([acc_r[:, :blk], acc_r[:, blk:]], 0))

    def transpose_in(dst, src):
        for ri in range(2):
            dst[ri] = src[ri].astype(jnp.float32).T.astype(jnp.bfloat16)

    @pl.when(sec == 0)
    def _():
        share_tiles(0)
        for ri in range(2):
            fbuf[0, ri] = src_ref[0, 0, ri].astype(jnp.float32).T.astype(jnp.bfloat16)
        for h in range(chunks):
            send_rows(0, 0, True, h)
        transpose_in(srct.at[1], src_ref.at[1, 0])
        share_tiles(1)
        wait_tiles(0)

        def fin0(h, r):
            vt[0, :, part(h)] = r
            put_field(1, 0, True, h, srct[1, :, part(h)].astype(jnp.float32) + coupling * r)

        run_app(0, 0, True, fin0)
        wait_tiles(1)
        src_copy = pltpu.make_async_remote_copy(
            src_ref=src_ref.at[0, 0], dst_ref=srcbuf, send_sem=ssrc, recv_sem=rsrc,
            device_id=(1, lat, col), device_id_type=MESH_ID,
        )

        def fin1(h, r):
            vt[1, :, part(h)] = r
            if h == 0:
                src_copy.wait_recv()
                transpose_in(srct.at[0], srcbuf)
            put_field(2, 1, False, h, srct[0, :, part(h)].astype(jnp.float32) + coupling * r)

        run_app(1, 1, True, fin1)

        def fin5(h, r):
            sol = vt[1, :, part(h)] + coupling * r
            outt[1, :, part(h)] = sol
            put_field(6, 0, True, h, sol)

        run_app(5, 1, False, fin5)

        def fin6(h, r):
            outt[0, :, part(h)] = vt[0, :, part(h)] + coupling * r

        run_app(6, 0, True, fin6)
        wait_row_sends(0, 0, True)
        wait_row_sends(1, 0, True)
        wait_row_sends(2, 1, False)
        wait_row_sends(6, 0, True)
        wait_tile_sends(0)
        wait_tile_sends(1)

    @pl.when(sec == 1)
    def _():
        src_copy = pltpu.make_async_remote_copy(
            src_ref=src_ref.at[0, 0], dst_ref=srcbuf, send_sem=ssrc, recv_sem=rsrc,
            device_id=(0, lat, col), device_id_type=MESH_ID,
        )
        src_copy.start()
        share_tiles(0)
        share_tiles(1)
        transpose_in(srct.at[1], src_ref.at[1, 0])
        wait_tiles(0)
        wait_tiles(1)

        def fin2(h, r):
            vt[0, :, part(h)] = r
            put_field(3, 1, True, h, srct[1, :, part(h)].astype(jnp.float32) + coupling * r)

        run_app(2, 0, False, fin2)

        def fin3(h, r):
            outt[1, :, part(h)] = r
            put_field(4, 1, True, h, r)

        run_app(3, 1, True, fin3)

        def fin4(h, r):
            sol = vt[0, :, part(h)] + coupling * r
            outt[0, :, part(h)] = sol
            put_field(5, 0, False, h, sol)

        run_app(4, 0, True, fin4)
        wait_row_sends(3, 1, True)
        wait_row_sends(4, 1, True)
        wait_row_sends(5, 0, False)
        wait_tile_sends(0)
        wait_tile_sends(1)
        src_copy.wait_send()

    for s in range(2):
        for ri in range(2):
            out_ref[s, 0, ri] = outt[s, ri].T


def shards(sources, inverse_tiles, pattern, phase_index):
    nlat = lax.axis_size("lat")
    ncol = lax.axis_size("col")
    koff = inverse_tiles.shape[2]
    reach = OFF // 2
    noff = koff * ncol
    blk, nrhs = sources.shape[3], sources.shape[4]
    angle = 2.0 * jnp.pi * phase_index[0].astype(jnp.float32) / PHASES
    trig = jnp.stack([jnp.cos(angle), jnp.sin(angle)])
    kernel = functools.partial(sweep_kernel, nlat, ncol, koff, reach, CHUNKS)
    vmem = pl.BlockSpec(memory_space=pltpu.VMEM)
    smem = pl.BlockSpec(memory_space=pltpu.SMEM)
    slabs = inverse_tiles.shape[0]
    return pl.pallas_call(
        kernel,
        out_shape=jax.ShapeDtypeStruct(sources.shape, jnp.float32),
        in_specs=[smem, smem, pl.BlockSpec(memory_space=pl.ANY), pl.BlockSpec(memory_space=pl.ANY)],
        out_specs=vmem,
        scratch_shapes=[
            pltpu.VMEM(sources.shape, jnp.bfloat16),
            pltpu.VMEM(inverse_tiles.shape, jnp.bfloat16),
            pltpu.VMEM(inverse_tiles.shape, jnp.bfloat16),
            pltpu.VMEM((slabs, noff, 2, blk, blk), jnp.bfloat16),
            pltpu.VMEM((slabs, noff // 2, 4 * blk, 2 * blk), jnp.bfloat16),
            pltpu.VMEM((APPS, noff, 2, nrhs, blk), jnp.bfloat16),
            pltpu.VMEM((APPS, 2, nrhs, blk), jnp.bfloat16),
            pltpu.VMEM((slabs, 2, nrhs, blk), jnp.bfloat16),
            pltpu.VMEM((slabs, 2, nrhs, blk), jnp.float32),
            pltpu.VMEM((slabs, 2, nrhs, blk), jnp.float32),
            pltpu.VMEM((2, blk, nrhs), jnp.bfloat16),
            pltpu.SemaphoreType.DMA((APPS, noff, CHUNKS)),
            pltpu.SemaphoreType.DMA((APPS, noff, CHUNKS)),
            pltpu.SemaphoreType.DMA((slabs, ncol)),
            pltpu.SemaphoreType.DMA((slabs, ncol)),
            pltpu.SemaphoreType.DMA(()),
            pltpu.SemaphoreType.DMA(()),
            pltpu.SemaphoreType.DMA((1 + slabs,)),
        ],
        compiler_params=pltpu.CompilerParams(
            has_side_effects=True, collective_id=0, vmem_limit_bytes=67043328
        ),
    )(trig, pattern, sources, inverse_tiles)


def solution(mesh):
    placed = (
        P("sec", ("lat", "col"), None, None, None),
        P("sec", "lat", "col", None, None, None),
        P("sec", "lat", "col"),
        P(),
    )
    return jax.shard_map(
        shards,
        mesh=mesh,
        in_specs=placed,
        out_specs=P("sec", ("lat", "col"), None, None, None),
        check_vma=False,
    )
```

```python
import functools

import jax
import jax.numpy as jnp
from jax import lax
from jax.experimental import pallas as pl
from jax.experimental.pallas import tpu as pltpu
from jax.sharding import PartitionSpec as P

OFF = 8
PHASES = 16
APPS = 7
CHUNKS = 4

coupling = 0.8

MESH_ID = pl.DeviceIdType.MESH


def sweep_kernel(
    nlat, ncol, koff, reach, chunks,
    trig_ref, pat_ref, src_hbm, tiles_hbm, out_ref,
    src_ref, tiles_ref, mtiles, tiles2, wbuf, xbuf, fbuf, srct, vt, outt, srcbuf,
    rs1, ss1, rst, sst, rsrc, ssrc, lsem,
):
    sec = lax.axis_index("sec")
    lat = lax.axis_index("lat")
    col = lax.axis_index("col")
    cos_v = trig_ref[0]
    sin_v = trig_ref[1]
    noff = koff * ncol
    shifts = [d for d in range(reach - noff + 1, reach + 1)]
    width = xbuf.shape[3] // chunks

    loads = [pltpu.make_async_copy(src_hbm, src_ref, lsem.at[0])]
    for slab in range(tiles_ref.shape[0]):
        loads.append(pltpu.make_async_copy(tiles_hbm.at[slab], tiles_ref.at[slab], lsem.at[1 + slab]))
    for load in loads:
        load.start()

    barrier = pltpu.get_barrier_semaphore()
    partners = 0
    for ds in range(2):
        for d in range(-reach, reach + 1):
            if ds == 0 and d == 0:
                continue
            q = col + d
            pl.semaphore_signal(
                barrier, 1,
                device_id=((sec + ds) % 2, (lat + q // ncol + nlat) % nlat, (q + ncol) % ncol),
                device_id_type=MESH_ID,
            )
            partners += 1
    pl.semaphore_wait(barrier, partners)
    loads[0].wait()

    def tile_copy(slab, c0v, r):
        return pltpu.make_async_remote_copy(
            src_ref=mtiles.at[slab, r],
            dst_ref=tiles2.at[slab, pl.ds(c0v * koff, koff)],
            send_sem=sst.at[slab, r],
            recv_sem=rst.at[slab, c0v],
            device_id=(sec, lat, r),
            device_id_type=MESH_ID,
        )

    def share_tiles(slab):
        loads[1 + slab].wait()
        for r in range(ncol):
            for j in range(koff):
                keep = pat_ref[slab, r, j] != 0
                tile = tiles_ref[slab, r, j]
                mtiles[slab, r, j] = jnp.where(keep, tile, jnp.zeros_like(tile))
        for c0v in range(ncol):
            @pl.when(col == c0v)
            def _():
                for r in range(ncol):
                    if r != c0v:
                        tile_copy(slab, c0v, r).start()
                tiles2[slab, pl.ds(c0v * koff, koff)] = mtiles[slab, c0v]

    def wait_tiles(slab):
        for c in range(ncol):
            @pl.when(col != c)
            def _():
                tile_copy(slab, c, c).wait_recv()
        blk = tiles2.shape[3]
        for k in range(noff):
            tr_t = tiles2[slab, k, 0].T
            ti_t = tiles2[slab, k, 1].T
            wbuf[slab, k, :blk, :blk] = tr_t
            wbuf[slab, k, :blk, blk:] = ti_t
            wbuf[slab, k, blk:, :blk] = (-ti_t.astype(jnp.float32)).astype(jnp.bfloat16)
            wbuf[slab, k, blk:, blk:] = tr_t

    def wait_tile_sends(slab):
        for c0v in range(ncol):
            @pl.when(col == c0v)
            def _():
                for r in range(ncol):
                    if r != c0v:
                        tile_copy(slab, c0v, r).wait_send()

    def part(h):
        return pl.ds(h * width, width)

    def row_copy(n, to_sec, c0v, d, h):
        q = c0v + d
        return pltpu.make_async_remote_copy(
            src_ref=fbuf.at[n, :, part(h)],
            dst_ref=xbuf.at[n, reach - d, :, part(h)],
            send_sem=ss1.at[n, reach - d, h],
            recv_sem=rs1.at[n, reach - d, h],
            device_id=(to_sec, (lat + q // ncol + nlat) % nlat, q % ncol),
            device_id_type=MESH_ID,
        )

    def far_first(c0v):
        def hops(d):
            q = c0v + d
            gap = abs(q % ncol - c0v)
            return min(gap, ncol - gap) + (q // ncol != 0)
        return sorted(shifts, key=lambda d: (-hops(d), d))

    def send_rows(n, to_sec, local, h):
        for c0v in range(ncol):
            @pl.when(col == c0v)
            def _():
                for d in far_first(c0v):
                    if local and d == 0:
                        continue
                    row_copy(n, to_sec, c0v, d, h).start()

    def wait_row_sends(n, to_sec, local):
        for c0v in range(ncol):
            @pl.when(col == c0v)
            def _():
                for h in range(chunks):
                    for d in shifts:
                        if local and d == 0:
                            continue
                        row_copy(n, to_sec, c0v, d, h).wait_send()

    def put_field(n, to_sec, local, h, value):
        fbuf[n, :, part(h)] = value.astype(jnp.bfloat16)
        send_rows(n, to_sec, local, h)

    def run_app(n, slab, local, finish):
        order = sorted(range(noff), key=lambda k: (abs(k - reach), k))
        dot = functools.partial(jnp.dot, preferred_element_type=jnp.float32)
        for h in range(chunks):
            acc_r = None
            for k in order:
                d = k - reach
                if not (local and d == 0):
                    row_copy(n, sec, 0, -d, h).wait_recv()
                lo = (lat == 0) & (k < reach - col)
                hi = (lat == nlat - 1) & (k >= reach - col + ncol)

                @pl.when((lo | hi) & (not (local and d == 0)))
                def _():
                    sn = jnp.where(lo, -sin_v, sin_v)
                    x = xbuf[n, k, :, part(h)].astype(jnp.float32)
                    xbuf[n, k, 0, part(h)] = (x[0] * cos_v - x[1] * sn).astype(jnp.bfloat16)
                    xbuf[n, k, 1, part(h)] = (x[0] * sn + x[1] * cos_v).astype(jnp.bfloat16)

                if local and d == 0:
                    xr = fbuf[n, 0, part(h)]
                    xi = fbuf[n, 1, part(h)]
                else:
                    xr = xbuf[n, k, 0, part(h)]
                    xi = xbuf[n, k, 1, part(h)]
                both = dot(jnp.concatenate([xr, xi], axis=1), wbuf[slab, k])
                acc_r = both if acc_r is None else acc_r + both
            blk = xbuf.shape[4]
            finish(h, jnp.stack([acc_r[:, :blk], acc_r[:, blk:]], 0))

    def emit_out(s):
        for ri in range(2):
            out_ref[s, 0, ri] = outt[s, ri].T

    def transpose_in(dst, src):
        for ri in range(2):
            dst[ri] = src[ri].astype(jnp.float32).T.astype(jnp.bfloat16)

    @pl.when(sec == 0)
    def _():
        share_tiles(0)
        for ri in range(2):
            fbuf[0, ri] = src_ref[0, 0, ri].astype(jnp.float32).T.astype(jnp.bfloat16)
        for h in range(chunks):
            send_rows(0, 0, True, h)
        transpose_in(srct.at[1], src_ref.at[1, 0])
        share_tiles(1)
        wait_tiles(0)

        def fin0(h, r):
            vt[0, :, part(h)] = r
            put_field(1, 0, True, h, srct[1, :, part(h)].astype(jnp.float32) + coupling * r)

        run_app(0, 0, True, fin0)
        wait_tiles(1)
        src_copy = pltpu.make_async_remote_copy(
            src_ref=src_ref.at[0, 0], dst_ref=srcbuf, send_sem=ssrc, recv_sem=rsrc,
            device_id=(1, lat, col), device_id_type=MESH_ID,
        )

        def fin1(h, r):
            vt[1, :, part(h)] = r
            if h == 0:
                src_copy.wait_recv()
                transpose_in(srct.at[0], srcbuf)
            put_field(2, 1, False, h, srct[0, :, part(h)].astype(jnp.float32) + coupling * r)

        run_app(1, 1, True, fin1)

        def fin5(h, r):
            sol = vt[1, :, part(h)] + coupling * r
            outt[1, :, part(h)] = sol
            put_field(6, 0, True, h, sol)

        run_app(5, 1, False, fin5)
        emit_out(1)

        def fin6(h, r):
            outt[0, :, part(h)] = vt[0, :, part(h)] + coupling * r

        run_app(6, 0, True, fin6)
        emit_out(0)
        wait_row_sends(0, 0, True)
        wait_row_sends(1, 0, True)
        wait_row_sends(2, 1, False)
        wait_row_sends(6, 0, True)
        wait_tile_sends(0)
        wait_tile_sends(1)

    @pl.when(sec == 1)
    def _():
        src_copy = pltpu.make_async_remote_copy(
            src_ref=src_ref.at[0, 0], dst_ref=srcbuf, send_sem=ssrc, recv_sem=rsrc,
            device_id=(0, lat, col), device_id_type=MESH_ID,
        )
        src_copy.start()
        share_tiles(0)
        share_tiles(1)
        transpose_in(srct.at[1], src_ref.at[1, 0])
        wait_tiles(0)
        wait_tiles(1)

        def fin2(h, r):
            vt[0, :, part(h)] = r
            put_field(3, 1, True, h, srct[1, :, part(h)].astype(jnp.float32) + coupling * r)

        run_app(2, 0, False, fin2)

        def fin3(h, r):
            outt[1, :, part(h)] = r
            put_field(4, 1, True, h, r)

        run_app(3, 1, True, fin3)
        emit_out(1)

        def fin4(h, r):
            sol = vt[0, :, part(h)] + coupling * r
            outt[0, :, part(h)] = sol
            put_field(5, 0, False, h, sol)

        run_app(4, 0, True, fin4)
        emit_out(0)
        wait_row_sends(3, 1, True)
        wait_row_sends(4, 1, True)
        wait_row_sends(5, 0, False)
        wait_tile_sends(0)
        wait_tile_sends(1)
        src_copy.wait_send()


def shards(sources, inverse_tiles, pattern, phase_index):
    nlat = lax.axis_size("lat")
    ncol = lax.axis_size("col")
    koff = inverse_tiles.shape[2]
    reach = OFF // 2
    noff = koff * ncol
    blk, nrhs = sources.shape[3], sources.shape[4]
    angle = 2.0 * jnp.pi * phase_index[0].astype(jnp.float32) / PHASES
    trig = jnp.stack([jnp.cos(angle), jnp.sin(angle)])
    kernel = functools.partial(sweep_kernel, nlat, ncol, koff, reach, CHUNKS)
    vmem = pl.BlockSpec(memory_space=pltpu.VMEM)
    smem = pl.BlockSpec(memory_space=pltpu.SMEM)
    slabs = inverse_tiles.shape[0]
    return pl.pallas_call(
        kernel,
        out_shape=jax.ShapeDtypeStruct(sources.shape, jnp.float32),
        in_specs=[smem, smem, pl.BlockSpec(memory_space=pl.ANY), pl.BlockSpec(memory_space=pl.ANY)],
        out_specs=vmem,
        scratch_shapes=[
            pltpu.VMEM(sources.shape, jnp.bfloat16),
            pltpu.VMEM(inverse_tiles.shape, jnp.bfloat16),
            pltpu.VMEM(inverse_tiles.shape, jnp.bfloat16),
            pltpu.VMEM((slabs, noff, 2, blk, blk), jnp.bfloat16),
            pltpu.VMEM((slabs, noff, 2 * blk, 2 * blk), jnp.bfloat16),
            pltpu.VMEM((APPS, noff, 2, nrhs, blk), jnp.bfloat16),
            pltpu.VMEM((APPS, 2, nrhs, blk), jnp.bfloat16),
            pltpu.VMEM((slabs, 2, nrhs, blk), jnp.bfloat16),
            pltpu.VMEM((slabs, 2, nrhs, blk), jnp.float32),
            pltpu.VMEM((slabs, 2, nrhs, blk), jnp.float32),
            pltpu.VMEM((2, blk, nrhs), jnp.bfloat16),
            pltpu.SemaphoreType.DMA((APPS, noff, CHUNKS)),
            pltpu.SemaphoreType.DMA((APPS, noff, CHUNKS)),
            pltpu.SemaphoreType.DMA((slabs, ncol)),
            pltpu.SemaphoreType.DMA((slabs, ncol)),
            pltpu.SemaphoreType.DMA(()),
            pltpu.SemaphoreType.DMA(()),
            pltpu.SemaphoreType.DMA((1 + slabs,)),
        ],
        compiler_params=pltpu.CompilerParams(
            has_side_effects=True, collective_id=0, vmem_limit_bytes=67043328
        ),
    )(trig, pattern, sources, inverse_tiles)


def solution(mesh):
    placed = (
        P("sec", ("lat", "col"), None, None, None),
        P("sec", "lat", "col", None, None, None),
        P("sec", "lat", "col"),
        P(),
    )
    return jax.shard_map(
        shards,
        mesh=mesh,
        in_specs=placed,
        out_specs=P("sec", ("lat", "col"), None, None, None),
        check_vma=False,
    )
```

```python
import functools

import jax
import jax.numpy as jnp
from jax import lax
from jax.experimental import pallas as pl
from jax.experimental.pallas import tpu as pltpu
from jax.sharding import PartitionSpec as P

OFF = 8
PHASES = 16
APPS = 7
CHUNKS = 4

coupling = 0.8

MESH_ID = pl.DeviceIdType.MESH


def sweep_kernel(
    nlat, ncol, koff, reach, chunks,
    trig_ref, pat_ref, src_hbm, tiles_hbm, out_ref,
    src_ref, tiles_ref, mtiles, tiles2, wbuf, xbuf, fbuf, srct, vt, outt, srcbuf,
    rs1, ss1, rst, sst, rsrc, ssrc, lsem,
):
    sec = lax.axis_index("sec")
    lat = lax.axis_index("lat")
    col = lax.axis_index("col")
    cos_v = trig_ref[0]
    sin_v = trig_ref[1]
    noff = koff * ncol
    shifts = [d for d in range(reach - noff + 1, reach + 1)]
    width = xbuf.shape[3] // chunks

    loads = [pltpu.make_async_copy(src_hbm, src_ref, lsem.at[0])]
    for slab in range(tiles_ref.shape[0]):
        loads.append(pltpu.make_async_copy(tiles_hbm.at[slab], tiles_ref.at[slab], lsem.at[1 + slab]))
    for load in loads:
        load.start()

    barrier = pltpu.get_barrier_semaphore()
    partners = 0
    for ds in range(2):
        for d in range(-reach, reach + 1):
            if ds == 0 and d == 0:
                continue
            q = col + d
            pl.semaphore_signal(
                barrier, 1,
                device_id=((sec + ds) % 2, (lat + q // ncol + nlat) % nlat, (q + ncol) % ncol),
                device_id_type=MESH_ID,
            )
            partners += 1
    pl.semaphore_wait(barrier, partners)
    loads[0].wait()

    def tile_copy(slab, c0v, r):
        return pltpu.make_async_remote_copy(
            src_ref=mtiles.at[slab, r],
            dst_ref=tiles2.at[slab, pl.ds(c0v * koff, koff)],
            send_sem=sst.at[slab, r],
            recv_sem=rst.at[slab, c0v],
            device_id=(sec, lat, r),
            device_id_type=MESH_ID,
        )

    def share_tiles(slab):
        loads[1 + slab].wait()
        for r in range(ncol):
            for j in range(koff):
                keep = pat_ref[slab, r, j] != 0
                tile = tiles_ref[slab, r, j]
                mtiles[slab, r, j] = jnp.where(keep, tile, jnp.zeros_like(tile))
        for c0v in range(ncol):
            @pl.when(col == c0v)
            def _():
                for r in range(ncol):
                    if r != c0v:
                        tile_copy(slab, c0v, r).start()
                tiles2[slab, pl.ds(c0v * koff, koff)] = mtiles[slab, c0v]

    def wait_tiles(slab):
        for c in range(ncol):
            @pl.when(col != c)
            def _():
                tile_copy(slab, c, c).wait_recv()
        blk = tiles2.shape[3]
        for k in range(noff):
            tr_t = tiles2[slab, k, 0].T
            ti_t = tiles2[slab, k, 1].T
            pair, half = (k - reach, 0) if k >= reach else (reach - 1 - k, 1)
            top = half * 2 * blk
            wbuf[slab, pair, top:top + blk, :blk] = tr_t
            wbuf[slab, pair, top:top + blk, blk:] = ti_t
            wbuf[slab, pair, top + blk:top + 2 * blk, :blk] = (-ti_t.astype(jnp.float32)).astype(jnp.bfloat16)
            wbuf[slab, pair, top + blk:top + 2 * blk, blk:] = tr_t

    def wait_tile_sends(slab):
        for c0v in range(ncol):
            @pl.when(col == c0v)
            def _():
                for r in range(ncol):
                    if r != c0v:
                        tile_copy(slab, c0v, r).wait_send()

    def part(h):
        return pl.ds(h * width, width)

    def row_copy(n, to_sec, c0v, d, h):
        q = c0v + d
        return pltpu.make_async_remote_copy(
            src_ref=fbuf.at[n, :, part(h)],
            dst_ref=xbuf.at[n, reach - d, :, part(h)],
            send_sem=ss1.at[n, reach - d, h],
            recv_sem=rs1.at[n, reach - d, h],
            device_id=(to_sec, (lat + q // ncol + nlat) % nlat, q % ncol),
            device_id_type=MESH_ID,
        )

    def far_first(c0v):
        def hops(d):
            q = c0v + d
            gap = abs(q % ncol - c0v)
            return min(gap, ncol - gap) + (q // ncol != 0)
        return sorted(shifts, key=lambda d: (-hops(d), d))

    def send_rows(n, to_sec, local, h):
        for c0v in range(ncol):
            @pl.when(col == c0v)
            def _():
                for d in far_first(c0v):
                    if local and d == 0:
                        continue
                    row_copy(n, to_sec, c0v, d, h).start()

    def wait_row_sends(n, to_sec, local):
        for c0v in range(ncol):
            @pl.when(col == c0v)
            def _():
                for h in range(chunks):
                    for d in shifts:
                        if local and d == 0:
                            continue
                        row_copy(n, to_sec, c0v, d, h).wait_send()

    def put_field(n, to_sec, local, h, value):
        fbuf[n, :, part(h)] = value.astype(jnp.bfloat16)
        send_rows(n, to_sec, local, h)

    def run_app(n, slab, local, finish):
        order = sorted(range(noff), key=lambda k: (abs(k - reach), k))
        dot = functools.partial(jnp.dot, preferred_element_type=jnp.float32)
        for h in range(chunks):
            acc_r = None
            pieces = []
            for k in order:
                d = k - reach
                if not (local and d == 0):
                    row_copy(n, sec, 0, -d, h).wait_recv()
                lo = (lat == 0) & (k < reach - col)
                hi = (lat == nlat - 1) & (k >= reach - col + ncol)

                @pl.when((lo | hi) & (not (local and d == 0)))
                def _():
                    sn = jnp.where(lo, -sin_v, sin_v)
                    x = xbuf[n, k, :, part(h)].astype(jnp.float32)
                    xbuf[n, k, 0, part(h)] = (x[0] * cos_v - x[1] * sn).astype(jnp.bfloat16)
                    xbuf[n, k, 1, part(h)] = (x[0] * sn + x[1] * cos_v).astype(jnp.bfloat16)

                if local and d == 0:
                    xr = fbuf[n, 0, part(h)]
                    xi = fbuf[n, 1, part(h)]
                else:
                    xr = xbuf[n, k, 0, part(h)]
                    xi = xbuf[n, k, 1, part(h)]
                pieces += [xr, xi]
                if len(pieces) == 4:
                    pair = max(k, 2 * reach - 1 - k) - reach
                    both = dot(jnp.concatenate(pieces, axis=1), wbuf[slab, pair])
                    acc_r = both if acc_r is None else acc_r + both
                    pieces = []
            blk = xbuf.shape[4]
            finish(h, jnp.stack([acc_r[:, :blk], acc_r[:, blk:]], 0))

    def emit_out(s):
        for ri in range(2):
            out_ref[s, 0, ri] = outt[s, ri].T

    def transpose_in(dst, src):
        for ri in range(2):
            dst[ri] = src[ri].astype(jnp.float32).T.astype(jnp.bfloat16)

    @pl.when(sec == 0)
    def _():
        share_tiles(0)
        for ri in range(2):
            fbuf[0, ri] = src_ref[0, 0, ri].astype(jnp.float32).T.astype(jnp.bfloat16)
        for h in range(chunks):
            send_rows(0, 0, True, h)
        transpose_in(srct.at[1], src_ref.at[1, 0])
        share_tiles(1)
        wait_tiles(0)

        def fin0(h, r):
            vt[0, :, part(h)] = r
            put_field(1, 0, True, h, srct[1, :, part(h)].astype(jnp.float32) + coupling * r)

        run_app(0, 0, True, fin0)
        wait_tiles(1)
        src_copy = pltpu.make_async_remote_copy(
            src_ref=src_ref.at[0, 0], dst_ref=srcbuf, send_sem=ssrc, recv_sem=rsrc,
            device_id=(1, lat, col), device_id_type=MESH_ID,
        )

        def fin1(h, r):
            vt[1, :, part(h)] = r
            if h == 0:
                src_copy.wait_recv()
                transpose_in(srct.at[0], srcbuf)
            put_field(2, 1, False, h, srct[0, :, part(h)].astype(jnp.float32) + coupling * r)

        run_app(1, 1, True, fin1)

        def fin5(h, r):
            sol = vt[1, :, part(h)] + coupling * r
            outt[1, :, part(h)] = sol
            put_field(6, 0, True, h, sol)

        run_app(5, 1, False, fin5)
        emit_out(1)

        def fin6(h, r):
            outt[0, :, part(h)] = vt[0, :, part(h)] + coupling * r

        run_app(6, 0, True, fin6)
        emit_out(0)
        wait_row_sends(0, 0, True)
        wait_row_sends(1, 0, True)
        wait_row_sends(2, 1, False)
        wait_row_sends(6, 0, True)
        wait_tile_sends(0)
        wait_tile_sends(1)

    @pl.when(sec == 1)
    def _():
        src_copy = pltpu.make_async_remote_copy(
            src_ref=src_ref.at[0, 0], dst_ref=srcbuf, send_sem=ssrc, recv_sem=rsrc,
            device_id=(0, lat, col), device_id_type=MESH_ID,
        )
        src_copy.start()
        share_tiles(0)
        share_tiles(1)
        transpose_in(srct.at[1], src_ref.at[1, 0])
        wait_tiles(0)
        wait_tiles(1)

        def fin2(h, r):
            vt[0, :, part(h)] = r
            put_field(3, 1, True, h, srct[1, :, part(h)].astype(jnp.float32) + coupling * r)

        run_app(2, 0, False, fin2)

        def fin3(h, r):
            outt[1, :, part(h)] = r
            put_field(4, 1, True, h, r)

        run_app(3, 1, True, fin3)
        emit_out(1)

        def fin4(h, r):
            sol = vt[0, :, part(h)] + coupling * r
            outt[0, :, part(h)] = sol
            put_field(5, 0, False, h, sol)

        run_app(4, 0, True, fin4)
        emit_out(0)
        wait_row_sends(3, 1, True)
        wait_row_sends(4, 1, True)
        wait_row_sends(5, 0, False)
        wait_tile_sends(0)
        wait_tile_sends(1)
        src_copy.wait_send()


def shards(sources, inverse_tiles, pattern, phase_index):
    nlat = lax.axis_size("lat")
    ncol = lax.axis_size("col")
    koff = inverse_tiles.shape[2]
    reach = OFF // 2
    noff = koff * ncol
    blk, nrhs = sources.shape[3], sources.shape[4]
    angle = 2.0 * jnp.pi * phase_index[0].astype(jnp.float32) / PHASES
    trig = jnp.stack([jnp.cos(angle), jnp.sin(angle)])
    kernel = functools.partial(sweep_kernel, nlat, ncol, koff, reach, CHUNKS)
    vmem = pl.BlockSpec(memory_space=pltpu.VMEM)
    smem = pl.BlockSpec(memory_space=pltpu.SMEM)
    slabs = inverse_tiles.shape[0]
    return pl.pallas_call(
        kernel,
        out_shape=jax.ShapeDtypeStruct(sources.shape, jnp.float32),
        in_specs=[smem, smem, pl.BlockSpec(memory_space=pl.ANY), pl.BlockSpec(memory_space=pl.ANY)],
        out_specs=vmem,
        scratch_shapes=[
            pltpu.VMEM(sources.shape, jnp.bfloat16),
            pltpu.VMEM(inverse_tiles.shape, jnp.bfloat16),
            pltpu.VMEM(inverse_tiles.shape, jnp.bfloat16),
            pltpu.VMEM((slabs, noff, 2, blk, blk), jnp.bfloat16),
            pltpu.VMEM((slabs, noff // 2, 4 * blk, 2 * blk), jnp.bfloat16),
            pltpu.VMEM((APPS, noff, 2, nrhs, blk), jnp.bfloat16),
            pltpu.VMEM((APPS, 2, nrhs, blk), jnp.bfloat16),
            pltpu.VMEM((slabs, 2, nrhs, blk), jnp.bfloat16),
            pltpu.VMEM((slabs, 2, nrhs, blk), jnp.float32),
            pltpu.VMEM((slabs, 2, nrhs, blk), jnp.float32),
            pltpu.VMEM((2, blk, nrhs), jnp.bfloat16),
            pltpu.SemaphoreType.DMA((APPS, noff, CHUNKS)),
            pltpu.SemaphoreType.DMA((APPS, noff, CHUNKS)),
            pltpu.SemaphoreType.DMA((slabs, ncol)),
            pltpu.SemaphoreType.DMA((slabs, ncol)),
            pltpu.SemaphoreType.DMA(()),
            pltpu.SemaphoreType.DMA(()),
            pltpu.SemaphoreType.DMA((1 + slabs,)),
        ],
        compiler_params=pltpu.CompilerParams(
            has_side_effects=True, collective_id=0, vmem_limit_bytes=67043328
        ),
    )(trig, pattern, sources, inverse_tiles)


def solution(mesh):
    placed = (
        P("sec", ("lat", "col"), None, None, None),
        P("sec", "lat", "col", None, None, None),
        P("sec", "lat", "col"),
        P(),
    )
    return jax.shard_map(
        shards,
        mesh=mesh,
        in_specs=placed,
        out_specs=P("sec", ("lat", "col"), None, None, None),
        check_vma=False,
    )
```
